1024 devices in a mesh: frame: 16 (over z_hi, y, core), row: 16 (over z_lo), head: 4 (over x).
Axes of the slice: x: 4, y: 4, z: 32 (z_hi: 2, z_lo: 16; z = z_hi * 16 + z_lo), core: 2. Of those that a mesh axis runs over, the one named last changes fastest.
Arguments:
- queries: bfloat16 [32, 128, 16, 12, 128], P('frame', 'row', 'head'), may hold values from -6 to 6
- keys: bfloat16 [32, 128, 16, 12, 128], P('frame', 'row', 'head'), may hold values from -6 to 6
- values: bfloat16 [32, 128, 16, 12, 128], P('frame', 'row', 'head'), may hold values from -6 to 6
- out_grad: bfloat16 [32, 128, 16, 12, 128], P('frame', 'row', 'head'), may hold values from -6 to 6
- active: int32 [32, 16, 2, 27], replicated, may hold values from 0 to 1, as said below
Outputs:
- attended: bfloat16 [32, 128, 16, 12, 128], P('frame', 'row', 'head')
- query_grad: bfloat16 [32, 128, 16, 12, 128], P('frame', 'row', 'head')
- key_grad: bfloat16 [32, 128, 16, 12, 128], P('frame', 'row', 'head')
- value_grad: bfloat16 [32, 128, 16, 12, 128], P('frame', 'row', 'head')
The draws below stay inside these ranges and needn't reach their ends.
Inputs may be any that keep to these rules, and one draw needn't show every extreme that they name: `active`: entry 13 (the tile with itself) is 1 for every tile; all other entries are 0 or 1.
All inputs are finite; a program needn't handle non-finite values.
Results may differ from the reference program's by a relative error of at most 0.011.
Values may be sent and summed in bfloat16 or wider, within the bound.
A program may use at most 32 MiB of HBM per device.

```python
import jax
import jax.numpy as jnp
from jax import lax

HEADS = 12
HD = 128
TF = 1
TR = 8
TC = 8
SLOTS = 27
COLS = 16
NF = 32
NR = 128
NTF = 32
NTR = 16
NTC = 2


def draw_queries(key, part):
    shape = (NF, NR, COLS, HEADS, HD)
    base_key = jax.random.fold_in(key, 11)
    result = jnp.clip(jax.random.normal(base_key, shape, jnp.float32), -6.0, 6.0)
    return result.astype(jnp.bfloat16)


def draw_keys(key, part):
    shape = (NF, NR, COLS, HEADS, HD)
    base_key = jax.random.fold_in(key, 17)
    result = jnp.clip(jax.random.normal(base_key, shape, jnp.float32), -6.0, 6.0)
    return result.astype(jnp.bfloat16)


def draw_active(key, part):
    level = jax.random.randint(jax.random.fold_in(key, 3), (NTF, NTR, NTC, 1), 1, 5)
    rolled = jax.random.randint(jax.random.fold_in(key, 5), (NTF, NTR, NTC, SLOTS), 0, 4)
    picked = (rolled < level).astype(jnp.int32)
    center = lax.broadcasted_iota(jnp.int32, (NTF, NTR, NTC, SLOTS), 3) == 13
    return jnp.where(center, 1, picked).astype(jnp.int32)


def shard_levels(stream_key, extent, shards, smallest, high):
    gain = 1.0
    for axis_at, blocks in shards:
        steps = jax.random.uniform(jax.random.fold_in(jax.random.fold_in(stream_key, 6), axis_at), (blocks,), jnp.float32, smallest / len(shards), high / len(shards))
        gain = gain * jnp.repeat(jnp.exp(steps), extent[axis_at] // blocks).reshape((-1,) + (1,) * (len(extent) - 1 - axis_at))
    return gain


def gaussian(stream_key, extent, deviation, bound, cuts=(), held_as=jnp.bfloat16):
    loudness = shard_levels(stream_key, extent, cuts, -0.22, 0.18) if cuts else 1.0
    entries = jax.random.normal(stream_key, extent, jnp.float32) * deviation * loudness
    return jnp.minimum(jnp.maximum(entries, -bound), bound).astype(held_as)


def setup_inputs(seed: int = 0) -> dict:
    key_of = jax.random.split(jax.random.key(seed), 6)
    return {
        "queries": draw_queries(jax.random.fold_in(key_of[5], 71), 0),
        "keys": draw_keys(jax.random.fold_in(key_of[5], 71), 0),
        "values": gaussian(key_of[2], (NF, NR, COLS, HEADS, HD), 1.0, 6.0, ((0, 16), (1, 16), (2, 4))),
        "out_grad": gaussian(key_of[3], (NF, NR, COLS, HEADS, HD), 1.0, 6.0, ((0, 16), (1, 16), (2, 4))),
        "active": draw_active(jax.random.fold_in(key_of[5], 71), 0),
    }


def product(form, left, right):
    return jnp.einsum(form, left.astype(jnp.float32), right.astype(jnp.float32))


def slot_masks(act_ext, one_ext, frame_tiles, row_tiles, sign):
    col_tiles = act_ext.shape[2]
    own = jnp.arange(col_tiles, dtype=jnp.int32)[:, None]
    other = jnp.arange(col_tiles, dtype=jnp.int32)[None, :]
    offsets = jnp.arange(3, dtype=jnp.int32) - 1
    matches = (((other - own) * sign)[:, :, None] == offsets[None, None, :]).astype(jnp.float32)
    layers = []
    for offset in range(9):
        frame_step = offset // 3 - 1
        row_step = offset % 3 - 1
        if sign > 0:
            chosen = act_ext[1:1 + frame_tiles, 1:1 + row_tiles, :, 3 * offset:3 * offset + 3]
            inside = one_ext[1 + frame_step:1 + frame_step + frame_tiles, 1 + row_step:1 + row_step + row_tiles]
        else:
            chosen = act_ext[1 - frame_step:1 - frame_step + frame_tiles, 1 - row_step:1 - row_step + row_tiles, :, 3 * offset:3 * offset + 3]
            inside = jnp.ones((frame_tiles, row_tiles), jnp.float32)
        layers.append(jnp.einsum("abio,ijo->abij", chosen.astype(jnp.float32), matches) * inside[:, :, None, None])
    tiles = jnp.transpose(jnp.stack(layers, axis=2), (0, 1, 3, 2, 4))
    spread = jnp.broadcast_to(tiles[:, :, None, :, None, :, None, :, None], (frame_tiles, row_tiles, TF * TR, col_tiles, TC, 9, TF * TR, col_tiles, TC))
    slab = TF * TR * col_tiles * TC
    return spread.reshape(frame_tiles, row_tiles, slab, 9 * slab) > 0.5


def gather_bands(wide, frame_tiles, row_tiles, sign):
    parts = []
    for offset in range(9):
        frame_step = sign * (offset // 3 - 1)
        row_step = sign * (offset % 3 - 1)
        parts.append(wide[1 + frame_step:1 + frame_step + frame_tiles, 1 + row_step:1 + row_step + row_tiles])
    stacked = jnp.stack(parts, axis=2)
    return stacked.reshape((frame_tiles, row_tiles, 9 * wide.shape[2]) + wide.shape[3:])


def query_side(query_slab, key_wide, value_wide, grad_slab, allowed, scaling):
    frame_tiles, row_tiles = query_slab.shape[0], query_slab.shape[1]
    key_band = gather_bands(key_wide, frame_tiles, row_tiles, 1)
    value_band = gather_bands(value_wide, frame_tiles, row_tiles, 1)
    scores = product("abqd,abkd->abqk", query_slab, key_band) * scaling
    scores = jnp.where(allowed, scores, -jnp.inf)
    highest = jnp.max(scores, axis=-1, keepdims=True)
    log_total = highest + jnp.log(jnp.sum(jnp.exp(scores - highest), axis=-1, keepdims=True))
    weights = jnp.where(allowed, jnp.exp(scores - log_total), 0.0).astype(jnp.bfloat16)
    weights = lax.optimization_barrier(weights)
    attended = product("abqk,abkd->abqd", weights, value_band).astype(jnp.bfloat16)
    attended = lax.optimization_barrier(attended)
    grad_dot = jnp.sum(grad_slab.astype(jnp.float32) * attended.astype(jnp.float32), axis=-1)
    grad_probs = product("abqd,abkd->abqk", grad_slab, value_band)
    grad_scores = (weights.astype(jnp.float32) * (grad_probs - grad_dot[..., None]) * scaling).astype(jnp.bfloat16)
    query_grad = product("abqk,abkd->abqd", grad_scores, key_band).astype(jnp.bfloat16)
    return attended, query_grad, log_total[..., 0], grad_dot


def key_side(key_slab, value_slab, query_wide, grad_wide, total_wide, dot_wide, allowed, scaling):
    frame_tiles, row_tiles = key_slab.shape[0], key_slab.shape[1]
    query_band = gather_bands(query_wide, frame_tiles, row_tiles, -1)
    grad_band = gather_bands(grad_wide, frame_tiles, row_tiles, -1)
    total_band = gather_bands(total_wide, frame_tiles, row_tiles, -1)
    dot_band = gather_bands(dot_wide, frame_tiles, row_tiles, -1)
    scores = product("abkd,abqd->abkq", key_slab, query_band) * scaling
    weights = jnp.where(allowed, jnp.exp(scores - total_band[:, :, None, :]), 0.0).astype(jnp.bfloat16)
    weights = lax.optimization_barrier(weights)
    grad_probs = product("abkd,abqd->abkq", value_slab, grad_band)
    grad_scores = (weights.astype(jnp.float32) * (grad_probs - dot_band[:, :, None, :]) * scaling).astype(jnp.bfloat16)
    key_grad = product("abkq,abqd->abkd", grad_scores, query_band).astype(jnp.bfloat16)
    value_grad = product("abkq,abqd->abkd", weights, grad_band).astype(jnp.bfloat16)
    return key_grad, value_grad


def to_slabs(tensor):
    shaped = tensor.reshape(NTF, TF, NTR, TR, COLS, HEADS, HD)
    return jnp.transpose(shaped, (5, 0, 2, 1, 3, 4, 6)).reshape(HEADS, NTF, NTR, TF * TR * COLS, HD)


def from_slabs(result):
    shaped = result.reshape(HEADS, NTF, NTR, TF, TR, COLS, HD)
    return jnp.transpose(shaped, (1, 3, 2, 4, 5, 0, 6)).reshape(NF, NR, COLS, HEADS, HD)


def pad_tiles(tensor):
    widths = ((1, 1), (1, 1)) + ((0, 0),) * (tensor.ndim - 2)
    return jnp.pad(tensor, widths)


def reference(queries, keys, values, out_grad, active):
    scaling = HD ** -0.5
    padded_active = jnp.pad(active, ((1, 1), (1, 1), (0, 0), (0, 0)))
    padded_ones = jnp.pad(jnp.ones((NTF, NTR), jnp.float32), 1)
    frame_list = jnp.arange(NTF, dtype=jnp.int32)

    def head_pass(pieces):
        query_pad, key_pad, value_pad, grad_pad = [pad_tiles(piece) for piece in pieces]

        def front(frame_tile):
            act_ext = lax.dynamic_slice_in_dim(padded_active, frame_tile, 3, 0)
            one_ext = lax.dynamic_slice_in_dim(padded_ones, frame_tile, 3, 0)
            allowed = slot_masks(act_ext, one_ext, 1, NTR, 1)
            key_wide = lax.dynamic_slice_in_dim(key_pad, frame_tile, 3, 0)
            value_wide = lax.dynamic_slice_in_dim(value_pad, frame_tile, 3, 0)
            query_here = lax.dynamic_slice_in_dim(query_pad, frame_tile + 1, 1, 0)[:, 1:-1]
            grad_here = lax.dynamic_slice_in_dim(grad_pad, frame_tile + 1, 1, 0)[:, 1:-1]
            return query_side(query_here, key_wide, value_wide, grad_here, allowed, scaling)

        attended, query_grad, log_total, grad_dot = lax.map(front, frame_list)
        total_pad = pad_tiles(log_total[:, 0])
        dot_pad = pad_tiles(grad_dot[:, 0])

        def back(frame_tile):
            act_ext = lax.dynamic_slice_in_dim(padded_active, frame_tile, 3, 0)
            one_ext = lax.dynamic_slice_in_dim(padded_ones, frame_tile, 3, 0)
            allowed = slot_masks(act_ext, one_ext, 1, NTR, -1)
            query_wide = lax.dynamic_slice_in_dim(query_pad, frame_tile, 3, 0)
            grad_wide = lax.dynamic_slice_in_dim(grad_pad, frame_tile, 3, 0)
            total_wide = lax.dynamic_slice_in_dim(total_pad, frame_tile, 3, 0)
            dot_wide = lax.dynamic_slice_in_dim(dot_pad, frame_tile, 3, 0)
            key_here = lax.dynamic_slice_in_dim(key_pad, frame_tile + 1, 1, 0)[:, 1:-1]
            value_here = lax.dynamic_slice_in_dim(value_pad, frame_tile + 1, 1, 0)[:, 1:-1]
            return key_side(key_here, value_here, query_wide, grad_wide, total_wide, dot_wide, allowed, scaling)

        key_grad, value_grad = lax.map(back, frame_list)
        return attended[:, 0], query_grad[:, 0], key_grad[:, 0], value_grad[:, 0]

    results = lax.map(head_pass, (to_slabs(queries), to_slabs(keys), to_slabs(values), to_slabs(out_grad)))
    return (from_slabs(results[0]), from_slabs(results[1]), from_slabs(results[2]), from_slabs(results[3]))
```

```python
import functools
import math

import jax
import jax.numpy as jnp
from jax import lax
from jax.experimental import pallas as pl
from jax.experimental.pallas import tpu as pltpu
from jax.sharding import PartitionSpec as P

MESH = pl.DeviceIdType.MESH
NEG = -1e30
KEY, VAL, QRY, GRD = 0, 1, 2, 3
SLOTS = 27


def nt(left, right):
    return lax.dot_general(
        left, right, (((1,), (1,)), ((), ())), preferred_element_type=jnp.float32
    )


def nn(left, right):
    return jnp.dot(left, right, preferred_element_type=jnp.float32)


def tile_kernel(sizes, bias, k_in, v_in, q_in, g_in, *refs):
    frames, rows, heads, groups, scaling = sizes
    outs, refs = refs[:4], refs[4:]
    land, pack, wide, stats, own, back = refs[:6]
    in_sem, a_send, a_recv, z_send, z_recv, c_send, c_recv, d_send, d_recv = refs[6:15]
    o_send, o_recv, out_sem = refs[15:18]
    ins = (k_in, v_in, q_in, g_in)
    heads_all = groups * heads
    tall = heads_all * 16

    f_at = lax.axis_index("frame")
    r_at = lax.axis_index("row")
    x_at = lax.axis_index("head")
    up, down = f_at < frames - 1, f_at > 0
    right, left = r_at < rows - 1, r_at > 0
    far_up, far_down = f_at == frames // 2 - 1, f_at == frames // 2
    peers = [lax.rem(x_at + k, heads) for k in range(heads)]
    froms = [lax.rem(x_at + heads - k, heads) for k in range(heads)]

    def loading(t):
        return pltpu.make_async_copy(ins[t], land.at[t], in_sem.at[t])

    for t in range(4):
        loading(t).start()

    barrier = pltpu.get_barrier_semaphore()

    def greet(frame, row, head):
        pl.semaphore_signal(barrier, inc=1, device_id=(frame, row, head), device_id_type=MESH)

    for k in range(1, heads):
        greet(f_at, r_at, peers[k])
    pl.when(right)(lambda: greet(f_at, r_at + 1, x_at))
    pl.when(left)(lambda: greet(f_at, r_at - 1, x_at))
    pl.when(up)(lambda: greet(f_at + 1, r_at, x_at))
    pl.when(down)(lambda: greet(f_at - 1, r_at, x_at))

    @pl.when(jnp.logical_not(left))
    def _():
        wide[:, :, :, 0] = jnp.zeros_like(wide[:, :, :, 0])
        stats[:, :, 0] = jnp.zeros_like(stats[:, :, 0])

    @pl.when(jnp.logical_not(right))
    def _():
        wide[:, :, :, 2] = jnp.zeros_like(wide[:, :, :, 2])
        stats[:, :, 2] = jnp.zeros_like(stats[:, :, 2])

    @pl.when(jnp.logical_not(down))
    def _():
        wide[:, :, 0] = jnp.zeros_like(wide[:, :, 0])
        stats[:, 0] = jnp.zeros_like(stats[:, 0])

    @pl.when(jnp.logical_not(up))
    def _():
        wide[:, :, 3] = jnp.zeros_like(wide[:, :, 3])
        stats[:, 3] = jnp.zeros_like(stats[:, 3])

    out_row = lax.broadcasted_iota(jnp.int32, (tall, tall), 0)
    in_row = lax.broadcasted_iota(jnp.int32, (tall, tall), 1)

    def swapped(row):
        return ((row % 16) // 4) * (4 * heads_all) + (row // 16) * 4 + row % 4

    to_heads = (swapped(out_row) == in_row).astype(jnp.bfloat16)
    to_rows = (swapped(in_row) == out_row).astype(jnp.bfloat16)

    def exchange(t, k):
        there = peers[k]
        return pltpu.make_async_remote_copy(
            src_ref=pack.at[t, pl.ds(there * groups, groups)],
            dst_ref=wide.at[t, :, pl.ds(1, 2), 1, pl.ds(pl.multiple_of(x_at * 32, 32), 32)],
            send_sem=a_send.at[t, k - 1],
            recv_sem=a_recv.at[t, k - 1],
            device_id=(f_at, r_at, there),
            device_id_type=MESH,
        )

    def arriving(t, k):
        spot = pl.ds(pl.multiple_of(froms[k] * 32, 32), 32)
        return pltpu.make_async_remote_copy(
            src_ref=pack.at[t, pl.ds(0, groups)],
            dst_ref=wide.at[t, :, pl.ds(1, 2), 1, spot],
            send_sem=a_send.at[t, k - 1],
            recv_sem=a_recv.at[t, k - 1],
            device_id=(f_at, r_at, froms[k]),
            device_id_type=MESH,
        )

    def block(t, frame, row):
        ref = stats if t == 4 else wide.at[t]
        return ref.at[:, frame, row]

    def pair(t, row):
        ref = stats if t == 4 else wide.at[t]
        return ref.at[:, pl.ds(1, 2), row]

    def hop(src, dst, ss, rs, frame, row):
        return pltpu.make_async_remote_copy(
            src_ref=src,
            dst_ref=dst,
            send_sem=ss,
            recv_sem=rs,
            device_id=(frame, row, x_at),
            device_id_type=MESH,
        )

    def to_right(t):
        return hop(pair(t, 1), pair(t, 0), z_send.at[t, 0], z_recv.at[t, 0], f_at, r_at + 1)

    def to_left(t):
        return hop(pair(t, 1), pair(t, 2), z_send.at[t, 1], z_recv.at[t, 1], f_at, r_at - 1)

    def to_up(t):
        return hop(block(t, 2, 1), block(t, 0, 1), c_send.at[t, 0], c_recv.at[t, 0], f_at + 1, r_at)

    def to_down(t):
        return hop(block(t, 1, 1), block(t, 3, 1), c_send.at[t, 1], c_recv.at[t, 1], f_at - 1, r_at)

    def side_up(t, row):
        sem = 0 if row == 0 else 1
        return hop(
            block(t, 2, row), block(t, 0, row), d_send.at[t, sem], d_recv.at[t, sem], f_at + 1, r_at
        )

    def side_down(t, row):
        sem = 2 if row == 0 else 3
        return hop(
            block(t, 1, row), block(t, 3, row), d_send.at[t, sem], d_recv.at[t, sem], f_at - 1, r_at
        )

    def along_right(t, frame):
        sem = 0 if frame == 0 else 2
        return hop(
            block(t, frame, 1), block(t, frame, 0), d_send.at[t, sem], d_recv.at[t, sem], f_at, r_at + 1
        )

    def along_left(t, frame):
        sem = 1 if frame == 0 else 3
        return hop(
            block(t, frame, 1), block(t, frame, 2), d_send.at[t, sem], d_recv.at[t, sem], f_at, r_at - 1
        )

    both = jnp.logical_and
    near_up = both(up, jnp.logical_not(far_up))
    near_down = both(down, jnp.logical_not(far_down))

    def first_halo(t):
        pl.when(up)(lambda: to_up(t).start())
        pl.when(down)(lambda: to_down(t).start())
        pl.when(right)(lambda: to_right(t).start())
        pl.when(left)(lambda: to_left(t).start())

    def second_halo(t):
        pl.when(left)(lambda: to_right(t).wait_recv())
        pl.when(right)(lambda: to_left(t).wait_recv())
        pl.when(both(near_up, left))(lambda: side_up(t, 0).start())
        pl.when(both(near_up, right))(lambda: side_up(t, 2).start())
        pl.when(both(near_down, left))(lambda: side_down(t, 0).start())
        pl.when(both(near_down, right))(lambda: side_down(t, 2).start())
        pl.when(down)(lambda: to_up(t).wait_recv())
        pl.when(up)(lambda: to_down(t).wait_recv())
        pl.when(both(far_down, right))(lambda: along_right(t, 0).start())
        pl.when(both(far_down, left))(lambda: along_left(t, 0).start())
        pl.when(both(far_up, right))(lambda: along_right(t, 3).start())
        pl.when(both(far_up, left))(lambda: along_left(t, 3).start())

    def last_halo(t):
        pl.when(both(down, left))(lambda: side_up(t, 0).wait_recv())
        pl.when(both(down, right))(lambda: side_up(t, 2).wait_recv())
        pl.when(both(up, left))(lambda: side_down(t, 0).wait_recv())
        pl.when(both(up, right))(lambda: side_down(t, 2).wait_recv())

    def halo_sent(t):
        pl.when(up)(lambda: to_up(t).wait_send())
        pl.when(down)(lambda: to_down(t).wait_send())
        pl.when(right)(lambda: to_right(t).wait_send())
        pl.when(left)(lambda: to_left(t).wait_send())
        pl.when(both(near_up, left))(lambda: side_up(t, 0).wait_send())
        pl.when(both(near_up, right))(lambda: side_up(t, 2).wait_send())
        pl.when(both(near_down, left))(lambda: side_down(t, 0).wait_send())
        pl.when(both(near_down, right))(lambda: side_down(t, 2).wait_send())
        pl.when(both(far_down, right))(lambda: along_right(t, 0).wait_send())
        pl.when(both(far_down, left))(lambda: along_left(t, 0).wait_send())
        pl.when(both(far_up, right))(lambda: along_right(t, 3).wait_send())
        pl.when(both(far_up, left))(lambda: along_left(t, 3).wait_send())

    for t in range(4):
        loading(t).wait()
        for g in range(4):
            part = nn(to_heads, land[t, pl.ds(g * tall, tall)]).astype(jnp.bfloat16)
            pack[t, :, g // 2, pl.ds(16 * (g % 2), 16)] = part.reshape(heads_all, 16, 128)
        if t == 0:
            known = [right, left, up, down]
            pl.semaphore_wait(barrier, heads - 1 + sum(c.astype(jnp.int32) for c in known))
        for k in range(1, heads):
            exchange(t, k).start()
        wide[t, :, pl.ds(1, 2), 1, pl.ds(pl.multiple_of(x_at * 32, 32), 32)] = pack[
            t, pl.ds(x_at * groups, groups)
        ]

    def gathered(t):
        for k in range(1, heads):
            arriving(t, k).wait_recv()

    gathered(KEY)
    first_halo(KEY)
    gathered(VAL)
    first_halo(VAL)
    second_halo(KEY)
    gathered(QRY)
    first_halo(QRY)
    second_halo(VAL)
    gathered(GRD)
    first_halo(GRD)
    second_halo(QRY)
    second_halo(GRD)
    last_halo(KEY)
    last_halo(VAL)

    lanes = lax.broadcasted_iota(jnp.int32, (1, 128), 1)
    lane_grid = lax.broadcasted_iota(jnp.int32, (128, 128), 1)
    power = scaling * math.log2(math.e)

    def entry(i, j, l, slot):
        return bias[((i * 3 + j) * 2 + l) * SLOTS + slot]

    def query_step(i, carry):
        h, f = i // 2, i % 2
        q = wide[QRY, h, f + 1, 1]
        g = wide[GRD, h, f + 1, 1]
        k_band = wide[KEY, h, pl.ds(f, 3)].reshape(9 * 128, 128)
        v_band = wide[VAL, h, pl.ds(f, 3)].reshape(9 * 128, 128)
        masks = []
        for l in range(2):
            cells = []
            for a in range(3):
                for b in range(3):
                    frame = 2 * f_at + f + a - 1
                    row = r_at + b - 1
                    inside = (frame >= 0) & (frame < 2 * frames) & (row >= 0) & (row < rows)
                    pieces = []
                    for m in range(2):
                        value = entry(f + 1, 1, l, 9 * a + 3 * b + m - l + 1)
                        pieces.append(jnp.where(inside, value, NEG))
                    cells.append(jnp.where(lanes < 64, pieces[0], pieces[1]))
            masks.append(jnp.concatenate(cells, axis=1))
        mask = jnp.concatenate([m[None] for m in masks], axis=0)
        s = nt(q, k_band)
        s = (s.reshape(2, 64, 9 * 128) + mask).reshape(128, 9 * 128)
        top = jnp.max(s, axis=1, keepdims=True)
        p = jnp.exp2((s - top) * power)
        total = jnp.sum(p, axis=1, keepdims=True)
        inverse = 1.0 / total
        out = (nn(p.astype(jnp.bfloat16), v_band) * inverse).astype(jnp.bfloat16)
        own[0, h, f] = out
        dot = jnp.sum(g.astype(jnp.float32) * out.astype(jnp.float32), axis=1, keepdims=True)
        dp = nt(g, v_band)
        ds = (p * (dp - dot)).astype(jnp.bfloat16)
        own[1, h, f] = (nn(ds, k_band) * (inverse * scaling)).astype(jnp.bfloat16)
        level = top * power + jnp.log2(total)
        both_stats = jnp.where(lane_grid == 0, level, dot)
        stats[h, f + 1, 1] = both_stats.T[0:8]
        return carry

    lax.fori_loop(0, groups * 2, query_step, 0)

    def giving(o, k):
        spot = pl.ds(pl.multiple_of(peers[k] * 32, 32), 32)
        return pltpu.make_async_remote_copy(
            src_ref=own.at[o, :, :, spot],
            dst_ref=back.at[o, pl.ds(x_at * groups, groups)],
            send_sem=o_send.at[o, k - 1],
            recv_sem=o_recv.at[o, k - 1],
            device_id=(f_at, r_at, peers[k]),
            device_id_type=MESH,
        )

    def taking(o, k):
        return pltpu.make_async_remote_copy(
            src_ref=own.at[o, :, :, pl.ds(0, 32)],
            dst_ref=back.at[o, pl.ds(froms[k] * groups, groups)],
            send_sem=o_send.at[o, k - 1],
            recv_sem=o_recv.at[o, k - 1],
            device_id=(f_at, r_at, froms[k]),
            device_id_type=MESH,
        )

    def give(o):
        for k in range(1, heads):
            giving(o, k).start()
        spot = pl.ds(pl.multiple_of(x_at * 32, 32), 32)
        back[o, pl.ds(x_at * groups, groups)] = own[o, :, :, spot]

    def storing(o):
        return pltpu.make_async_copy(land.at[o], outs[o], out_sem.at[o])

    def finish(o):
        for k in range(1, heads):
            taking(o, k).wait_recv()
        for g in range(4):
            part = back[o, :, g // 2, pl.ds(16 * (g % 2), 16)].reshape(tall, 128)
            land[o, pl.ds(g * tall, tall)] = nn(to_rows, part).astype(jnp.bfloat16)
        storing(o).start()

    first_halo(4)
    give(0)
    give(1)
    second_halo(4)
    last_halo(QRY)
    last_halo(GRD)
    finish(0)
    finish(1)
    last_halo(4)

    def key_step(i, carry):
        h, f = i // 2, i % 2
        k = wide[KEY, h, f + 1, 1]
        v = wide[VAL, h, f + 1, 1]
        q_band = wide[QRY, h, pl.ds(f, 3)].reshape(9 * 128, 128)
        g_band = wide[GRD, h, pl.ds(f, 3)].reshape(9 * 128, 128)
        shifts, dots = [[], []], []
        for a in range(3):
            for b in range(3):
                pack_here = stats[h, f + a, b]
                level, dot = pack_here[0:1], pack_here[1:2]
                dots.append(dot)
                for l in range(2):
                    pieces = [
                        entry(f + a, b, l, 9 * (2 - a) + 3 * (2 - b) + l - m + 1) for m in range(2)
                    ]
                    shifts[l].append(jnp.where(lanes < 64, pieces[0], pieces[1]) - level)
        shift = jnp.concatenate([jnp.concatenate(s, axis=1)[None] for s in shifts], axis=0)
        dot_row = jnp.concatenate(dots, axis=1)
        s = nt(k, q_band) * power
        p = jnp.exp2(s.reshape(2, 64, 9 * 128) + shift).reshape(128, 9 * 128)
        own[3, h, f] = nn(p.astype(jnp.bfloat16), g_band).astype(jnp.bfloat16)
        dp = nt(v, g_band)
        ds = (p * (dp - dot_row)).astype(jnp.bfloat16)
        own[2, h, f] = (nn(ds, q_band) * scaling).astype(jnp.bfloat16)
        return carry

    lax.fori_loop(0, groups * 2, key_step, 0)
    give(2)
    give(3)
    finish(2)
    finish(3)

    for t in range(4):
        for k in range(1, heads):
            exchange(t, k).wait_send()
            giving(t, k).wait_send()
    for t in range(5):
        halo_sent(t)
    for o in range(4):
        storing(o).wait()


def on_device(sizes, queries, keys, values, out_grad, active):
    frames, rows, heads, groups, scaling = sizes
    frames_here, rows_here, cols_here, heads_all, head_dim = queries.shape
    f_at = lax.axis_index("frame")
    r_at = lax.axis_index("row")
    padded = jnp.pad(active, ((1, 1), (1, 1), (0, 0), (0, 0)))
    near = lax.dynamic_slice(
        padded, (f_at * 2, r_at, 0, 0), (4, 3, active.shape[2], active.shape[3])
    )
    bias = ((1 - near).astype(jnp.float32) * NEG).reshape(-1)
    tall = frames_here * rows_here * cols_here * heads_all

    def flat(tensor):
        return jnp.transpose(tensor, (0, 1, 3, 2, 4)).reshape(tall, head_dim)

    def unflat(tensor):
        shaped = tensor.reshape(frames_here, rows_here, heads_all, cols_here, head_dim)
        return jnp.transpose(shaped, (0, 1, 3, 2, 4))

    dma = pltpu.SemaphoreType.DMA
    block = (128, head_dim)
    kinds = heads - 1
    anywhere = pl.BlockSpec(memory_space=pl.ANY)
    results = pl.pallas_call(
        functools.partial(tile_kernel, sizes),
        out_shape=[jax.ShapeDtypeStruct((tall, head_dim), jnp.bfloat16)] * 4,
        in_specs=[pl.BlockSpec(memory_space=pltpu.SMEM)] + [anywhere] * 4,
        out_specs=[anywhere] * 4,
        scratch_shapes=[
            pltpu.VMEM((4, tall, head_dim), jnp.bfloat16),
            pltpu.VMEM((4, heads_all, 2, 32, head_dim), jnp.bfloat16),
            pltpu.VMEM((4, groups, 4, 3) + block, jnp.bfloat16),
            pltpu.VMEM((groups, 4, 3, 8, 128), jnp.float32),
            pltpu.VMEM((4, groups, 2) + block, jnp.bfloat16),
            pltpu.VMEM((4, heads_all, 2, 32, head_dim), jnp.bfloat16),
            dma((4,)),
            dma((4, kinds)),
            dma((4, kinds)),
            dma((5, 2)),
            dma((5, 2)),
            dma((5, 2)),
            dma((5, 2)),
            dma((5, 4)),
            dma((5, 4)),
            dma((4, kinds)),
            dma((4, kinds)),
            dma((4,)),
        ],
        compiler_params=pltpu.CompilerParams(
            collective_id=0, has_side_effects=True, vmem_limit_bytes=48 << 20
        ),
    )(bias, flat(keys), flat(values), flat(queries), flat(out_grad))
    return tuple(unflat(r) for r in results)


def solution(mesh):
    frames, rows, heads = (mesh.shape[a] for a in ("frame", "row", "head"))
    sizes = (frames, rows, heads, 12 // heads, 128**-0.5)
    spec = P("frame", "row", "head", None, None)
    return jax.shard_map(
        functools.partial(on_device, sizes),
        mesh=mesh,
        in_specs=(spec,) * 4 + (P(),),
        out_specs=(spec,) * 4,
        check_vma=False,
    )
```

```python
import functools
import math

import jax
import jax.numpy as jnp
from jax import lax
from jax.experimental import pallas as pl
from jax.experimental.pallas import tpu as pltpu
from jax.sharding import PartitionSpec as P

MESH = pl.DeviceIdType.MESH
NEG = -1e30
KEY, VAL, QRY, GRD = 0, 1, 2, 3
SLOTS = 27


def nt(left, right):
    return lax.dot_general(
        left, right, (((1,), (1,)), ((), ())), preferred_element_type=jnp.float32
    )


def nn(left, right):
    return jnp.dot(left, right, preferred_element_type=jnp.float32)


def tile_kernel(sizes, bias, k_in, v_in, q_in, g_in, *refs):
    frames, rows, heads, groups, scaling = sizes
    outs, refs = refs[:4], refs[4:]
    land, pack, wide, stats, own, back, relay = refs[:7]
    in_sem, a_send, a_recv, z_send, z_recv, c_send, c_recv, d_send, d_recv = refs[7:16]
    o_send, o_recv, out_sem, leg_send, leg_recv = refs[16:21]
    ins = (k_in, v_in, q_in, g_in)
    heads_all = groups * heads
    tall = heads_all * 16

    f_at = lax.axis_index("frame")
    r_at = lax.axis_index("row")
    x_at = lax.axis_index("head")
    up, down = f_at < frames - 1, f_at > 0
    right, left = r_at < rows - 1, r_at > 0
    far_up, far_down = f_at == frames // 2 - 1, f_at == frames // 2
    both = jnp.logical_and
    near_up = both(up, jnp.logical_not(far_up))
    near_down = both(down, jnp.logical_not(far_down))
    far = jnp.logical_or(far_up, far_down)

    half, turn = frames // 2, 2 * rows
    upper, place = f_at // half, f_at % half
    core, column = f_at % 2, place // 2
    z_at = upper * rows + r_at
    first_relay = core + upper == 1
    shifted = lax.rem(z_at + rows * (1 - core), turn)
    odd = lax.rem(shifted, 2)
    began = jnp.where(odd == 1, shifted - (rows - 1), lax.rem(shifted + turn - rows - 1, turn))
    second_relay = both(began >= 0, began < rows) & (lax.rem(began + turn, 2) == 1 - odd)

    def far_spot(z):
        return lax.rem(z + rows - 1 + 2 * lax.rem(r_at, 2), turn)

    def relays_of(z, member):
        spot = far_spot(z)
        return (spot // rows) * half + member, lax.rem(spot, rows)

    def start_relay(t):
        return upper * half + 2 * t + core, r_at

    peers = [lax.rem(x_at + k, heads) for k in range(heads)]
    froms = [lax.rem(x_at + heads - k, heads) for k in range(heads)]

    def loading(t):
        return pltpu.make_async_copy(ins[t], land.at[t], in_sem.at[t])

    for t in range(4):
        loading(t).start()

    barrier = pltpu.get_barrier_semaphore()

    def greet(frame, row, head):
        pl.semaphore_signal(barrier, inc=1, device_id=(frame, row, head), device_id_type=MESH)

    for k in range(1, heads):
        greet(f_at, r_at, peers[k])
    pl.when(right)(lambda: greet(f_at, r_at + 1, x_at))
    pl.when(left)(lambda: greet(f_at, r_at - 1, x_at))
    pl.when(up)(lambda: greet(f_at + 1, r_at, x_at))
    pl.when(down)(lambda: greet(f_at - 1, r_at, x_at))
    origin = (half - 1 + upper, r_at)
    next_relay = relays_of(z_at, place)
    last_from = ((1 - core) * half + place, began)
    last_to = (half - 1 + core, began)

    @pl.when(far)
    def _():
        for t in range(4):
            pl.when(column != t)(lambda: greet(*start_relay(t), x_at))
            greet(*relays_of(z_at + rows, 2 * t + 1 - core), x_at)

    pl.when(both(first_relay, jnp.logical_not(far)))(lambda: greet(*origin, x_at))
    pl.when(first_relay)(lambda: greet(*next_relay, x_at))

    @pl.when(second_relay)
    def _():
        greet(*last_from, x_at)
        greet(*last_to, x_at)


    @pl.when(jnp.logical_not(left))
    def _():
        wide[:, :, :, 0] = jnp.zeros_like(wide[:, :, :, 0])
        stats[:, :, 0] = jnp.zeros_like(stats[:, :, 0])

    @pl.when(jnp.logical_not(right))
    def _():
        wide[:, :, :, 2] = jnp.zeros_like(wide[:, :, :, 2])
        stats[:, :, 2] = jnp.zeros_like(stats[:, :, 2])

    @pl.when(jnp.logical_not(down))
    def _():
        wide[:, :, 0] = jnp.zeros_like(wide[:, :, 0])
        stats[:, 0] = jnp.zeros_like(stats[:, 0])

    @pl.when(jnp.logical_not(up))
    def _():
        wide[:, :, 3] = jnp.zeros_like(wide[:, :, 3])
        stats[:, 3] = jnp.zeros_like(stats[:, 3])

    out_row = lax.broadcasted_iota(jnp.int32, (tall, tall), 0)
    in_row = lax.broadcasted_iota(jnp.int32, (tall, tall), 1)

    def swapped(row):
        return ((row % 16) // 4) * (4 * heads_all) + (row // 16) * 4 + row % 4

    to_heads = (swapped(out_row) == in_row).astype(jnp.bfloat16)
    to_rows = (swapped(in_row) == out_row).astype(jnp.bfloat16)

    def exchange(t, k):
        there = peers[k]
        return pltpu.make_async_remote_copy(
            src_ref=pack.at[t, pl.ds(there * groups, groups)],
            dst_ref=wide.at[t, :, pl.ds(1, 2), 1, pl.ds(pl.multiple_of(x_at * 32, 32), 32)],
            send_sem=a_send.at[t, k - 1],
            recv_sem=a_recv.at[t, k - 1],
            device_id=(f_at, r_at, there),
            device_id_type=MESH,
        )

    def arriving(t, k):
        spot = pl.ds(pl.multiple_of(froms[k] * 32, 32), 32)
        return pltpu.make_async_remote_copy(
            src_ref=pack.at[t, pl.ds(0, groups)],
            dst_ref=wide.at[t, :, pl.ds(1, 2), 1, spot],
            send_sem=a_send.at[t, k - 1],
            recv_sem=a_recv.at[t, k - 1],
            device_id=(f_at, r_at, froms[k]),
            device_id_type=MESH,
        )

    def block(t, frame, row):
        ref = stats if t == 4 else wide.at[t]
        return ref.at[:, frame, row]

    def pair(t, row):
        ref = stats if t == 4 else wide.at[t]
        return ref.at[:, pl.ds(1, 2), row]

    def hop(src, dst, ss, rs, frame, row):
        return pltpu.make_async_remote_copy(
            src_ref=src,
            dst_ref=dst,
            send_sem=ss,
            recv_sem=rs,
            device_id=(frame, row, x_at),
            device_id_type=MESH,
        )

    def to_right(t):
        return hop(pair(t, 1), pair(t, 0), z_send.at[t, 0], z_recv.at[t, 0], f_at, r_at + 1)

    def to_left(t):
        return hop(pair(t, 1), pair(t, 2), z_send.at[t, 1], z_recv.at[t, 1], f_at, r_at - 1)

    def to_up(t):
        return hop(block(t, 2, 1), block(t, 0, 1), c_send.at[t, 0], c_recv.at[t, 0], f_at + 1, r_at)

    def to_down(t):
        return hop(block(t, 1, 1), block(t, 3, 1), c_send.at[t, 1], c_recv.at[t, 1], f_at - 1, r_at)

    def side_up(t, row):
        sem = 0 if row == 0 else 1
        return hop(
            block(t, 2, row), block(t, 0, row), d_send.at[t, sem], d_recv.at[t, sem], f_at + 1, r_at
        )

    def side_down(t, row):
        sem = 2 if row == 0 else 3
        return hop(
            block(t, 1, row), block(t, 3, row), d_send.at[t, sem], d_recv.at[t, sem], f_at - 1, r_at
        )

    def along_right(t, frame):
        sem = 0 if frame == 0 else 2
        return hop(
            block(t, frame, 1), block(t, frame, 0), d_send.at[t, sem], d_recv.at[t, sem], f_at, r_at + 1
        )

    def along_left(t, frame):
        sem = 1 if frame == 0 else 3
        return hop(
            block(t, frame, 1), block(t, frame, 2), d_send.at[t, sem], d_recv.at[t, sem], f_at, r_at - 1
        )

    edge = jnp.where(far_up, 2, 1)

    def leg_one(t):
        return hop(
            block(t, edge, 1), relay.at[0], leg_send.at[t], leg_recv.at[0], *start_relay(t)
        )

    def leg_two(src):
        return hop(src, relay.at[1], leg_send.at[4], leg_recv.at[1], *next_relay)

    def leg_three(t):
        side = 1 - core
        return hop(
            relay.at[1], block(t, 3 * side, 1), leg_send.at[5], c_recv.at[t, side], *last_to
        )

    def first_halo(t):
        out_up, out_down = (up, down) if t == 4 else (near_up, near_down)
        if t < 4:
            pl.when(both(far, column != t))(lambda: leg_one(t).start())
        pl.when(right)(lambda: to_right(t).start())
        pl.when(left)(lambda: to_left(t).start())
        pl.when(out_up)(lambda: to_up(t).start())
        pl.when(out_down)(lambda: to_down(t).start())

    def relay_one(t):
        here = both(first_relay, column == t)

        @pl.when(both(here, jnp.logical_not(far)))
        def _():
            leg_one(t).wait_recv()
            leg_two(relay.at[0]).start()

        pl.when(both(here, far))(lambda: leg_two(block(t, edge, 1)).start())

    def relay_two(t):
        @pl.when(both(second_relay, column == t))
        def _():
            leg_two(relay.at[0]).wait_recv()
            leg_three(t).start()

    def second_halo(t):
        pl.when(left)(lambda: to_right(t).wait_recv())
        pl.when(right)(lambda: to_left(t).wait_recv())
        pl.when(both(near_up, left))(lambda: side_up(t, 0).start())
        pl.when(both(near_up, right))(lambda: side_up(t, 2).start())
        pl.when(both(near_down, left))(lambda: side_down(t, 0).start())
        pl.when(both(near_down, right))(lambda: side_down(t, 2).start())

    def far_halo(t):
        pl.when(far_down)(lambda: to_up(t).wait_recv())
        pl.when(far_up)(lambda: to_down(t).wait_recv())
        pl.when(both(far_down, right))(lambda: along_right(t, 0).start())
        pl.when(both(far_down, left))(lambda: along_left(t, 0).start())
        pl.when(both(far_up, right))(lambda: along_right(t, 3).start())
        pl.when(both(far_up, left))(lambda: along_left(t, 3).start())

    def low_halo(t):
        pl.when(near_down)(lambda: to_up(t).wait_recv())
        pl.when(both(down, left))(lambda: side_up(t, 0).wait_recv())
        pl.when(both(down, right))(lambda: side_up(t, 2).wait_recv())

    def high_halo(t):
        pl.when(near_up)(lambda: to_down(t).wait_recv())
        pl.when(both(up, left))(lambda: side_down(t, 0).wait_recv())
        pl.when(both(up, right))(lambda: side_down(t, 2).wait_recv())

    def early_halo(*kinds):
        @pl.when(jnp.logical_not(far_down))
        def _():
            for t in kinds:
                low_halo(t)

        @pl.when(far_down)
        def _():
            for t in kinds:
                high_halo(t)

    def late_halo(*kinds):
        @pl.when(far_down)
        def _():
            for t in kinds:
                low_halo(t)

        @pl.when(jnp.logical_not(far_down))
        def _():
            for t in kinds:
                high_halo(t)

    def halo_sent(t):
        out_up, out_down = (up, down) if t == 4 else (near_up, near_down)
        if t < 4:
            pl.when(both(far, column != t))(lambda: leg_one(t).wait_send())
        pl.when(out_up)(lambda: to_up(t).wait_send())
        pl.when(out_down)(lambda: to_down(t).wait_send())
        pl.when(right)(lambda: to_right(t).wait_send())
        pl.when(left)(lambda: to_left(t).wait_send())
        pl.when(both(near_up, left))(lambda: side_up(t, 0).wait_send())
        pl.when(both(near_up, right))(lambda: side_up(t, 2).wait_send())
        pl.when(both(near_down, left))(lambda: side_down(t, 0).wait_send())
        pl.when(both(near_down, right))(lambda: side_down(t, 2).wait_send())
        pl.when(both(far_down, right))(lambda: along_right(t, 0).wait_send())
        pl.when(both(far_down, left))(lambda: along_left(t, 0).wait_send())
        pl.when(both(far_up, right))(lambda: along_right(t, 3).wait_send())
        pl.when(both(far_up, left))(lambda: along_left(t, 3).wait_send())

    for t in range(4):
        loading(t).wait()
        for g in range(4):
            part = nn(to_heads, land[t, pl.ds(g * tall, tall)]).astype(jnp.bfloat16)
            pack[t, :, g // 2, pl.ds(16 * (g % 2), 16)] = part.reshape(heads_all, 16, 128)
        if t == 0:
            known = [right, left, up, down, both(first_relay, jnp.logical_not(far)), first_relay]
            count = heads - 1 + sum(c.astype(jnp.int32) for c in known)
            count += 2 * second_relay.astype(jnp.int32) + 7 * far.astype(jnp.int32)
            pl.semaphore_wait(barrier, count)
        for k in range(1, heads):
            exchange(t, k).start()
        wide[t, :, pl.ds(1, 2), 1, pl.ds(pl.multiple_of(x_at * 32, 32), 32)] = pack[
            t, pl.ds(x_at * groups, groups)
        ]

    def gathered(t):
        for k in range(1, heads):
            arriving(t, k).wait_recv()

    gathered(KEY)
    first_halo(KEY)
    gathered(VAL)
    first_halo(VAL)
    relay_one(KEY)
    second_halo(KEY)
    gathered(QRY)
    first_halo(QRY)
    relay_one(VAL)
    second_halo(VAL)
    gathered(GRD)
    first_halo(GRD)
    relay_one(QRY)
    relay_two(KEY)
    second_halo(QRY)
    relay_one(GRD)
    relay_two(VAL)
    second_halo(GRD)
    early_halo(KEY, VAL)

    flip = far_down.astype(jnp.int32)
    lanes = lax.broadcasted_iota(jnp.int32, (1, 128), 1)
    lane_grid = lax.broadcasted_iota(jnp.int32, (128, 128), 1)
    power = scaling * math.log2(math.e)

    def entry(i, j, l, slot):
        return bias[((i * 3 + j) * 2 + l) * SLOTS + slot]

    def query_step(i, carry):
        h, f = i % groups, (i // groups) ^ flip
        q = wide[QRY, h, f + 1, 1]
        g = wide[GRD, h, f + 1, 1]
        k_band = wide[KEY, h, pl.ds(f, 3)].reshape(9 * 128, 128)
        v_band = wide[VAL, h, pl.ds(f, 3)].reshape(9 * 128, 128)
        masks = []
        for l in range(2):
            cells = []
            for a in range(3):
                for b in range(3):
                    frame = 2 * f_at + f + a - 1
                    row = r_at + b - 1
                    inside = (frame >= 0) & (frame < 2 * frames) & (row >= 0) & (row < rows)
                    pieces = []
                    for m in range(2):
                        value = entry(f + 1, 1, l, 9 * a + 3 * b + m - l + 1)
                        pieces.append(jnp.where(inside, value, NEG))
                    cells.append(jnp.where(lanes < 64, pieces[0], pieces[1]))
            masks.append(jnp.concatenate(cells, axis=1))
        mask = jnp.concatenate([m[None] for m in masks], axis=0)
        s = nt(q, k_band)
        s = (s.reshape(2, 64, 9 * 128) + mask).reshape(128, 9 * 128)
        top = jnp.max(s, axis=1, keepdims=True)
        p = jnp.exp2((s - top) * power)
        total = jnp.sum(p, axis=1, keepdims=True)
        inverse = 1.0 / total
        out = (nn(p.astype(jnp.bfloat16), v_band) * inverse).astype(jnp.bfloat16)
        own[0, h, f] = out
        dot = jnp.sum(g.astype(jnp.float32) * out.astype(jnp.float32), axis=1, keepdims=True)
        dp = nt(g, v_band)
        ds = (p * (dp - dot)).astype(jnp.bfloat16)
        own[1, h, f] = (nn(ds, k_band) * (inverse * scaling)).astype(jnp.bfloat16)
        level = top * power + jnp.log2(total)
        both_stats = jnp.where(lane_grid == 0, level, dot)
        stats[h, f + 1, 1] = both_stats.T[0:8]
        return carry

    lax.fori_loop(0, groups, query_step, 0)
    relay_two(QRY)
    relay_two(GRD)
    far_halo(KEY)
    far_halo(VAL)
    late_halo(KEY, VAL)
    lax.fori_loop(groups, groups * 2, query_step, 0)

    def giving(o, k):
        spot = pl.ds(pl.multiple_of(peers[k] * 32, 32), 32)
        return pltpu.make_async_remote_copy(
            src_ref=own.at[o, :, :, spot],
            dst_ref=back.at[o, pl.ds(x_at * groups, groups)],
            send_sem=o_send.at[o, k - 1],
            recv_sem=o_recv.at[o, k - 1],
            device_id=(f_at, r_at, peers[k]),
            device_id_type=MESH,
        )

    def taking(o, k):
        return pltpu.make_async_remote_copy(
            src_ref=own.at[o, :, :, pl.ds(0, 32)],
            dst_ref=back.at[o, pl.ds(froms[k] * groups, groups)],
            send_sem=o_send.at[o, k - 1],
            recv_sem=o_recv.at[o, k - 1],
            device_id=(f_at, r_at, froms[k]),
            device_id_type=MESH,
        )

    def give(o):
        for k in range(1, heads):
            giving(o, k).start()
        spot = pl.ds(pl.multiple_of(x_at * 32, 32), 32)
        back[o, pl.ds(x_at * groups, groups)] = own[o, :, :, spot]

    def storing(o):
        return pltpu.make_async_copy(land.at[o], outs[o], out_sem.at[o])

    def finish(o):
        for k in range(1, heads):
            taking(o, k).wait_recv()
        for g in range(4):
            part = back[o, :, g // 2, pl.ds(16 * (g % 2), 16)].reshape(tall, 128)
            land[o, pl.ds(g * tall, tall)] = nn(to_rows, part).astype(jnp.bfloat16)
        storing(o).start()

    first_halo(4)
    far_halo(QRY)
    far_halo(GRD)
    give(0)
    give(1)
    second_halo(4)
    early_halo(QRY, GRD, 4)

    def key_step(i, carry):
        h, f = i % groups, (i // groups) ^ flip
        k = wide[KEY, h, f + 1, 1]
        v = wide[VAL, h, f + 1, 1]
        q_band = wide[QRY, h, pl.ds(f, 3)].reshape(9 * 128, 128)
        g_band = wide[GRD, h, pl.ds(f, 3)].reshape(9 * 128, 128)
        shifts, dots = [[], []], []
        for a in range(3):
            for b in range(3):
                pack_here = stats[h, f + a, b]
                level, dot = pack_here[0:1], pack_here[1:2]
                dots.append(dot)
                for l in range(2):
                    pieces = [
                        entry(f + a, b, l, 9 * (2 - a) + 3 * (2 - b) + l - m + 1) for m in range(2)
                    ]
                    shifts[l].append(jnp.where(lanes < 64, pieces[0], pieces[1]) - level)
        shift = jnp.concatenate([jnp.concatenate(s, axis=1)[None] for s in shifts], axis=0)
        dot_row = jnp.concatenate(dots, axis=1)
        s = nt(k, q_band) * power
        p = jnp.exp2(s.reshape(2, 64, 9 * 128) + shift).reshape(128, 9 * 128)
        own[3, h, f] = nn(p.astype(jnp.bfloat16), g_band).astype(jnp.bfloat16)
        dp = nt(v, g_band)
        ds = (p * (dp - dot_row)).astype(jnp.bfloat16)
        own[2, h, f] = (nn(ds, q_band) * scaling).astype(jnp.bfloat16)
        return carry

    lax.fori_loop(0, groups, key_step, 0)
    far_halo(4)
    late_halo(QRY, GRD, 4)
    lax.fori_loop(groups, groups * 2, key_step, 0)
    give(2)
    give(3)
    finish(0)
    finish(1)
    finish(2)
    finish(3)

    for t in range(4):
        for k in range(1, heads):
            exchange(t, k).wait_send()
            giving(t, k).wait_send()
    for t in range(5):
        halo_sent(t)
    pl.when(first_relay)(lambda: leg_two(relay.at[0]).wait_send())
    pl.when(second_relay)(lambda: leg_three(0).wait_send())
    for o in range(4):
        storing(o).wait()


def on_device(sizes, queries, keys, values, out_grad, active):
    frames, rows, heads, groups, scaling = sizes
    frames_here, rows_here, cols_here, heads_all, head_dim = queries.shape
    f_at = lax.axis_index("frame")
    r_at = lax.axis_index("row")
    padded = jnp.pad(active, ((1, 1), (1, 1), (0, 0), (0, 0)))
    near = lax.dynamic_slice(
        padded, (f_at * 2, r_at, 0, 0), (4, 3, active.shape[2], active.shape[3])
    )
    bias = ((1 - near).astype(jnp.float32) * NEG).reshape(-1)
    tall = frames_here * rows_here * cols_here * heads_all

    def flat(tensor):
        return jnp.transpose(tensor, (0, 1, 3, 2, 4)).reshape(tall, head_dim)

    def unflat(tensor):
        shaped = tensor.reshape(frames_here, rows_here, heads_all, cols_here, head_dim)
        return jnp.transpose(shaped, (0, 1, 3, 2, 4))

    dma = pltpu.SemaphoreType.DMA
    block = (128, head_dim)
    kinds = heads - 1
    anywhere = pl.BlockSpec(memory_space=pl.ANY)
    results = pl.pallas_call(
        functools.partial(tile_kernel, sizes),
        out_shape=[jax.ShapeDtypeStruct((tall, head_dim), jnp.bfloat16)] * 4,
        in_specs=[pl.BlockSpec(memory_space=pltpu.SMEM)] + [anywhere] * 4,
        out_specs=[anywhere] * 4,
        scratch_shapes=[
            pltpu.VMEM((4, tall, head_dim), jnp.bfloat16),
            pltpu.VMEM((4, heads_all, 2, 32, head_dim), jnp.bfloat16),
            pltpu.VMEM((4, groups, 4, 3) + block, jnp.bfloat16),
            pltpu.VMEM((groups, 4, 3, 8, 128), jnp.float32),
            pltpu.VMEM((4, groups, 2) + block, jnp.bfloat16),
            pltpu.VMEM((4, heads_all, 2, 32, head_dim), jnp.bfloat16),
            pltpu.VMEM((2, groups) + block, jnp.bfloat16),
            dma((4,)),
            dma((4, kinds)),
            dma((4, kinds)),
            dma((5, 2)),
            dma((5, 2)),
            dma((5, 2)),
            dma((5, 2)),
            dma((5, 4)),
            dma((5, 4)),
            dma((4, kinds)),
            dma((4, kinds)),
            dma((4,)),
            dma((6,)),
            dma((2,)),
        ],
        compiler_params=pltpu.CompilerParams(
            collective_id=0, has_side_effects=True, vmem_limit_bytes=48 << 20
        ),
    )(bias, flat(keys), flat(values), flat(queries), flat(out_grad))
    return tuple(unflat(r) for r in results)


def solution(mesh):
    frames, rows, heads = (mesh.shape[a] for a in ("frame", "row", "head"))
    sizes = (frames, rows, heads, 12 // heads, 128**-0.5)
    spec = P("frame", "row", "head", None, None)
    return jax.shard_map(
        functools.partial(on_device, sizes),
        mesh=mesh,
        in_specs=(spec,) * 4 + (P(),),
        out_specs=(spec,) * 4,
        check_vma=False,
    )
```

```python
import functools
import math

import jax
import jax.numpy as jnp
from jax import lax
from jax.experimental import pallas as pl
from jax.experimental.pallas import tpu as pltpu
from jax.sharding import PartitionSpec as P

MESH = pl.DeviceIdType.MESH
NEG = -1e30
KEY, VAL, QRY, GRD = 0, 1, 2, 3
SLOTS = 27


def nt(left, right):
    return lax.dot_general(
        left, right, (((1,), (1,)), ((), ())), preferred_element_type=jnp.float32
    )


def nn(left, right):
    return jnp.dot(left, right, preferred_element_type=jnp.float32)


def tile_kernel(sizes, act_in, k_in, v_in, q_in, g_in, *refs):
    frames, rows, heads, groups, scaling = sizes
    outs, refs = refs[:4], refs[4:]
    land, pack, wide, stats, own, back, part, front, behind, across, act = refs[:11]
    in_sem, a_send, a_recv, z_send, z_recv, c_send, c_recv, d_send, d_recv = refs[11:20]
    o_send, o_recv, out_sem, part_sem, act_sem, ready = refs[20:26]
    ins = (k_in, v_in, q_in, g_in)
    heads_all = groups * heads
    tall = heads_all * 16

    f_at = lax.axis_index("frame")
    r_at = lax.axis_index("row")
    x_at = lax.axis_index("head")
    up, down = f_at < frames - 1, f_at > 0
    right, left = r_at < rows - 1, r_at > 0
    far_up, far_down = f_at == frames // 2 - 1, f_at == frames // 2
    both = jnp.logical_and
    near_up = both(up, jnp.logical_not(far_up))
    near_down = both(down, jnp.logical_not(far_down))
    far = jnp.logical_or(far_up, far_down)

    half = frames // 2
    spread = min(3, half - 1)
    proxy_up, proxy_down = f_at == half - 1 - spread, f_at == half + spread
    proxy = jnp.logical_or(proxy_up, proxy_down)
    edge = far_up.astype(jnp.int32)
    beyond = 3 * edge
    flip = far_down.astype(jnp.int32)

    peers = [lax.rem(x_at + k, heads) for k in range(heads)]
    froms = [lax.rem(x_at + heads - k, heads) for k in range(heads)]

    def loading(t):
        return pltpu.make_async_copy(ins[t], land.at[t], in_sem.at[t])

    def loading_act(j):
        row = jnp.clip(r_at - 1 + j, 0, rows - 1)
        return pltpu.make_async_copy(act_in.at[row], act.at[j], act_sem.at[j])

    for t in range(4):
        loading(t).start()
    for j in range(3):
        loading_act(j).start()

    barrier = pltpu.get_barrier_semaphore()

    def greet(frame, row, head):
        pl.semaphore_signal(barrier, inc=1, device_id=(frame, row, head), device_id_type=MESH)

    for k in range(1, heads):
        greet(f_at, r_at, peers[k])
    pl.when(right)(lambda: greet(f_at, r_at + 1, x_at))
    pl.when(left)(lambda: greet(f_at, r_at - 1, x_at))
    pl.when(near_up)(lambda: greet(f_at + 1, r_at, x_at))
    pl.when(near_down)(lambda: greet(f_at - 1, r_at, x_at))

    @pl.when(far)
    def _():
        greet(jnp.where(far_up, half - 1 - spread, half + spread), r_at, x_at)
        greet(jnp.where(far_up, half + spread, half - 1 - spread), r_at, x_at)

    @pl.when(jnp.logical_not(left))
    def _():
        wide[:, :, :, 0] = jnp.zeros_like(wide[:, :, :, 0])
        stats[:, :, 0] = jnp.zeros_like(stats[:, :, 0])

    @pl.when(jnp.logical_not(right))
    def _():
        wide[:, :, :, 2] = jnp.zeros_like(wide[:, :, :, 2])
        stats[:, :, 2] = jnp.zeros_like(stats[:, :, 2])

    @pl.when(jnp.logical_not(down))
    def _():
        wide[:, :, 0] = jnp.zeros_like(wide[:, :, 0])
        stats[:, 0] = jnp.zeros_like(stats[:, 0])

    @pl.when(jnp.logical_not(up))
    def _():
        wide[:, :, 3] = jnp.zeros_like(wide[:, :, 3])
        stats[:, 3] = jnp.zeros_like(stats[:, 3])

    out_row = lax.broadcasted_iota(jnp.int32, (tall, tall), 0)
    in_row = lax.broadcasted_iota(jnp.int32, (tall, tall), 1)

    def swapped(row):
        return ((row % 16) // 4) * (4 * heads_all) + (row // 16) * 4 + row % 4

    to_heads = (swapped(out_row) == in_row).astype(jnp.bfloat16)
    to_rows = (swapped(in_row) == out_row).astype(jnp.bfloat16)

    def exchange(t, k):
        there = peers[k]
        return pltpu.make_async_remote_copy(
            src_ref=pack.at[t, pl.ds(there * groups, groups)],
            dst_ref=wide.at[t, :, pl.ds(1, 2), 1, pl.ds(pl.multiple_of(x_at * 32, 32), 32)],
            send_sem=a_send.at[t, k - 1],
            recv_sem=a_recv.at[t, k - 1],
            device_id=(f_at, r_at, there),
            device_id_type=MESH,
        )

    def arriving(t, k):
        spot = pl.ds(pl.multiple_of(froms[k] * 32, 32), 32)
        return pltpu.make_async_remote_copy(
            src_ref=pack.at[t, pl.ds(0, groups)],
            dst_ref=wide.at[t, :, pl.ds(1, 2), 1, spot],
            send_sem=a_send.at[t, k - 1],
            recv_sem=a_recv.at[t, k - 1],
            device_id=(f_at, r_at, froms[k]),
            device_id_type=MESH,
        )

    def block(t, frame, row):
        ref = stats if t == 4 else wide.at[t]
        return ref.at[:, frame, row]

    def pair(t, row):
        ref = stats if t == 4 else wide.at[t]
        return ref.at[:, pl.ds(1, 2), row]

    def hop(src, dst, ss, rs, frame, row):
        return pltpu.make_async_remote_copy(
            src_ref=src,
            dst_ref=dst,
            send_sem=ss,
            recv_sem=rs,
            device_id=(frame, row, x_at),
            device_id_type=MESH,
        )

    def to_right(t):
        return hop(pair(t, 1), pair(t, 0), z_send.at[t, 0], z_recv.at[t, 0], f_at, r_at + 1)

    def to_left(t):
        return hop(pair(t, 1), pair(t, 2), z_send.at[t, 1], z_recv.at[t, 1], f_at, r_at - 1)

    def to_up(t):
        return hop(block(t, 2, 1), block(t, 0, 1), c_send.at[t, 0], c_recv.at[t, 0], f_at + 1, r_at)

    def to_down(t):
        return hop(block(t, 1, 1), block(t, 3, 1), c_send.at[t, 1], c_recv.at[t, 1], f_at - 1, r_at)

    def side_up(t, row):
        sem = 0 if row == 0 else 1
        return hop(
            block(t, 2, row), block(t, 0, row), d_send.at[t, sem], d_recv.at[t, sem], f_at + 1, r_at
        )

    def side_down(t, row):
        sem = 2 if row == 0 else 3
        return hop(
            block(t, 1, row), block(t, 3, row), d_send.at[t, sem], d_recv.at[t, sem], f_at - 1, r_at
        )

    def along_right(t, frame):
        sem = 0 if frame == 0 else 2
        return hop(
            block(t, frame, 1), block(t, frame, 0), d_send.at[t, sem], d_recv.at[t, sem], f_at, r_at + 1
        )

    def along_left(t, frame):
        sem = 1 if frame == 0 else 3
        return hop(
            block(t, frame, 1), block(t, frame, 2), d_send.at[t, sem], d_recv.at[t, sem], f_at, r_at - 1
        )

    def tell():
        pair_at = jnp.where(proxy_up, half - 1, half)
        pl.semaphore_signal(ready, inc=1, device_id=(pair_at, r_at, x_at), device_id_type=MESH)

    def first_halo(t):
        pl.when(right)(lambda: to_right(t).start())
        pl.when(left)(lambda: to_left(t).start())
        pl.when(near_up)(lambda: to_up(t).start())
        pl.when(near_down)(lambda: to_down(t).start())

    def summary(side):
        there = jnp.where(far_up, half, half - 1)
        return hop(part.at[0], part.at[1], part_sem.at[0], part_sem.at[1], there, r_at)

    def second_halo(t):
        pl.when(left)(lambda: to_right(t).wait_recv())
        pl.when(right)(lambda: to_left(t).wait_recv())
        pl.when(both(near_up, left))(lambda: side_up(t, 0).start())
        pl.when(both(near_up, right))(lambda: side_up(t, 2).start())
        pl.when(both(near_down, left))(lambda: side_down(t, 0).start())
        pl.when(both(near_down, right))(lambda: side_down(t, 2).start())

    def far_halo(t):
        if t < 4:
            pl.when(far_down)(lambda: to_up(t).wait_recv())
            pl.when(far_up)(lambda: to_down(t).wait_recv())
        pl.when(both(far_down, right))(lambda: along_right(t, 0).start())
        pl.when(both(far_down, left))(lambda: along_left(t, 0).start())
        pl.when(both(far_up, right))(lambda: along_right(t, 3).start())
        pl.when(both(far_up, left))(lambda: along_left(t, 3).start())

    def low_halo(t):
        pl.when(near_down)(lambda: to_up(t).wait_recv())
        pl.when(both(down, left))(lambda: side_up(t, 0).wait_recv())
        pl.when(both(down, right))(lambda: side_up(t, 2).wait_recv())

    def high_halo(t):
        pl.when(near_up)(lambda: to_down(t).wait_recv())
        pl.when(both(up, left))(lambda: side_down(t, 0).wait_recv())
        pl.when(both(up, right))(lambda: side_down(t, 2).wait_recv())

    def early_halo(*kinds):
        @pl.when(jnp.logical_not(far_down))
        def _():
            for t in kinds:
                low_halo(t)

        @pl.when(far_down)
        def _():
            for t in kinds:
                high_halo(t)

    def late_halo(*kinds):
        @pl.when(far_down)
        def _():
            for t in kinds:
                low_halo(t)

        @pl.when(jnp.logical_not(far_down))
        def _():
            for t in kinds:
                high_halo(t)

    def halo_sent(t):
        out_up, out_down = (up, down) if t < 4 else (near_up, near_down)
        pl.when(out_up)(lambda: to_up(t).wait_send())
        pl.when(out_down)(lambda: to_down(t).wait_send())
        pl.when(right)(lambda: to_right(t).wait_send())
        pl.when(left)(lambda: to_left(t).wait_send())
        pl.when(both(near_up, left))(lambda: side_up(t, 0).wait_send())
        pl.when(both(near_up, right))(lambda: side_up(t, 2).wait_send())
        pl.when(both(near_down, left))(lambda: side_down(t, 0).wait_send())
        pl.when(both(near_down, right))(lambda: side_down(t, 2).wait_send())
        pl.when(both(far_down, right))(lambda: along_right(t, 0).wait_send())
        pl.when(both(far_down, left))(lambda: along_left(t, 0).wait_send())
        pl.when(both(far_up, right))(lambda: along_right(t, 3).wait_send())
        pl.when(both(far_up, left))(lambda: along_left(t, 3).wait_send())

    for j in range(3):
        loading_act(j).wait()

    lanes = lax.broadcasted_iota(jnp.int32, (1, 128), 1)

    def placed(i, j):
        frame, row = 2 * f_at - 1 + i, r_at - 1 + j
        return (frame >= 0) & (frame < 2 * frames) & (row >= 0) & (row < rows)

    def entry(i, j, l, slot, inside):
        frame = jnp.clip(2 * f_at - 1 + i, 0, 2 * frames - 1)
        return jnp.where(inside & (act[j, slot, l, frame] == 1), 0.0, NEG)

    def halves(pair_of):
        return jnp.where(lanes < 64, pair_of[0], pair_of[1])

    def mask_step(i, carry):
        f, a = i // 3, i % 3
        for b in range(3):
            span = pl.ds(pl.multiple_of(a * 384 + b * 128, 128), 128)
            inside = placed(f + a, b)
            for l in range(2):
                slots = [9 * a + 3 * b + m - l + 1 for m in range(2)]
                front[f, l, :, span] = halves([entry(f + 1, 1, l, n, inside) for n in slots])
                slots = [9 * (2 - a) + 3 * (2 - b) + l - m + 1 for m in range(2)]
                behind[f, l, :, span] = halves([entry(f + a, b, l, n, inside) for n in slots])
        return carry

    lax.fori_loop(0, 6, mask_step, 0)

    @pl.when(far)
    def _():
        for b in range(3):
            inside = placed(edge + 1, b)
            for l in range(2):
                slots = [18 * (1 - edge) + 3 * b + l - m + 1 for m in range(2)]
                pieces = [entry(beyond, 1, m, n, inside) for m, n in enumerate(slots)]
                across[2 * b + l] = halves(pieces)

    for t in range(4):
        loading(t).wait()
        for g in range(4):
            moved = nn(to_heads, land[t, pl.ds(g * tall, tall)]).astype(jnp.bfloat16)
            pack[t, :, g // 2, pl.ds(16 * (g % 2), 16)] = moved.reshape(heads_all, 16, 128)
        if t == 0:
            known = [right, left, near_up, near_down, proxy, proxy]
            pl.semaphore_wait(barrier, heads - 1 + sum(c.astype(jnp.int32) for c in known))
            pl.when(proxy)(tell)
        for k in range(1, heads):
            exchange(t, k).start()
        wide[t, :, pl.ds(1, 2), 1, pl.ds(pl.multiple_of(x_at * 32, 32), 32)] = pack[
            t, pl.ds(x_at * groups, groups)
        ]

    def gathered(t):
        for k in range(1, heads):
            arriving(t, k).wait_recv()

    gathered(KEY)
    first_halo(KEY)
    gathered(VAL)
    first_halo(VAL)
    second_halo(KEY)
    gathered(QRY)
    first_halo(QRY)
    second_halo(VAL)
    gathered(GRD)
    first_halo(GRD)

    @pl.when(far)
    def _():
        pl.semaphore_wait(ready, 1)
        for t in range(4):
            pl.when(far_up)(lambda: to_up(t).start())
            pl.when(far_down)(lambda: to_down(t).start())

    second_halo(QRY)
    second_halo(GRD)

    lane_grid = lax.broadcasted_iota(jnp.int32, (128, 128), 1)
    power = scaling * math.log2(math.e)
    wide_rows = 9 * 128

    def as_rows(level, dot):
        return jnp.where(lane_grid == 0, level, dot).T[0:8]

    def query_step(i, carry):
        h, f = i % groups, (i // groups) ^ flip
        q = wide[QRY, h, f + 1, 1]
        g = wide[GRD, h, f + 1, 1]
        k_band = wide[KEY, h, pl.ds(f, 3)].reshape(wide_rows, 128)
        v_band = wide[VAL, h, pl.ds(f, 3)].reshape(wide_rows, 128)
        s = (nt(q, k_band).reshape(2, 64, wide_rows) + front[f]).reshape(128, wide_rows)
        top = jnp.max(s, axis=1, keepdims=True)
        p = jnp.exp2((s - top) * power)
        total = jnp.sum(p, axis=1, keepdims=True)
        inverse = 1.0 / total
        out = (nn(p.astype(jnp.bfloat16), v_band) * inverse).astype(jnp.bfloat16)
        own[0, h, f] = out
        dot = jnp.sum(g.astype(jnp.float32) * out.astype(jnp.float32), axis=1, keepdims=True)
        ds = (p * (nt(g, v_band) - dot)).astype(jnp.bfloat16)
        own[1, h, f] = (nn(ds, k_band) * (inverse * scaling)).astype(jnp.bfloat16)
        stats[h, f + 1, 1] = as_rows(top * power + jnp.log2(total), dot)
        return carry

    def near_step(h, carry):
        q = wide[QRY, h, edge + 1, 1]
        g = wide[GRD, h, edge + 1, 1]
        k_band = wide[KEY, h, pl.ds(1, 2)].reshape(6 * 128, 128)
        v_band = wide[VAL, h, pl.ds(1, 2)].reshape(6 * 128, 128)
        offset = pl.multiple_of((1 - edge) * 384, 128)
        mask = front[edge, :, :, pl.ds(offset, 768)]
        s = (nt(q, k_band).reshape(2, 64, 768) + mask).reshape(128, 768)
        top = jnp.max(s, axis=1, keepdims=True)
        p = jnp.exp2((s - top) * power)
        total = jnp.sum(p, axis=1, keepdims=True)
        dot = jnp.sum(p * nt(g, v_band), axis=1, keepdims=True) / total
        part[0, h] = as_rows(top * power + jnp.log2(total), dot)
        return carry

    def across_step(h, carry):
        q = wide[QRY, h, beyond, 1]
        g = wide[GRD, h, beyond, 1]
        k_band = wide[KEY, h, edge + 1].reshape(384, 128)
        v_band = wide[VAL, h, edge + 1].reshape(384, 128)
        s = ((nt(k_band, q) * power).reshape(6, 64, 128) + across[...]).reshape(384, 128)
        top = jnp.max(s, axis=0, keepdims=True)
        p = jnp.exp2(s - top)
        total = jnp.sum(p, axis=0, keepdims=True)
        dot = jnp.sum(p * nt(v_band, g), axis=0, keepdims=True) / total
        level = top + jnp.log2(total)
        level_near, dot_near = part[1, h, 0:1], part[1, h, 1:2]
        peak = jnp.maximum(level, level_near)
        whole = peak + jnp.log2(jnp.exp2(level - peak) + jnp.exp2(level_near - peak))
        mixed = jnp.exp2(level - whole) * dot + jnp.exp2(level_near - whole) * dot_near
        stats[h, beyond, 1, 0:1] = whole
        stats[h, beyond, 1, 1:2] = mixed
        return carry

    def key_step(i, carry):
        h, f = i % groups, (i // groups) ^ flip
        k = wide[KEY, h, f + 1, 1]
        v = wide[VAL, h, f + 1, 1]
        q_band = wide[QRY, h, pl.ds(f, 3)].reshape(wide_rows, 128)
        g_band = wide[GRD, h, pl.ds(f, 3)].reshape(wide_rows, 128)
        tiles = [stats[h, f + a, b] for a in range(3) for b in range(3)]
        level = jnp.concatenate([t[0:1] for t in tiles], axis=1)
        dot = jnp.concatenate([t[1:2] for t in tiles], axis=1)
        s = (nt(k, q_band) * power).reshape(2, 64, wide_rows) + (behind[f] - level)
        p = jnp.exp2(s.reshape(128, wide_rows))
        own[3, h, f] = nn(p.astype(jnp.bfloat16), g_band).astype(jnp.bfloat16)
        ds = (p * (nt(v, g_band) - dot)).astype(jnp.bfloat16)
        own[2, h, f] = (nn(ds, q_band) * scaling).astype(jnp.bfloat16)
        return carry

    def giving(o, half_at, k):
        f = half_at ^ flip
        spot = pl.ds(pl.multiple_of(peers[k] * 32, 32), 32)
        return pltpu.make_async_remote_copy(
            src_ref=own.at[o, :, f, spot],
            dst_ref=back.at[o, pl.ds(x_at * groups, groups), f],
            send_sem=o_send.at[o, half_at, k - 1],
            recv_sem=o_recv.at[o, half_at, k - 1],
            device_id=(f_at, r_at, peers[k]),
            device_id_type=MESH,
        )

    def taking(o, half_at, k):
        f = half_at ^ flip
        return pltpu.make_async_remote_copy(
            src_ref=own.at[o, :, f, pl.ds(0, 32)],
            dst_ref=back.at[o, pl.ds(froms[k] * groups, groups), f],
            send_sem=o_send.at[o, half_at, k - 1],
            recv_sem=o_recv.at[o, half_at, k - 1],
            device_id=(f_at, r_at, froms[k]),
            device_id_type=MESH,
        )

    def give(half_at, *kinds):
        f = half_at ^ flip
        for o in kinds:
            for k in range(1, heads):
                giving(o, half_at, k).start()
        for o in kinds:
            spot = pl.ds(pl.multiple_of(x_at * 32, 32), 32)
            back[o, pl.ds(x_at * groups, groups), f] = own[o, :, f, spot]

    def storing(o, half_at):
        f = half_at ^ flip
        span = pl.ds(pl.multiple_of(f * 2 * tall, 2 * tall), 2 * tall)
        return pltpu.make_async_copy(land.at[o, span], outs[o].at[span], out_sem.at[o, half_at])

    def finish(half_at, *kinds):
        f = half_at ^ flip
        for o in kinds:
            for k in range(1, heads):
                taking(o, half_at, k).wait_recv()
            for g in range(2):
                piece = back[o, :, f, pl.ds(16 * g, 16)].reshape(tall, 128)
                span = pl.ds(pl.multiple_of((f * 2 + g) * tall, tall), tall)
                land[o, span] = nn(to_rows, piece).astype(jnp.bfloat16)
            storing(o, half_at).start()

    early_halo(KEY, VAL)
    lax.fori_loop(0, groups, query_step, 0)
    give(0, 0, 1)

    @pl.when(far)
    def _():
        lax.fori_loop(0, groups, near_step, 0)
        summary(0).start()

    for t in range(4):
        far_halo(t)

    @pl.when(far)
    def _():
        summary(0).wait_recv()
        lax.fori_loop(0, groups, across_step, 0)

    far_halo(4)
    late_halo(KEY, VAL)
    lax.fori_loop(groups, groups * 2, query_step, 0)
    first_halo(4)
    give(1, 0, 1)
    finish(0, 0, 1)
    second_halo(4)
    early_halo(QRY, GRD, 4)
    lax.fori_loop(0, groups, key_step, 0)
    give(0, 2, 3)
    finish(1, 0, 1)
    late_halo(QRY, GRD, 4)
    lax.fori_loop(groups, groups * 2, key_step, 0)
    give(1, 2, 3)
    finish(0, 2, 3)
    finish(1, 2, 3)

    for t in range(4):
        for k in range(1, heads):
            exchange(t, k).wait_send()
            giving(t, 0, k).wait_send()
            giving(t, 1, k).wait_send()
    for t in range(5):
        halo_sent(t)
    pl.when(far)(lambda: summary(0).wait_send())
    for o in range(4):
        storing(o, 0).wait()
        storing(o, 1).wait()


def on_device(sizes, queries, keys, values, out_grad, active):
    frames, rows, heads, groups, scaling = sizes
    frames_here, rows_here, cols_here, heads_all, head_dim = queries.shape
    table = jnp.transpose(active, (1, 3, 2, 0))
    tall = frames_here * rows_here * cols_here * heads_all

    def flat(tensor):
        return jnp.transpose(tensor, (0, 1, 3, 2, 4)).reshape(tall, head_dim)

    def unflat(tensor):
        shaped = tensor.reshape(frames_here, rows_here, heads_all, cols_here, head_dim)
        return jnp.transpose(shaped, (0, 1, 3, 2, 4))

    dma = pltpu.SemaphoreType.DMA
    block = (128, head_dim)
    kinds = heads - 1
    anywhere = pl.BlockSpec(memory_space=pl.ANY)
    results = pl.pallas_call(
        functools.partial(tile_kernel, sizes),
        out_shape=[jax.ShapeDtypeStruct((tall, head_dim), jnp.bfloat16)] * 4,
        in_specs=[anywhere] * 5,
        out_specs=[anywhere] * 4,
        scratch_shapes=[
            pltpu.VMEM((4, tall, head_dim), jnp.bfloat16),
            pltpu.VMEM((4, heads_all, 2, 32, head_dim), jnp.bfloat16),
            pltpu.VMEM((4, groups, 4, 3) + block, jnp.bfloat16),
            pltpu.VMEM((groups, 4, 3, 8, 128), jnp.float32),
            pltpu.VMEM((4, groups, 2) + block, jnp.bfloat16),
            pltpu.VMEM((4, heads_all, 2, 32, head_dim), jnp.bfloat16),
            pltpu.VMEM((2, groups, 8, 128), jnp.float32),
            pltpu.VMEM((2, 2, 1, 9 * 128), jnp.float32),
            pltpu.VMEM((2, 2, 1, 9 * 128), jnp.float32),
            pltpu.VMEM((6, 1, 128), jnp.float32),
            pltpu.SMEM((3,) + table.shape[1:], jnp.int32),
            dma((4,)),
            dma((4, kinds)),
            dma((4, kinds)),
            dma((5, 2)),
            dma((5, 2)),
            dma((5, 2)),
            dma((5, 2)),
            dma((5, 4)),
            dma((5, 4)),
            dma((4, 2, kinds)),
            dma((4, 2, kinds)),
            dma((4, 2)),
            dma((2,)),
            dma((3,)),
            pltpu.SemaphoreType.REGULAR,
        ],
        compiler_params=pltpu.CompilerParams(
            collective_id=0, has_side_effects=True, vmem_limit_bytes=48 << 20
        ),
    )(table, flat(keys), flat(values), flat(queries), flat(out_grad))
    return tuple(unflat(r) for r in results)


def solution(mesh):
    frames, rows, heads = (mesh.shape[a] for a in ("frame", "row", "head"))
    sizes = (frames, rows, heads, 12 // heads, 128**-0.5)
    spec = P("frame", "row", "head", None, None)
    return jax.shard_map(
        functools.partial(on_device, sizes),
        mesh=mesh,
        in_specs=(spec,) * 4 + (P(),),
        out_specs=(spec,) * 4,
        check_vma=False,
    )
```

```python
import functools
import math

import jax
import jax.numpy as jnp
from jax import lax
from jax.experimental import pallas as pl
from jax.experimental.pallas import tpu as pltpu
from jax.sharding import PartitionSpec as P

MESH = pl.DeviceIdType.MESH
NEG = -1e30
KEY, VAL, QRY, GRD = 0, 1, 2, 3
VMEM = 63 << 20


def nt(left, right):
    return lax.dot_general(
        left, right, (((1,), (1,)), ((), ())), preferred_element_type=jnp.float32
    )


def nn(left, right):
    return jnp.dot(left, right, preferred_element_type=jnp.float32)


def tile_kernel(sizes, act_in, k_in, v_in, q_in, g_in, *refs):
    frames, rows, heads, groups, scaling = sizes
    outs, refs = refs[:4], refs[4:]
    land, pack, wide, stats, own, back, part, front, behind, across, relay, act = refs[:12]
    in_sem, a_send, a_recv, z_send, z_recv, c_send, c_recv, d_send, d_recv = refs[12:21]
    o_send, o_recv, out_sem, part_sem, act_sem, leg_send, leg_recv, ready = refs[21:29]
    ins = (k_in, v_in, q_in, g_in)
    heads_all = groups * heads
    tall = heads_all * 16

    f_at = lax.axis_index("frame")
    r_at = lax.axis_index("row")
    x_at = lax.axis_index("head")
    up, down = f_at < frames - 1, f_at > 0
    right, left = r_at < rows - 1, r_at > 0
    far_up, far_down = f_at == frames // 2 - 1, f_at == frames // 2
    both = jnp.logical_and
    near_up = both(up, jnp.logical_not(far_up))
    near_down = both(down, jnp.logical_not(far_down))
    far = jnp.logical_or(far_up, far_down)

    half, turn = frames // 2, 2 * rows
    upper, place = f_at // half, f_at % half
    core, column = f_at % 2, place // 2
    z_at = upper * rows + r_at
    first_relay = core + upper == 1
    shifted = lax.rem(z_at + rows * (1 - core), turn)
    odd = lax.rem(shifted, 2)
    began = jnp.where(odd == 1, shifted - (rows - 1), lax.rem(shifted + turn - rows - 1, turn))
    second_relay = both(began >= 0, began < rows) & (lax.rem(began + turn, 2) == 1 - odd)
    near = jnp.logical_not(far)

    def relays_of(z, member):
        spot = lax.rem(z + rows - 1 + 2 * lax.rem(r_at, 2), turn)
        return (spot // rows) * half + member, lax.rem(spot, rows)

    def start_relay(t):
        return upper * half + 2 * t + core, r_at

    def proxy_of(side, row):
        return half - 4 + 7 * side, row

    proxy = f_at == proxy_of(upper, r_at)[0]
    next_relay = relays_of(z_at, place)
    last_to = (half - 1 + core, began)
    edge = far_up.astype(jnp.int32)
    beyond = 3 * edge
    flip = far_down.astype(jnp.int32)

    peers = [lax.rem(x_at + k, heads) for k in range(heads)]
    froms = [lax.rem(x_at + heads - k, heads) for k in range(heads)]

    def loading(t):
        return pltpu.make_async_copy(ins[t], land.at[t], in_sem.at[t])

    def loading_act(j):
        row = jnp.clip(r_at - 1 + j, 0, rows - 1)
        return pltpu.make_async_copy(act_in.at[row], act.at[j], act_sem.at[j])

    for t in range(4):
        loading(t).start()
    for j in range(3):
        loading_act(j).start()

    barrier = pltpu.get_barrier_semaphore()

    def greet(frame, row, head):
        pl.semaphore_signal(barrier, inc=1, device_id=(frame, row, head), device_id_type=MESH)

    for k in range(1, heads):
        greet(f_at, r_at, peers[k])
    pl.when(right)(lambda: greet(f_at, r_at + 1, x_at))
    pl.when(left)(lambda: greet(f_at, r_at - 1, x_at))
    pl.when(near_up)(lambda: greet(f_at + 1, r_at, x_at))
    pl.when(near_down)(lambda: greet(f_at - 1, r_at, x_at))

    @pl.when(far)
    def _():
        greet(*proxy_of(1 - upper, r_at), x_at)
        for t in range(4):
            greet(*relays_of(z_at + rows, 2 * t + 1 - core), x_at)

    pl.when(both(first_relay, near))(lambda: greet(half - 1 + upper, r_at, x_at))
    pl.when(first_relay)(lambda: greet(*proxy_of(upper, r_at), x_at))
    pl.when(second_relay)(lambda: greet(*proxy_of(1 - core, began), x_at))

    @pl.when(jnp.logical_not(left))
    def _():
        wide[:, :, :, 0] = jnp.zeros_like(wide[:, :, :, 0])
        stats[:, :, 0] = jnp.zeros_like(stats[:, :, 0])

    @pl.when(jnp.logical_not(right))
    def _():
        wide[:, :, :, 2] = jnp.zeros_like(wide[:, :, :, 2])
        stats[:, :, 2] = jnp.zeros_like(stats[:, :, 2])

    @pl.when(jnp.logical_not(down))
    def _():
        wide[:, :, 0] = jnp.zeros_like(wide[:, :, 0])
        stats[:, 0] = jnp.zeros_like(stats[:, 0])

    @pl.when(jnp.logical_not(up))
    def _():
        wide[:, :, 3] = jnp.zeros_like(wide[:, :, 3])
        stats[:, 3] = jnp.zeros_like(stats[:, 3])

    out_row = lax.broadcasted_iota(jnp.int32, (tall, tall), 0)
    in_row = lax.broadcasted_iota(jnp.int32, (tall, tall), 1)

    def swapped(row):
        return ((row % 16) // 4) * (4 * heads_all) + (row // 16) * 4 + row % 4

    to_heads = (swapped(out_row) == in_row).astype(jnp.bfloat16)
    to_rows = (swapped(in_row) == out_row).astype(jnp.bfloat16)

    def exchange(t, k):
        there = peers[k]
        return pltpu.make_async_remote_copy(
            src_ref=pack.at[t, pl.ds(there * groups, groups)],
            dst_ref=wide.at[t, :, pl.ds(1, 2), 1, pl.ds(pl.multiple_of(x_at * 32, 32), 32)],
            send_sem=a_send.at[t, k - 1],
            recv_sem=a_recv.at[t, k - 1],
            device_id=(f_at, r_at, there),
            device_id_type=MESH,
        )

    def arriving(t, k):
        spot = pl.ds(pl.multiple_of(froms[k] * 32, 32), 32)
        return pltpu.make_async_remote_copy(
            src_ref=pack.at[t, pl.ds(0, groups)],
            dst_ref=wide.at[t, :, pl.ds(1, 2), 1, spot],
            send_sem=a_send.at[t, k - 1],
            recv_sem=a_recv.at[t, k - 1],
            device_id=(f_at, r_at, froms[k]),
            device_id_type=MESH,
        )

    def block(t, frame, row):
        ref = stats if t == 4 else wide.at[t]
        return ref.at[:, frame, row]

    def pair(t, row):
        ref = stats if t == 4 else wide.at[t]
        return ref.at[:, pl.ds(1, 2), row]

    def hop(src, dst, ss, rs, frame, row):
        return pltpu.make_async_remote_copy(
            src_ref=src,
            dst_ref=dst,
            send_sem=ss,
            recv_sem=rs,
            device_id=(frame, row, x_at),
            device_id_type=MESH,
        )

    def to_right(t):
        return hop(pair(t, 1), pair(t, 0), z_send.at[t, 0], z_recv.at[t, 0], f_at, r_at + 1)

    def to_left(t):
        return hop(pair(t, 1), pair(t, 2), z_send.at[t, 1], z_recv.at[t, 1], f_at, r_at - 1)

    def to_up(t):
        return hop(block(t, 2, 1), block(t, 0, 1), c_send.at[t, 0], c_recv.at[t, 0], f_at + 1, r_at)

    def to_down(t):
        return hop(block(t, 1, 1), block(t, 3, 1), c_send.at[t, 1], c_recv.at[t, 1], f_at - 1, r_at)

    def side_up(t, row):
        sem = 0 if row == 0 else 1
        return hop(
            block(t, 2, row), block(t, 0, row), d_send.at[t, sem], d_recv.at[t, sem], f_at + 1, r_at
        )

    def side_down(t, row):
        sem = 2 if row == 0 else 3
        return hop(
            block(t, 1, row), block(t, 3, row), d_send.at[t, sem], d_recv.at[t, sem], f_at - 1, r_at
        )

    def along_right(t, frame):
        sem = 0 if frame == 0 else 2
        return hop(
            block(t, frame, 1), block(t, frame, 0), d_send.at[t, sem], d_recv.at[t, sem], f_at, r_at + 1
        )

    def along_left(t, frame):
        sem = 1 if frame == 0 else 3
        return hop(
            block(t, frame, 1), block(t, frame, 2), d_send.at[t, sem], d_recv.at[t, sem], f_at, r_at - 1
        )

    def tell():
        for t in range(4):
            there = (upper * half + 2 * t + 1 - core, r_at, x_at)
            pl.semaphore_signal(ready, inc=1, device_id=there, device_id_type=MESH)

    def leg_one(t):
        return hop(
            block(t, edge + 1, 1), relay.at[0], leg_send.at[t], leg_recv.at[0], *start_relay(t)
        )

    def leg_two(src):
        return hop(src, relay.at[1], leg_send.at[4], leg_recv.at[1], *next_relay)

    def leg_three(t):
        side = 1 - core
        return hop(
            relay.at[1], block(t, 3 * side, 1), leg_send.at[5], c_recv.at[t, side], *last_to
        )

    def first_halo(t):
        if t < 4:
            pl.when(both(far, column != t))(lambda: leg_one(t).start())
        pl.when(right)(lambda: to_right(t).start())
        pl.when(left)(lambda: to_left(t).start())
        pl.when(near_up)(lambda: to_up(t).start())
        pl.when(near_down)(lambda: to_down(t).start())

    def relay_one():
        for t in range(4):
            here = both(first_relay, column == t)

            @pl.when(both(here, near))
            def _():
                leg_one(t).wait_recv()
                pl.semaphore_wait(ready, 1)
                leg_two(relay.at[0]).start()

            @pl.when(both(here, far))
            def _():
                pl.semaphore_wait(ready, 1)
                leg_two(block(t, edge + 1, 1)).start()

    def relay_two(group):
        for t in range(4):

            @pl.when(both(group, both(second_relay, column == t)))
            def _():
                leg_two(relay.at[0]).wait_recv()
                leg_three(t).start()

    def summary(side):
        there = jnp.where(far_up, half, half - 1)
        return hop(part.at[0], part.at[1], part_sem.at[0], part_sem.at[1], there, r_at)

    def second_halo(t):
        pl.when(left)(lambda: to_right(t).wait_recv())
        pl.when(right)(lambda: to_left(t).wait_recv())
        pl.when(both(near_up, left))(lambda: side_up(t, 0).start())
        pl.when(both(near_up, right))(lambda: side_up(t, 2).start())
        pl.when(both(near_down, left))(lambda: side_down(t, 0).start())
        pl.when(both(near_down, right))(lambda: side_down(t, 2).start())

    def far_halo(t):
        if t < 4:
            pl.when(far_down)(lambda: to_up(t).wait_recv())
            pl.when(far_up)(lambda: to_down(t).wait_recv())
        pl.when(both(far_down, right))(lambda: along_right(t, 0).start())
        pl.when(both(far_down, left))(lambda: along_left(t, 0).start())
        pl.when(both(far_up, right))(lambda: along_right(t, 3).start())
        pl.when(both(far_up, left))(lambda: along_left(t, 3).start())

    def low_halo(t):
        pl.when(near_down)(lambda: to_up(t).wait_recv())
        pl.when(both(down, left))(lambda: side_up(t, 0).wait_recv())
        pl.when(both(down, right))(lambda: side_up(t, 2).wait_recv())

    def high_halo(t):
        pl.when(near_up)(lambda: to_down(t).wait_recv())
        pl.when(both(up, left))(lambda: side_down(t, 0).wait_recv())
        pl.when(both(up, right))(lambda: side_down(t, 2).wait_recv())

    def early_halo(*kinds):
        @pl.when(jnp.logical_not(far_down))
        def _():
            for t in kinds:
                low_halo(t)

        @pl.when(far_down)
        def _():
            for t in kinds:
                high_halo(t)

    def late_halo(*kinds):
        @pl.when(far_down)
        def _():
            for t in kinds:
                low_halo(t)

        @pl.when(jnp.logical_not(far_down))
        def _():
            for t in kinds:
                high_halo(t)

    def halo_sent(t):
        if t < 4:
            pl.when(both(far, column != t))(lambda: leg_one(t).wait_send())
        pl.when(near_up)(lambda: to_up(t).wait_send())
        pl.when(near_down)(lambda: to_down(t).wait_send())
        pl.when(right)(lambda: to_right(t).wait_send())
        pl.when(left)(lambda: to_left(t).wait_send())
        pl.when(both(near_up, left))(lambda: side_up(t, 0).wait_send())
        pl.when(both(near_up, right))(lambda: side_up(t, 2).wait_send())
        pl.when(both(near_down, left))(lambda: side_down(t, 0).wait_send())
        pl.when(both(near_down, right))(lambda: side_down(t, 2).wait_send())
        pl.when(both(far_down, right))(lambda: along_right(t, 0).wait_send())
        pl.when(both(far_down, left))(lambda: along_left(t, 0).wait_send())
        pl.when(both(far_up, right))(lambda: along_right(t, 3).wait_send())
        pl.when(both(far_up, left))(lambda: along_left(t, 3).wait_send())

    for j in range(3):
        loading_act(j).wait()

    lanes = lax.broadcasted_iota(jnp.int32, (1, 128), 1)

    def placed(i, j):
        frame, row = 2 * f_at - 1 + i, r_at - 1 + j
        return (frame >= 0) & (frame < 2 * frames) & (row >= 0) & (row < rows)

    def entry(i, j, l, slot, inside):
        frame = jnp.clip(2 * f_at - 1 + i, 0, 2 * frames - 1)
        return jnp.where(inside & (act[j, slot, l, frame] == 1), 0.0, NEG)

    def halves(pair_of):
        return jnp.where(lanes < 64, pair_of[0], pair_of[1])

    def mask_step(i, carry):
        f, a = i // 3, i % 3
        for b in range(3):
            span = pl.ds(pl.multiple_of(a * 384 + b * 128, 128), 128)
            inside = placed(f + a, b)
            for l in range(2):
                slots = [9 * a + 3 * b + m - l + 1 for m in range(2)]
                front[f, l, :, span] = halves([entry(f + 1, 1, l, n, inside) for n in slots])
                slots = [9 * (2 - a) + 3 * (2 - b) + l - m + 1 for m in range(2)]
                behind[f, l, :, span] = halves([entry(f + a, b, l, n, inside) for n in slots])
        return carry

    lax.fori_loop(0, 6, mask_step, 0)

    @pl.when(far)
    def _():
        for b in range(3):
            inside = placed(edge + 1, b)
            for l in range(2):
                slots = [18 * (1 - edge) + 3 * b + l - m + 1 for m in range(2)]
                pieces = [entry(beyond, 1, m, n, inside) for m, n in enumerate(slots)]
                across[2 * b + l] = halves(pieces)

    for t in range(4):
        loading(t).wait()
        for g in range(4):
            moved = nn(to_heads, land[t, pl.ds(g * tall, tall)]).astype(jnp.bfloat16)
            pack[t, :, g // 2, pl.ds(16 * (g % 2), 16)] = moved.reshape(heads_all, 16, 128)
        if t == 0:
            known = [right, left, near_up, near_down, second_relay]
            count = heads - 1 + sum(c.astype(jnp.int32) for c in known)
            count += 3 * far.astype(jnp.int32) + 9 * proxy.astype(jnp.int32)
            pl.semaphore_wait(barrier, count)
            pl.when(proxy)(tell)
        for k in range(1, heads):
            exchange(t, k).start()
        wide[t, :, pl.ds(1, 2), 1, pl.ds(pl.multiple_of(x_at * 32, 32), 32)] = pack[
            t, pl.ds(x_at * groups, groups)
        ]

    def gathered(t):
        for k in range(1, heads):
            arriving(t, k).wait_recv()

    gathered(KEY)
    first_halo(KEY)
    gathered(VAL)
    first_halo(VAL)
    second_halo(KEY)
    gathered(QRY)
    first_halo(QRY)
    second_halo(VAL)
    gathered(GRD)
    first_halo(GRD)

    lane_grid = lax.broadcasted_iota(jnp.int32, (128, 128), 1)
    power = scaling * math.log2(math.e)
    wide_rows = 9 * 128

    def as_rows(level, dot):
        return jnp.where(lane_grid == 0, level, dot).T[0:8]

    def query_step(i, carry):
        h, f = i % groups, (i // groups) ^ flip
        q = wide[QRY, h, f + 1, 1]
        g = wide[GRD, h, f + 1, 1]
        k_band = wide[KEY, h, pl.ds(f, 3)].reshape(wide_rows, 128)
        v_band = wide[VAL, h, pl.ds(f, 3)].reshape(wide_rows, 128)
        s = (nt(q, k_band).reshape(2, 64, wide_rows) + front[f]).reshape(128, wide_rows)
        top = jnp.max(s, axis=1, keepdims=True)
        p = jnp.exp2((s - top) * power)
        total = jnp.sum(p, axis=1, keepdims=True)
        inverse = 1.0 / total
        out = (nn(p.astype(jnp.bfloat16), v_band) * inverse).astype(jnp.bfloat16)
        own[0, h, f] = out
        dot = jnp.sum(g.astype(jnp.float32) * out.astype(jnp.float32), axis=1, keepdims=True)
        ds = (p * (nt(g, v_band) - dot)).astype(jnp.bfloat16)
        own[1, h, f] = (nn(ds, k_band) * (inverse * scaling)).astype(jnp.bfloat16)
        stats[h, f + 1, 1] = as_rows(top * power + jnp.log2(total), dot)
        return carry

    def near_step(h, carry):
        q = wide[QRY, h, edge + 1, 1]
        g = wide[GRD, h, edge + 1, 1]
        k_band = wide[KEY, h, pl.ds(1, 2)].reshape(6 * 128, 128)
        v_band = wide[VAL, h, pl.ds(1, 2)].reshape(6 * 128, 128)
        offset = pl.multiple_of((1 - edge) * 384, 128)
        mask = front[edge, :, :, pl.ds(offset, 768)]
        s = (nt(q, k_band).reshape(2, 64, 768) + mask).reshape(128, 768)
        top = jnp.max(s, axis=1, keepdims=True)
        p = jnp.exp2((s - top) * power)
        total = jnp.sum(p, axis=1, keepdims=True)
        dot = jnp.sum(p * nt(g, v_band), axis=1, keepdims=True) / total
        part[0, h] = as_rows(top * power + jnp.log2(total), dot)
        return carry

    def across_step(h, carry):
        q = wide[QRY, h, beyond, 1]
        g = wide[GRD, h, beyond, 1]
        k_band = wide[KEY, h, edge + 1].reshape(384, 128)
        v_band = wide[VAL, h, edge + 1].reshape(384, 128)
        s = ((nt(k_band, q) * power).reshape(6, 64, 128) + across[...]).reshape(384, 128)
        top = jnp.max(s, axis=0, keepdims=True)
        p = jnp.exp2(s - top)
        total = jnp.sum(p, axis=0, keepdims=True)
        dot = jnp.sum(p * nt(v_band, g), axis=0, keepdims=True) / total
        level = top + jnp.log2(total)
        level_near, dot_near = part[1, h, 0:1], part[1, h, 1:2]
        peak = jnp.maximum(level, level_near)
        whole = peak + jnp.log2(jnp.exp2(level - peak) + jnp.exp2(level_near - peak))
        mixed = jnp.exp2(level - whole) * dot + jnp.exp2(level_near - whole) * dot_near
        stats[h, beyond, 1, 0:1] = whole
        stats[h, beyond, 1, 1:2] = mixed
        return carry

    def key_step(i, carry):
        h, f = i % groups, (i // groups) ^ flip
        k = wide[KEY, h, f + 1, 1]
        v = wide[VAL, h, f + 1, 1]
        q_band = wide[QRY, h, pl.ds(f, 3)].reshape(wide_rows, 128)
        g_band = wide[GRD, h, pl.ds(f, 3)].reshape(wide_rows, 128)
        tiles = [stats[h, f + a, b] for a in range(3) for b in range(3)]
        level = jnp.concatenate([t[0:1] for t in tiles], axis=1)
        dot = jnp.concatenate([t[1:2] for t in tiles], axis=1)
        s = (nt(k, q_band) * power).reshape(2, 64, wide_rows) + (behind[f] - level)
        p = jnp.exp2(s.reshape(128, wide_rows))
        own[3, h, f] = nn(p.astype(jnp.bfloat16), g_band).astype(jnp.bfloat16)
        ds = (p * (nt(v, g_band) - dot)).astype(jnp.bfloat16)
        own[2, h, f] = (nn(ds, q_band) * scaling).astype(jnp.bfloat16)
        return carry

    def giving(o, half_at, k):
        f = half_at ^ flip
        spot = pl.ds(pl.multiple_of(peers[k] * 32, 32), 32)
        return pltpu.make_async_remote_copy(
            src_ref=own.at[o, :, f, spot],
            dst_ref=back.at[o, pl.ds(x_at * groups, groups), f],
            send_sem=o_send.at[o, half_at, k - 1],
            recv_sem=o_recv.at[o, half_at, k - 1],
            device_id=(f_at, r_at, peers[k]),
            device_id_type=MESH,
        )

    def taking(o, half_at, k):
        f = half_at ^ flip
        return pltpu.make_async_remote_copy(
            src_ref=own.at[o, :, f, pl.ds(0, 32)],
            dst_ref=back.at[o, pl.ds(froms[k] * groups, groups), f],
            send_sem=o_send.at[o, half_at, k - 1],
            recv_sem=o_recv.at[o, half_at, k - 1],
            device_id=(f_at, r_at, froms[k]),
            device_id_type=MESH,
        )

    def give(half_at, *kinds):
        f = half_at ^ flip
        for o in kinds:
            for k in range(1, heads):
                giving(o, half_at, k).start()
        for o in kinds:
            spot = pl.ds(pl.multiple_of(x_at * 32, 32), 32)
            back[o, pl.ds(x_at * groups, groups), f] = own[o, :, f, spot]

    def storing(o, half_at):
        f = half_at ^ flip
        span = pl.ds(pl.multiple_of(f * 2 * tall, 2 * tall), 2 * tall)
        return pltpu.make_async_copy(land.at[o, span], outs[o].at[span], out_sem.at[o, half_at])

    def finish(half_at, *kinds):
        f = half_at ^ flip
        for o in kinds:
            for k in range(1, heads):
                taking(o, half_at, k).wait_recv()
            for g in range(2):
                piece = back[o, :, f, pl.ds(16 * g, 16)].reshape(tall, 128)
                span = pl.ds(pl.multiple_of((f * 2 + g) * tall, tall), tall)
                land[o, span] = nn(to_rows, piece).astype(jnp.bfloat16)
            storing(o, half_at).start()

    @pl.when(far)
    def _():
        lax.fori_loop(0, groups, near_step, 0)

    second_halo(QRY)
    relay_one()
    pl.when(far)(lambda: summary(0).start())
    second_halo(GRD)
    early_halo(KEY, VAL)
    lax.fori_loop(0, groups, query_step, 0)
    give(0, 0, 1)
    relay_two(far)

    for t in range(4):
        far_halo(t)

    @pl.when(far)
    def _():
        summary(0).wait_recv()
        lax.fori_loop(0, groups, across_step, 0)

    far_halo(4)
    late_halo(KEY, VAL)
    lax.fori_loop(groups, groups * 2, query_step, 0)
    first_halo(4)
    give(1, 0, 1)
    relay_two(near)
    finish(0, 0, 1)
    second_halo(4)
    early_halo(QRY, GRD, 4)
    lax.fori_loop(0, groups, key_step, 0)
    give(0, 2, 3)
    finish(1, 0, 1)
    late_halo(QRY, GRD, 4)
    lax.fori_loop(groups, groups * 2, key_step, 0)
    give(1, 2, 3)
    finish(0, 2, 3)
    finish(1, 2, 3)

    for t in range(4):
        for k in range(1, heads):
            exchange(t, k).wait_send()
            giving(t, 0, k).wait_send()
            giving(t, 1, k).wait_send()
    for t in range(5):
        halo_sent(t)
    pl.when(far)(lambda: summary(0).wait_send())
    pl.when(first_relay)(lambda: leg_two(relay.at[0]).wait_send())
    pl.when(second_relay)(lambda: leg_three(0).wait_send())
    for o in range(4):
        storing(o, 0).wait()
        storing(o, 1).wait()


def on_device(sizes, queries, keys, values, out_grad, active):
    frames, rows, heads, groups, scaling = sizes
    frames_here, rows_here, cols_here, heads_all, head_dim = queries.shape
    table = jnp.transpose(active, (1, 3, 2, 0))
    tall = frames_here * rows_here * cols_here * heads_all

    def flat(tensor):
        return jnp.transpose(tensor, (0, 1, 3, 2, 4)).reshape(tall, head_dim)

    def unflat(tensor):
        shaped = tensor.reshape(frames_here, rows_here, heads_all, cols_here, head_dim)
        return jnp.transpose(shaped, (0, 1, 3, 2, 4))

    dma = pltpu.SemaphoreType.DMA
    block = (128, head_dim)
    kinds = heads - 1
    anywhere = pl.BlockSpec(memory_space=pl.ANY)
    results = pl.pallas_call(
        functools.partial(tile_kernel, sizes),
        out_shape=[jax.ShapeDtypeStruct((tall, head_dim), jnp.bfloat16)] * 4,
        in_specs=[anywhere] * 5,
        out_specs=[anywhere] * 4,
        scratch_shapes=[
            pltpu.VMEM((4, tall, head_dim), jnp.bfloat16),
            pltpu.VMEM((4, heads_all, 2, 32, head_dim), jnp.bfloat16),
            pltpu.VMEM((4, groups, 4, 3) + block, jnp.bfloat16),
            pltpu.VMEM((groups, 4, 3, 8, 128), jnp.float32),
            pltpu.VMEM((4, groups, 2) + block, jnp.bfloat16),
            pltpu.VMEM((4, heads_all, 2, 32, head_dim), jnp.bfloat16),
            pltpu.VMEM((2, groups, 8, 128), jnp.float32),
            pltpu.VMEM((2, 2, 1, 9 * 128), jnp.float32),
            pltpu.VMEM((2, 2, 1, 9 * 128), jnp.float32),
            pltpu.VMEM((6, 1, 128), jnp.float32),
            pltpu.VMEM((2, groups) + block, jnp.bfloat16),
            pltpu.SMEM((3,) + table.shape[1:], jnp.int32),
            dma((4,)),
            dma((4, kinds)),
            dma((4, kinds)),
            dma((5, 2)),
            dma((5, 2)),
            dma((5, 2)),
            dma((5, 2)),
            dma((5, 4)),
            dma((5, 4)),
            dma((4, 2, kinds)),
            dma((4, 2, kinds)),
            dma((4, 2)),
            dma((2,)),
            dma((3,)),
            dma((6,)),
            dma((2,)),
            pltpu.SemaphoreType.REGULAR,
        ],
        compiler_params=pltpu.CompilerParams(
            collective_id=0, has_side_effects=True, vmem_limit_bytes=VMEM
        ),
    )(table, flat(keys), flat(values), flat(queries), flat(out_grad))
    return tuple(unflat(r) for r in results)


def solution(mesh):
    frames, rows, heads = (mesh.shape[a] for a in ("frame", "row", "head"))
    sizes = (frames, rows, heads, 12 // heads, 128**-0.5)
    spec = P("frame", "row", "head", None, None)
    return jax.shard_map(
        functools.partial(on_device, sizes),
        mesh=mesh,
        in_specs=(spec,) * 4 + (P(),),
        out_specs=(spec,) * 4,
        check_vma=False,
    )
```

```python
import functools
import math

import jax
import jax.numpy as jnp
from jax import lax
from jax.experimental import pallas as pl
from jax.experimental.pallas import tpu as pltpu
from jax.sharding import PartitionSpec as P

MESH = pl.DeviceIdType.MESH
NEG = -1e30
KEY, VAL, QRY, GRD = 0, 1, 2, 3
VMEM = 63 << 20


def nt(left, right):
    return lax.dot_general(
        left, right, (((1,), (1,)), ((), ())), preferred_element_type=jnp.float32
    )


def nn(left, right):
    return jnp.dot(left, right, preferred_element_type=jnp.float32)


def tile_kernel(sizes, act_in, k_in, v_in, q_in, g_in, *refs):
    frames, rows, heads, groups, scaling = sizes
    outs, refs = refs[:4], refs[4:]
    land, pack, wide, stats, own, part, front, behind, across, relay, act = refs[:11]
    in_sem, a_send, a_recv, z_send, z_recv, c_send, c_recv, d_send, d_recv = refs[11:20]
    o_send, o_recv, out_sem, part_sem, act_sem, leg_send, leg_recv, ready = refs[20:28]
    ins = (k_in, v_in, q_in, g_in)
    heads_all = groups * heads
    tall = heads_all * 16

    f_at = lax.axis_index("frame")
    r_at = lax.axis_index("row")
    x_at = lax.axis_index("head")
    up, down = f_at < frames - 1, f_at > 0
    right, left = r_at < rows - 1, r_at > 0
    far_up, far_down = f_at == frames // 2 - 1, f_at == frames // 2
    both = jnp.logical_and
    near_up = both(up, jnp.logical_not(far_up))
    near_down = both(down, jnp.logical_not(far_down))
    far = jnp.logical_or(far_up, far_down)

    half, turn = frames // 2, 2 * rows
    upper, place = f_at // half, f_at % half
    core, column = f_at % 2, place // 2
    z_at = upper * rows + r_at
    first_relay = core + upper == 1
    shifted = lax.rem(z_at + rows * (1 - core), turn)
    odd = lax.rem(shifted, 2)
    began = jnp.where(odd == 1, shifted - (rows - 1), lax.rem(shifted + turn - rows - 1, turn))
    second_relay = both(began >= 0, began < rows) & (lax.rem(began + turn, 2) == 1 - odd)
    near = jnp.logical_not(far)

    def relays_of(z, row, member):
        spot = lax.rem(z + rows - 1 + 2 * lax.rem(row, 2), turn)
        return (spot // rows) * half + member, lax.rem(spot, rows)

    def start_relay(t):
        return upper * half + 2 * t + core, r_at

    def proxy_of(side, row):
        return half - 4 + 7 * side, row

    proxy = f_at == proxy_of(upper, r_at)[0]
    next_relay = relays_of(z_at, r_at, place)
    targets = [both(second_relay, both(began + 1 - v >= 0, began + 1 - v < rows)) for v in range(3)]
    edge = far_up.astype(jnp.int32)
    beyond = 3 * edge
    flip = far_down.astype(jnp.int32)

    peers = [lax.rem(x_at + k, heads) for k in range(heads)]
    froms = [lax.rem(x_at + heads - k, heads) for k in range(heads)]

    def loading(t):
        return pltpu.make_async_copy(ins[t], land.at[t], in_sem.at[t])

    def loading_act(j):
        row = jnp.clip(r_at - 1 + j, 0, rows - 1)
        return pltpu.make_async_copy(act_in.at[row], act.at[j], act_sem.at[j])

    for t in range(4):
        loading(t).start()
    for j in range(3):
        loading_act(j).start()

    barrier = pltpu.get_barrier_semaphore()

    def greet(frame, row, head):
        pl.semaphore_signal(barrier, inc=1, device_id=(frame, row, head), device_id_type=MESH)

    for k in range(1, heads):
        greet(f_at, r_at, peers[k])
    pl.when(right)(lambda: greet(f_at, r_at + 1, x_at))
    pl.when(left)(lambda: greet(f_at, r_at - 1, x_at))
    pl.when(near_up)(lambda: greet(f_at + 1, r_at, x_at))
    pl.when(near_down)(lambda: greet(f_at - 1, r_at, x_at))

    @pl.when(far)
    def _():
        greet(*proxy_of(1 - upper, r_at), x_at)
        for v, known in enumerate((left, f_at >= 0, right)):

            @pl.when(known)
            def _():
                for t in range(4):
                    z, row = z_at + rows + v - 1, r_at + v - 1
                    greet(*relays_of(z, row, 2 * t + 1 - core), x_at)

    pl.when(both(first_relay, near))(lambda: greet(half - 1 + upper, r_at, x_at))
    pl.when(first_relay)(lambda: greet(*proxy_of(upper, r_at), x_at))
    pl.when(second_relay)(lambda: greet(*proxy_of(1 - core, began), x_at))

    @pl.when(jnp.logical_not(left))
    def _():
        wide[:, :, :, 0] = jnp.zeros_like(wide[:, :, :, 0])
        stats[:, :, 0] = jnp.zeros_like(stats[:, :, 0])

    @pl.when(jnp.logical_not(right))
    def _():
        wide[:, :, :, 2] = jnp.zeros_like(wide[:, :, :, 2])
        stats[:, :, 2] = jnp.zeros_like(stats[:, :, 2])

    @pl.when(jnp.logical_not(down))
    def _():
        wide[:, :, 0] = jnp.zeros_like(wide[:, :, 0])
        stats[:, 0] = jnp.zeros_like(stats[:, 0])

    @pl.when(jnp.logical_not(up))
    def _():
        wide[:, :, 3] = jnp.zeros_like(wide[:, :, 3])
        stats[:, 3] = jnp.zeros_like(stats[:, 3])

    out_row = lax.broadcasted_iota(jnp.int32, (tall, tall), 0)
    in_row = lax.broadcasted_iota(jnp.int32, (tall, tall), 1)

    def swapped(row):
        return ((row % 16) // 4) * (4 * heads_all) + (row // 16) * 4 + row % 4

    to_heads = (swapped(out_row) == in_row).astype(jnp.bfloat16)

    def exchange(t, k):
        there = peers[k]
        return pltpu.make_async_remote_copy(
            src_ref=pack.at[t, pl.ds(there * groups, groups)],
            dst_ref=wide.at[t, :, pl.ds(1, 2), 1, pl.ds(pl.multiple_of(x_at * 32, 32), 32)],
            send_sem=a_send.at[t, k - 1],
            recv_sem=a_recv.at[t, k - 1],
            device_id=(f_at, r_at, there),
            device_id_type=MESH,
        )

    def arriving(t, k):
        spot = pl.ds(pl.multiple_of(froms[k] * 32, 32), 32)
        return pltpu.make_async_remote_copy(
            src_ref=pack.at[t, pl.ds(0, groups)],
            dst_ref=wide.at[t, :, pl.ds(1, 2), 1, spot],
            send_sem=a_send.at[t, k - 1],
            recv_sem=a_recv.at[t, k - 1],
            device_id=(f_at, r_at, froms[k]),
            device_id_type=MESH,
        )

    def block(t, frame, row):
        ref = stats if t == 4 else wide.at[t]
        return ref.at[:, frame, row]

    def pair(t, row):
        ref = stats if t == 4 else wide.at[t]
        return ref.at[:, pl.ds(1, 2), row]

    def hop(src, dst, ss, rs, frame, row):
        return pltpu.make_async_remote_copy(
            src_ref=src,
            dst_ref=dst,
            send_sem=ss,
            recv_sem=rs,
            device_id=(frame, row, x_at),
            device_id_type=MESH,
        )

    def to_right(t):
        return hop(pair(t, 1), pair(t, 0), z_send.at[t, 0], z_recv.at[t, 0], f_at, r_at + 1)

    def to_left(t):
        return hop(pair(t, 1), pair(t, 2), z_send.at[t, 1], z_recv.at[t, 1], f_at, r_at - 1)

    def to_up(t):
        return hop(block(t, 2, 1), block(t, 0, 1), c_send.at[t, 0], c_recv.at[t, 0], f_at + 1, r_at)

    def to_down(t):
        return hop(block(t, 1, 1), block(t, 3, 1), c_send.at[t, 1], c_recv.at[t, 1], f_at - 1, r_at)

    def side_up(t, row):
        sem = 0 if row == 0 else 1
        return hop(
            block(t, 2, row), block(t, 0, row), d_send.at[t, sem], d_recv.at[t, sem], f_at + 1, r_at
        )

    def side_down(t, row):
        sem = 2 if row == 0 else 3
        return hop(
            block(t, 1, row), block(t, 3, row), d_send.at[t, sem], d_recv.at[t, sem], f_at - 1, r_at
        )

    def along_right(t, frame):
        sem = 0 if frame == 0 else 2
        return hop(
            block(t, frame, 1), block(t, frame, 0), d_send.at[t, sem], d_recv.at[t, sem], f_at, r_at + 1
        )

    def along_left(t, frame):
        sem = 1 if frame == 0 else 3
        return hop(
            block(t, frame, 1), block(t, frame, 2), d_send.at[t, sem], d_recv.at[t, sem], f_at, r_at - 1
        )

    def tell():
        for t in range(4):
            there = (upper * half + 2 * t + 1 - core, r_at, x_at)
            pl.semaphore_signal(ready, inc=1, device_id=there, device_id_type=MESH)

    def leg_one(t, h):
        return hop(
            wide.at[t, h, edge + 1, 1],
            relay.at[0, h],
            leg_send.at[t * groups + h],
            leg_recv.at[0, h],
            *start_relay(t),
        )

    def leg_two(src, h):
        return hop(
            src, relay.at[1, h], leg_send.at[4 * groups + h], leg_recv.at[1, h], *next_relay
        )

    def leg_three(t, h, v):
        side = 1 - core
        sem = c_recv.at[t, side] if v == 1 else d_recv.at[t, 2 * side + v // 2]
        return hop(
            relay.at[1, h],
            wide.at[t, h, 3 * side, v],
            leg_send.at[(5 + v) * groups + h],
            sem,
            half - 1 + core,
            began + 1 - v,
        )

    def first_halo(t):
        if t < 4:

            @pl.when(both(far, column != t))
            def _():
                for h in range(groups):
                    leg_one(t, h).start()

        pl.when(near_up)(lambda: to_up(t).start())
        pl.when(near_down)(lambda: to_down(t).start())

    def row_halo(t):
        pl.when(right)(lambda: to_right(t).start())
        pl.when(left)(lambda: to_left(t).start())

    def relay_one():
        for t in range(4):
            here = both(first_relay, column == t)

            @pl.when(both(here, near))
            def _():
                for h in range(groups):
                    leg_one(t, h).wait_recv()
                    if h == 0:
                        pl.semaphore_wait(ready, 1)
                    leg_two(relay.at[0, h], h).start()

            @pl.when(both(here, far))
            def _():
                pl.semaphore_wait(ready, 1)
                for h in range(groups):
                    leg_two(wide.at[t, h, edge + 1, 1], h).start()

    def relay_two(group):
        for t in range(4):
            for h in range(groups):
                here = both(group, column == t)

                @pl.when(both(here, second_relay))
                def _():
                    leg_two(relay.at[0, h], h).wait_recv()

                for v in (1, 0, 2):
                    pl.when(both(here, targets[v]))(lambda: leg_three(t, h, v).start())

    def summary(side):
        there = jnp.where(far_up, half, half - 1)
        return hop(part.at[0], part.at[1], part_sem.at[0], part_sem.at[1], there, r_at)

    def second_halo(t):
        pl.when(left)(lambda: to_right(t).wait_recv())
        pl.when(right)(lambda: to_left(t).wait_recv())
        pl.when(both(near_up, left))(lambda: side_up(t, 0).start())
        pl.when(both(near_up, right))(lambda: side_up(t, 2).start())
        pl.when(both(near_down, left))(lambda: side_down(t, 0).start())
        pl.when(both(near_down, right))(lambda: side_down(t, 2).start())

    def far_halo(t):
        if t < 4:
            pl.when(far_down)(lambda: to_up(t).wait_recv())
            pl.when(far_up)(lambda: to_down(t).wait_recv())
        if t == 4:
            pl.when(both(far_down, right))(lambda: along_right(t, 0).start())
            pl.when(both(far_down, left))(lambda: along_left(t, 0).start())
            pl.when(both(far_up, right))(lambda: along_right(t, 3).start())
            pl.when(both(far_up, left))(lambda: along_left(t, 3).start())

    def low_halo(t):
        pl.when(near_down)(lambda: to_up(t).wait_recv())
        pl.when(both(down, left))(lambda: side_up(t, 0).wait_recv())
        pl.when(both(down, right))(lambda: side_up(t, 2).wait_recv())

    def high_halo(t):
        pl.when(near_up)(lambda: to_down(t).wait_recv())
        pl.when(both(up, left))(lambda: side_down(t, 0).wait_recv())
        pl.when(both(up, right))(lambda: side_down(t, 2).wait_recv())

    def early_halo(*kinds):
        @pl.when(jnp.logical_not(far_down))
        def _():
            for t in kinds:
                low_halo(t)

        @pl.when(far_down)
        def _():
            for t in kinds:
                high_halo(t)

    def late_halo(*kinds):
        @pl.when(far_down)
        def _():
            for t in kinds:
                low_halo(t)

        @pl.when(jnp.logical_not(far_down))
        def _():
            for t in kinds:
                high_halo(t)

    def halo_sent(t):
        if t < 4:

            @pl.when(both(far, column != t))
            def _():
                for h in range(groups):
                    leg_one(t, h).wait_send()

        pl.when(near_up)(lambda: to_up(t).wait_send())
        pl.when(near_down)(lambda: to_down(t).wait_send())
        pl.when(right)(lambda: to_right(t).wait_send())
        pl.when(left)(lambda: to_left(t).wait_send())
        pl.when(both(near_up, left))(lambda: side_up(t, 0).wait_send())
        pl.when(both(near_up, right))(lambda: side_up(t, 2).wait_send())
        pl.when(both(near_down, left))(lambda: side_down(t, 0).wait_send())
        pl.when(both(near_down, right))(lambda: side_down(t, 2).wait_send())
        if t == 4:
            pl.when(both(far_down, right))(lambda: along_right(t, 0).wait_send())
            pl.when(both(far_down, left))(lambda: along_left(t, 0).wait_send())
            pl.when(both(far_up, right))(lambda: along_right(t, 3).wait_send())
            pl.when(both(far_up, left))(lambda: along_left(t, 3).wait_send())

    for j in range(3):
        loading_act(j).wait()

    lanes = lax.broadcasted_iota(jnp.int32, (1, 128), 1)

    def placed(i, j):
        frame, row = 2 * f_at - 1 + i, r_at - 1 + j
        return (frame >= 0) & (frame < 2 * frames) & (row >= 0) & (row < rows)

    def entry(i, j, l, slot, inside):
        frame = jnp.clip(2 * f_at - 1 + i, 0, 2 * frames - 1)
        return jnp.where(inside & (act[j, slot, l, frame] == 1), 0.0, NEG)

    def halves(pair_of):
        return jnp.where(lanes < 64, pair_of[0], pair_of[1])

    def mask_step(i, carry):
        f, a = i // 3, i % 3
        for b in range(3):
            span = pl.ds(pl.multiple_of(a * 384 + b * 128, 128), 128)
            inside = placed(f + a, b)
            for l in range(2):
                slots = [9 * a + 3 * b + m - l + 1 for m in range(2)]
                front[f, l, :, span] = halves([entry(f + 1, 1, l, n, inside) for n in slots])
                slots = [9 * (2 - a) + 3 * (2 - b) + l - m + 1 for m in range(2)]
                behind[f, l, :, span] = halves([entry(f + a, b, l, n, inside) for n in slots])
        return carry

    lax.fori_loop(0, 6, mask_step, 0)

    @pl.when(far)
    def _():
        for b in range(3):
            inside = placed(edge + 1, b)
            for l in range(2):
                slots = [18 * (1 - edge) + 3 * b + l - m + 1 for m in range(2)]
                pieces = [entry(beyond, 1, m, n, inside) for m, n in enumerate(slots)]
                across[2 * b + l] = halves(pieces)

    for t in range(4):
        loading(t).wait()
        for g in range(4):
            moved = nn(to_heads, land[t, pl.ds(g * tall, tall)]).astype(jnp.bfloat16)
            pack[t, :, g // 2, pl.ds(16 * (g % 2), 16)] = moved.reshape(heads_all, 16, 128)
        if t == 0:
            known = [right, left, near_up, near_down] + targets
            count = heads - 1 + sum(c.astype(jnp.int32) for c in known)
            count += 3 * far.astype(jnp.int32) + 9 * proxy.astype(jnp.int32)
            pl.semaphore_wait(barrier, count)
            pl.when(proxy)(tell)
        for k in range(1, heads):
            exchange(t, k).start()
        wide[t, :, pl.ds(1, 2), 1, pl.ds(pl.multiple_of(x_at * 32, 32), 32)] = pack[
            t, pl.ds(x_at * groups, groups)
        ]

    def gathered(t):
        for k in range(1, heads):
            arriving(t, k).wait_recv()

    gathered(KEY)
    first_halo(KEY)
    row_halo(KEY)
    gathered(VAL)
    first_halo(VAL)
    row_halo(VAL)
    second_halo(KEY)
    gathered(QRY)
    first_halo(QRY)
    second_halo(VAL)
    gathered(GRD)
    first_halo(GRD)

    lane_grid = lax.broadcasted_iota(jnp.int32, (128, 128), 1)
    power = scaling * math.log2(math.e)
    wide_rows = 9 * 128

    def as_rows(level, dot):
        return jnp.where(lane_grid == 0, level, dot).T[0:8]

    def query_step(i, carry):
        h, f = i % groups, (i // groups) ^ flip
        q = wide[QRY, h, f + 1, 1]
        g = wide[GRD, h, f + 1, 1]
        k_band = wide[KEY, h, pl.ds(f, 3)].reshape(wide_rows, 128)
        v_band = wide[VAL, h, pl.ds(f, 3)].reshape(wide_rows, 128)
        s = (nt(q, k_band).reshape(2, 64, wide_rows) + front[f]).reshape(128, wide_rows)
        top = jnp.max(s, axis=1, keepdims=True)
        p = jnp.exp2((s - top) * power)
        total = jnp.sum(p, axis=1, keepdims=True)
        inverse = 1.0 / total
        out = (nn(p.astype(jnp.bfloat16), v_band) * inverse).astype(jnp.bfloat16)
        own[0, h, f] = out
        dot = jnp.sum(g.astype(jnp.float32) * out.astype(jnp.float32), axis=1, keepdims=True)
        ds = (p * (nt(g, v_band) - dot)).astype(jnp.bfloat16)
        own[1, h, f] = (nn(ds, k_band) * (inverse * scaling)).astype(jnp.bfloat16)
        stats[h, f + 1, 1] = as_rows(top * power + jnp.log2(total), dot)
        return carry

    def near_step(h, carry):
        q = wide[QRY, h, edge + 1, 1]
        g = wide[GRD, h, edge + 1, 1]
        k_band = wide[KEY, h, pl.ds(1, 2)].reshape(6 * 128, 128)
        v_band = wide[VAL, h, pl.ds(1, 2)].reshape(6 * 128, 128)
        offset = pl.multiple_of((1 - edge) * 384, 128)
        mask = front[edge, :, :, pl.ds(offset, 768)]
        s = (nt(q, k_band).reshape(2, 64, 768) + mask).reshape(128, 768)
        top = jnp.max(s, axis=1, keepdims=True)
        p = jnp.exp2((s - top) * power)
        total = jnp.sum(p, axis=1, keepdims=True)
        dot = jnp.sum(p * nt(g, v_band), axis=1, keepdims=True) / total
        part[0, h] = as_rows(top * power + jnp.log2(total), dot)
        return carry

    def across_step(h, carry):
        q = wide[QRY, h, beyond, 1]
        g = wide[GRD, h, beyond, 1]
        k_band = wide[KEY, h, edge + 1].reshape(384, 128)
        v_band = wide[VAL, h, edge + 1].reshape(384, 128)
        s = ((nt(k_band, q) * power).reshape(6, 64, 128) + across[...]).reshape(384, 128)
        top = jnp.max(s, axis=0, keepdims=True)
        p = jnp.exp2(s - top)
        total = jnp.sum(p, axis=0, keepdims=True)
        dot = jnp.sum(p * nt(v_band, g), axis=0, keepdims=True) / total
        level = top + jnp.log2(total)
        level_near, dot_near = part[1, h, 0:1], part[1, h, 1:2]
        peak = jnp.maximum(level, level_near)
        whole = peak + jnp.log2(jnp.exp2(level - peak) + jnp.exp2(level_near - peak))
        mixed = jnp.exp2(level - whole) * dot + jnp.exp2(level_near - whole) * dot_near
        stats[h, beyond, 1, 0:1] = whole
        stats[h, beyond, 1, 1:2] = mixed
        return carry

    def key_step(i, carry):
        h, f = i % groups, (i // groups) ^ flip
        k = wide[KEY, h, f + 1, 1]
        v = wide[VAL, h, f + 1, 1]
        q_band = wide[QRY, h, pl.ds(f, 3)].reshape(wide_rows, 128)
        g_band = wide[GRD, h, pl.ds(f, 3)].reshape(wide_rows, 128)
        tiles = [stats[h, f + a, b] for a in range(3) for b in range(3)]
        level = jnp.concatenate([t[0:1] for t in tiles], axis=1)
        dot = jnp.concatenate([t[1:2] for t in tiles], axis=1)
        s = (nt(k, q_band) * power).reshape(2, 64, wide_rows) + (behind[f] - level)
        p = jnp.exp2(s.reshape(128, wide_rows))
        own[3, h, f] = nn(p.astype(jnp.bfloat16), g_band).astype(jnp.bfloat16)
        ds = (p * (nt(v, g_band) - dot)).astype(jnp.bfloat16)
        own[2, h, f] = (nn(ds, q_band) * scaling).astype(jnp.bfloat16)
        return carry

    def giving(o, half_at, k):
        f = half_at ^ flip
        spot = pl.ds(pl.multiple_of(peers[k] * 32, 32), 32)
        return pltpu.make_async_remote_copy(
            src_ref=own.at[o, :, f, spot],
            dst_ref=outs[o].at[pl.ds(x_at * groups, groups), f],
            send_sem=o_send.at[o, half_at, k - 1],
            recv_sem=o_recv.at[o, half_at, k - 1],
            device_id=(f_at, r_at, peers[k]),
            device_id_type=MESH,
        )

    def taking(o, half_at, k):
        f = half_at ^ flip
        return pltpu.make_async_remote_copy(
            src_ref=own.at[o, :, f, pl.ds(0, 32)],
            dst_ref=outs[o].at[pl.ds(froms[k] * groups, groups), f],
            send_sem=o_send.at[o, half_at, k - 1],
            recv_sem=o_recv.at[o, half_at, k - 1],
            device_id=(f_at, r_at, froms[k]),
            device_id_type=MESH,
        )

    def give(half_at, *kinds):
        f = half_at ^ flip
        for o in kinds:
            for k in range(1, heads):
                giving(o, half_at, k).start()
            keeping(o, half_at).start()

    def keeping(o, half_at):
        f = half_at ^ flip
        spot = pl.ds(pl.multiple_of(x_at * 32, 32), 32)
        return pltpu.make_async_copy(
            own.at[o, :, f, spot],
            outs[o].at[pl.ds(x_at * groups, groups), f],
            out_sem.at[o, half_at],
        )

    relay_one()

    @pl.when(far)
    def _():
        lax.fori_loop(0, groups, near_step, 0)

    pl.when(far)(lambda: summary(0).start())
    early_halo(KEY, VAL)
    row_halo(QRY)
    row_halo(GRD)
    lax.fori_loop(0, groups, query_step, 0)
    give(0, 0, 1)
    relay_two(far)

    @pl.when(far)
    def _():
        second_halo(QRY)
        second_halo(GRD)

    for t in range(4):
        far_halo(t)

    @pl.when(far)
    def _():
        summary(0).wait_recv()
        lax.fori_loop(0, groups, across_step, 0)

    far_halo(4)
    late_halo(KEY, VAL)
    lax.fori_loop(groups, groups * 2, query_step, 0)
    first_halo(4)
    row_halo(4)

    @pl.when(near)
    def _():
        second_halo(QRY)
        second_halo(GRD)

    give(1, 0, 1)
    relay_two(near)
    second_halo(4)
    early_halo(QRY, GRD, 4)
    lax.fori_loop(0, groups, key_step, 0)
    give(0, 2, 3)
    late_halo(QRY, GRD, 4)
    lax.fori_loop(groups, groups * 2, key_step, 0)
    give(1, 2, 3)

    for t in range(4):
        for k in range(1, heads):
            exchange(t, k).wait_send()
            giving(t, 0, k).wait_send()
            giving(t, 1, k).wait_send()
    for t in range(5):
        halo_sent(t)
    pl.when(far)(lambda: summary(0).wait_send())
    for h in range(groups):
        pl.when(first_relay)(lambda: leg_two(relay.at[0, h], h).wait_send())
        for v in range(3):
            pl.when(targets[v])(lambda: leg_three(0, h, v).wait_send())
    for o in range(4):
        for half_at in range(2):
            keeping(o, half_at).wait()
            for k in range(1, heads):
                taking(o, half_at, k).wait_recv()


def on_device(sizes, queries, keys, values, out_grad, active):
    frames, rows, heads, groups, scaling = sizes
    frames_here, rows_here, cols_here, heads_all, head_dim = queries.shape
    table = jnp.transpose(active, (1, 3, 2, 0))
    tall = frames_here * rows_here * cols_here * heads_all

    def flat(tensor):
        return jnp.transpose(tensor, (0, 1, 3, 2, 4)).reshape(tall, head_dim)

    def unflat(tensor):
        shaped = tensor.reshape(heads_all, frames_here, rows_here, cols_here, head_dim)
        return jnp.transpose(shaped, (1, 2, 3, 0, 4))

    dma = pltpu.SemaphoreType.DMA
    block = (128, head_dim)
    kinds = heads - 1
    anywhere = pl.BlockSpec(memory_space=pl.ANY)
    results = pl.pallas_call(
        functools.partial(tile_kernel, sizes),
        out_shape=[jax.ShapeDtypeStruct((heads_all, 2, 32, head_dim), jnp.bfloat16)] * 4,
        in_specs=[anywhere] * 5,
        out_specs=[anywhere] * 4,
        scratch_shapes=[
            pltpu.VMEM((4, tall, head_dim), jnp.bfloat16),
            pltpu.VMEM((4, heads_all, 2, 32, head_dim), jnp.bfloat16),
            pltpu.VMEM((4, groups, 4, 3) + block, jnp.bfloat16),
            pltpu.VMEM((groups, 4, 3, 8, 128), jnp.float32),
            pltpu.VMEM((4, groups, 2) + block, jnp.bfloat16),
            pltpu.VMEM((2, groups, 8, 128), jnp.float32),
            pltpu.VMEM((2, 2, 1, 9 * 128), jnp.float32),
            pltpu.VMEM((2, 2, 1, 9 * 128), jnp.float32),
            pltpu.VMEM((6, 1, 128), jnp.float32),
            pltpu.VMEM((2, groups) + block, jnp.bfloat16),
            pltpu.SMEM((3,) + table.shape[1:], jnp.int32),
            dma((4,)),
            dma((4, kinds)),
            dma((4, kinds)),
            dma((5, 2)),
            dma((5, 2)),
            dma((5, 2)),
            dma((5, 2)),
            dma((5, 4)),
            dma((5, 4)),
            dma((4, 2, kinds)),
            dma((4, 2, kinds)),
            dma((4, 2)),
            dma((2,)),
            dma((3,)),
            dma((8 * groups,)),
            dma((2, groups)),
            pltpu.SemaphoreType.REGULAR,
        ],
        compiler_params=pltpu.CompilerParams(
            collective_id=0, has_side_effects=True, vmem_limit_bytes=VMEM
        ),
    )(table, flat(keys), flat(values), flat(queries), flat(out_grad))
    return tuple(unflat(r) for r in results)


def solution(mesh):
    frames, rows, heads = (mesh.shape[a] for a in ("frame", "row", "head"))
    sizes = (frames, rows, heads, 12 // heads, 128**-0.5)
    spec = P("frame", "row", "head", None, None)
    return jax.shard_map(
        functools.partial(on_device, sizes),
        mesh=mesh,
        in_specs=(spec,) * 4 + (P(),),
        out_specs=(spec,) * 4,
        check_vma=False,
    )
```

```python
import functools
import math

import jax
import jax.numpy as jnp
from jax import lax
from jax.experimental import pallas as pl
from jax.experimental.pallas import tpu as pltpu
from jax.sharding import PartitionSpec as P

MESH = pl.DeviceIdType.MESH
NEG = -1e30
KEY, VAL, QRY, GRD = 0, 1, 2, 3
VMEM = 63 << 20


def nt(left, right):
    return lax.dot_general(
        left, right, (((1,), (1,)), ((), ())), preferred_element_type=jnp.float32
    )


def nn(left, right):
    return jnp.dot(left, right, preferred_element_type=jnp.float32)


def tile_kernel(sizes, act_in, k_in, v_in, q_in, g_in, *refs):
    frames, rows, heads, groups, scaling = sizes
    outs, refs = refs[:4], refs[4:]
    land, pack, wide, stats, own, part, front, behind, across, relay, act = refs[:11]
    in_sem, a_send, a_recv, z_send, z_recv, c_send, c_recv, d_send, d_recv = refs[11:20]
    o_send, o_recv, out_sem, part_sem, act_sem, leg_send, leg_recv, ready = refs[20:28]
    ins = (k_in, v_in, q_in, g_in)
    heads_all = groups * heads
    tall = heads_all * 16

    f_at = lax.axis_index("frame")
    r_at = lax.axis_index("row")
    x_at = lax.axis_index("head")
    up, down = f_at < frames - 1, f_at > 0
    right, left = r_at < rows - 1, r_at > 0
    far_up, far_down = f_at == frames // 2 - 1, f_at == frames // 2
    both = jnp.logical_and
    near_up = both(up, jnp.logical_not(far_up))
    near_down = both(down, jnp.logical_not(far_down))
    far = jnp.logical_or(far_up, far_down)

    half, turn = frames // 2, 2 * rows
    upper, place = f_at // half, f_at % half
    core, column = f_at % 2, place // 2
    z_at = upper * rows + r_at
    first_relay = core + upper == 1
    shifted = lax.rem(z_at + rows * (1 - core), turn)
    odd = lax.rem(shifted, 2)
    began = jnp.where(odd == 1, shifted - (rows - 1), lax.rem(shifted + turn - rows - 1, turn))
    second_relay = both(began >= 0, began < rows) & (lax.rem(began + turn, 2) == 1 - odd)
    near = jnp.logical_not(far)
    soon = both(upper == 1, r_at < rows // 2)
    later = jnp.logical_not(soon)

    def relays_of(z, row, member):
        spot = lax.rem(z + rows - 1 + 2 * lax.rem(row, 2), turn)
        return (spot // rows) * half + member, lax.rem(spot, rows)

    def start_relay(t):
        return upper * half + 2 * t + core, r_at

    def proxy_of(side, row):
        return half - 4 + 7 * side, row

    proxy = f_at == proxy_of(upper, r_at)[0]
    next_relay = relays_of(z_at, r_at, place)
    targets = [both(second_relay, both(began + 1 - v >= 0, began + 1 - v < rows)) for v in range(3)]
    edge = far_up.astype(jnp.int32)
    beyond = 3 * edge
    flip = far_down.astype(jnp.int32)

    peers = [lax.rem(x_at + k, heads) for k in range(heads)]
    froms = [lax.rem(x_at + heads - k, heads) for k in range(heads)]

    def loading(t):
        return pltpu.make_async_copy(ins[t], land.at[t], in_sem.at[t])

    def loading_act(j):
        row = jnp.clip(r_at - 1 + j, 0, rows - 1)
        return pltpu.make_async_copy(act_in.at[row], act.at[j], act_sem.at[j])

    for t in range(4):
        loading(t).start()
    for j in range(3):
        loading_act(j).start()

    barrier = pltpu.get_barrier_semaphore()

    def greet(frame, row, head):
        pl.semaphore_signal(barrier, inc=1, device_id=(frame, row, head), device_id_type=MESH)

    for k in range(1, heads):
        greet(f_at, r_at, peers[k])
    pl.when(right)(lambda: greet(f_at, r_at + 1, x_at))
    pl.when(left)(lambda: greet(f_at, r_at - 1, x_at))
    pl.when(near_up)(lambda: greet(f_at + 1, r_at, x_at))
    pl.when(near_down)(lambda: greet(f_at - 1, r_at, x_at))

    @pl.when(far)
    def _():
        greet(*proxy_of(1 - upper, r_at), x_at)
        for v, known in enumerate((left, f_at >= 0, right)):

            @pl.when(known)
            def _():
                for t in range(4):
                    z, row = z_at + rows + v - 1, r_at + v - 1
                    greet(*relays_of(z, row, 2 * t + 1 - core), x_at)

    pl.when(both(first_relay, near))(lambda: greet(half - 1 + upper, r_at, x_at))
    pl.when(first_relay)(lambda: greet(*proxy_of(upper, r_at), x_at))
    pl.when(second_relay)(lambda: greet(*proxy_of(1 - core, began), x_at))

    @pl.when(jnp.logical_not(left))
    def _():
        wide[:, :, :, 0] = jnp.zeros_like(wide[:, :, :, 0])
        stats[:, :, 0] = jnp.zeros_like(stats[:, :, 0])

    @pl.when(jnp.logical_not(right))
    def _():
        wide[:, :, :, 2] = jnp.zeros_like(wide[:, :, :, 2])
        stats[:, :, 2] = jnp.zeros_like(stats[:, :, 2])

    @pl.when(jnp.logical_not(down))
    def _():
        wide[:, :, 0] = jnp.zeros_like(wide[:, :, 0])
        stats[:, 0] = jnp.zeros_like(stats[:, 0])

    @pl.when(jnp.logical_not(up))
    def _():
        wide[:, :, 3] = jnp.zeros_like(wide[:, :, 3])
        stats[:, 3] = jnp.zeros_like(stats[:, 3])

    out_row = lax.broadcasted_iota(jnp.int32, (tall, tall), 0)
    in_row = lax.broadcasted_iota(jnp.int32, (tall, tall), 1)

    def swapped(row):
        return ((row % 16) // 4) * (4 * heads_all) + (row // 16) * 4 + row % 4

    to_heads = (swapped(out_row) == in_row).astype(jnp.bfloat16)

    def exchange(t, k):
        there = peers[k]
        return pltpu.make_async_remote_copy(
            src_ref=pack.at[t, pl.ds(there * groups, groups)],
            dst_ref=wide.at[t, :, pl.ds(1, 2), 1, pl.ds(pl.multiple_of(x_at * 32, 32), 32)],
            send_sem=a_send.at[t, k - 1],
            recv_sem=a_recv.at[t, k - 1],
            device_id=(f_at, r_at, there),
            device_id_type=MESH,
        )

    def arriving(t, k):
        spot = pl.ds(pl.multiple_of(froms[k] * 32, 32), 32)
        return pltpu.make_async_remote_copy(
            src_ref=pack.at[t, pl.ds(0, groups)],
            dst_ref=wide.at[t, :, pl.ds(1, 2), 1, spot],
            send_sem=a_send.at[t, k - 1],
            recv_sem=a_recv.at[t, k - 1],
            device_id=(f_at, r_at, froms[k]),
            device_id_type=MESH,
        )

    def block(t, frame, row):
        ref = stats if t == 4 else wide.at[t]
        return ref.at[:, frame, row]

    def pair(t, row):
        ref = stats if t == 4 else wide.at[t]
        return ref.at[:, pl.ds(1, 2), row]

    def hop(src, dst, ss, rs, frame, row):
        return pltpu.make_async_remote_copy(
            src_ref=src,
            dst_ref=dst,
            send_sem=ss,
            recv_sem=rs,
            device_id=(frame, row, x_at),
            device_id_type=MESH,
        )

    def to_right(t):
        return hop(pair(t, 1), pair(t, 0), z_send.at[t, 0], z_recv.at[t, 0], f_at, r_at + 1)

    def to_left(t):
        return hop(pair(t, 1), pair(t, 2), z_send.at[t, 1], z_recv.at[t, 1], f_at, r_at - 1)

    def to_up(t):
        return hop(block(t, 2, 1), block(t, 0, 1), c_send.at[t, 0], c_recv.at[t, 0], f_at + 1, r_at)

    def to_down(t):
        return hop(block(t, 1, 1), block(t, 3, 1), c_send.at[t, 1], c_recv.at[t, 1], f_at - 1, r_at)

    def side_up(t, row):
        sem = 0 if row == 0 else 1
        return hop(
            block(t, 2, row), block(t, 0, row), d_send.at[t, sem], d_recv.at[t, sem], f_at + 1, r_at
        )

    def side_down(t, row):
        sem = 2 if row == 0 else 3
        return hop(
            block(t, 1, row), block(t, 3, row), d_send.at[t, sem], d_recv.at[t, sem], f_at - 1, r_at
        )

    def along_right(t, frame):
        sem = 0 if frame == 0 else 2
        return hop(
            block(t, frame, 1), block(t, frame, 0), d_send.at[t, sem], d_recv.at[t, sem], f_at, r_at + 1
        )

    def along_left(t, frame):
        sem = 1 if frame == 0 else 3
        return hop(
            block(t, frame, 1), block(t, frame, 2), d_send.at[t, sem], d_recv.at[t, sem], f_at, r_at - 1
        )

    def tell():
        for t in range(4):
            there = (upper * half + 2 * t + 1 - core, r_at, x_at)
            pl.semaphore_signal(ready, inc=1, device_id=there, device_id_type=MESH)

    def leg_one(t, h):
        return hop(
            wide.at[t, h, edge + 1, 1],
            relay.at[0, h],
            leg_send.at[t * groups + h],
            leg_recv.at[0, h],
            *start_relay(t),
        )

    def leg_two(src, h):
        return hop(
            src, relay.at[1, h], leg_send.at[4 * groups + h], leg_recv.at[1, h], *next_relay
        )

    def leg_three(t, h, v):
        side = 1 - core
        sem = c_recv.at[t, side] if v == 1 else d_recv.at[t, 2 * side + v // 2]
        return hop(
            relay.at[1, h],
            wide.at[t, h, 3 * side, v],
            leg_send.at[(5 + v) * groups + h],
            sem,
            half - 1 + core,
            began + 1 - v,
        )

    def first_halo(t):
        if t < 4:

            @pl.when(both(far, column != t))
            def _():
                for h in range(groups):
                    leg_one(t, h).start()

        pl.when(near_up)(lambda: to_up(t).start())
        pl.when(near_down)(lambda: to_down(t).start())

    def row_halo(t):
        pl.when(right)(lambda: to_right(t).start())
        pl.when(left)(lambda: to_left(t).start())

    def relay_one(group, *kinds):
        for t in kinds:
            here = both(group, both(first_relay, column == t))

            @pl.when(both(here, near))
            def _():
                for h in range(groups):
                    leg_one(t, h).wait_recv()
                    if h == 0:
                        pl.semaphore_wait(ready, 1)
                    leg_two(relay.at[0, h], h).start()

            @pl.when(both(here, far))
            def _():
                pl.semaphore_wait(ready, 1)
                for h in range(groups):
                    leg_two(wide.at[t, h, edge + 1, 1], h).start()

    def relay_two(group):
        for t in range(4):
            for h in range(groups):
                here = both(group, column == t)

                @pl.when(both(here, second_relay))
                def _():
                    leg_two(relay.at[0, h], h).wait_recv()

                for v in (1, 0, 2):
                    pl.when(both(here, targets[v]))(lambda: leg_three(t, h, v).start())

    def summary(side):
        there = jnp.where(far_up, half, half - 1)
        return hop(part.at[0], part.at[1], part_sem.at[0], part_sem.at[1], there, r_at)

    def second_halo(t):
        pl.when(left)(lambda: to_right(t).wait_recv())
        pl.when(right)(lambda: to_left(t).wait_recv())
        pl.when(both(near_up, left))(lambda: side_up(t, 0).start())
        pl.when(both(near_up, right))(lambda: side_up(t, 2).start())
        pl.when(both(near_down, left))(lambda: side_down(t, 0).start())
        pl.when(both(near_down, right))(lambda: side_down(t, 2).start())

    def far_halo(t):
        if t < 4:
            pl.when(far_down)(lambda: to_up(t).wait_recv())
            pl.when(far_up)(lambda: to_down(t).wait_recv())
        if t == 4:
            pl.when(both(far_down, right))(lambda: along_right(t, 0).start())
            pl.when(both(far_down, left))(lambda: along_left(t, 0).start())
            pl.when(both(far_up, right))(lambda: along_right(t, 3).start())
            pl.when(both(far_up, left))(lambda: along_left(t, 3).start())

    def low_halo(t):
        pl.when(near_down)(lambda: to_up(t).wait_recv())
        pl.when(both(down, left))(lambda: side_up(t, 0).wait_recv())
        pl.when(both(down, right))(lambda: side_up(t, 2).wait_recv())

    def high_halo(t):
        pl.when(near_up)(lambda: to_down(t).wait_recv())
        pl.when(both(up, left))(lambda: side_down(t, 0).wait_recv())
        pl.when(both(up, right))(lambda: side_down(t, 2).wait_recv())

    def early_halo(*kinds):
        @pl.when(jnp.logical_not(far_down))
        def _():
            for t in kinds:
                low_halo(t)

        @pl.when(far_down)
        def _():
            for t in kinds:
                high_halo(t)

    def late_halo(*kinds):
        @pl.when(far_down)
        def _():
            for t in kinds:
                low_halo(t)

        @pl.when(jnp.logical_not(far_down))
        def _():
            for t in kinds:
                high_halo(t)

    def halo_sent(t):
        if t < 4:

            @pl.when(both(far, column != t))
            def _():
                for h in range(groups):
                    leg_one(t, h).wait_send()

        pl.when(near_up)(lambda: to_up(t).wait_send())
        pl.when(near_down)(lambda: to_down(t).wait_send())
        pl.when(right)(lambda: to_right(t).wait_send())
        pl.when(left)(lambda: to_left(t).wait_send())
        pl.when(both(near_up, left))(lambda: side_up(t, 0).wait_send())
        pl.when(both(near_up, right))(lambda: side_up(t, 2).wait_send())
        pl.when(both(near_down, left))(lambda: side_down(t, 0).wait_send())
        pl.when(both(near_down, right))(lambda: side_down(t, 2).wait_send())
        if t == 4:
            pl.when(both(far_down, right))(lambda: along_right(t, 0).wait_send())
            pl.when(both(far_down, left))(lambda: along_left(t, 0).wait_send())
            pl.when(both(far_up, right))(lambda: along_right(t, 3).wait_send())
            pl.when(both(far_up, left))(lambda: along_left(t, 3).wait_send())

    for j in range(3):
        loading_act(j).wait()

    lanes = lax.broadcasted_iota(jnp.int32, (1, 128), 1)

    def placed(i, j):
        frame, row = 2 * f_at - 1 + i, r_at - 1 + j
        return (frame >= 0) & (frame < 2 * frames) & (row >= 0) & (row < rows)

    def entry(i, j, l, slot, inside):
        frame = jnp.clip(2 * f_at - 1 + i, 0, 2 * frames - 1)
        return jnp.where(inside & (act[j, slot, l, frame] == 1), 0.0, NEG)

    def halves(pair_of):
        return jnp.where(lanes < 64, pair_of[0], pair_of[1])

    def mask_step(i, carry):
        f, a = i // 3, i % 3
        for b in range(3):
            span = pl.ds(pl.multiple_of(a * 384 + b * 128, 128), 128)
            inside = placed(f + a, b)
            for l in range(2):
                slots = [9 * a + 3 * b + m - l + 1 for m in range(2)]
                front[f, l, :, span] = halves([entry(f + 1, 1, l, n, inside) for n in slots])
                slots = [9 * (2 - a) + 3 * (2 - b) + l - m + 1 for m in range(2)]
                behind[f, l, :, span] = halves([entry(f + a, b, l, n, inside) for n in slots])
        return carry

    lax.fori_loop(0, 6, mask_step, 0)

    @pl.when(far)
    def _():
        for b in range(3):
            inside = placed(edge + 1, b)
            for l in range(2):
                slots = [18 * (1 - edge) + 3 * b + l - m + 1 for m in range(2)]
                pieces = [entry(beyond, 1, m, n, inside) for m, n in enumerate(slots)]
                across[2 * b + l] = halves(pieces)

    for t in range(4):
        loading(t).wait()
        for g in range(4):
            moved = nn(to_heads, land[t, pl.ds(g * tall, tall)]).astype(jnp.bfloat16)
            pack[t, :, g // 2, pl.ds(16 * (g % 2), 16)] = moved.reshape(heads_all, 16, 128)
        if t == 0:
            known = [right, left, near_up, near_down] + targets
            count = heads - 1 + sum(c.astype(jnp.int32) for c in known)
            count += 3 * far.astype(jnp.int32) + 9 * proxy.astype(jnp.int32)
            pl.semaphore_wait(barrier, count)
            pl.when(proxy)(tell)
        for k in range(1, heads):
            exchange(t, k).start()
        wide[t, :, pl.ds(1, 2), 1, pl.ds(pl.multiple_of(x_at * 32, 32), 32)] = pack[
            t, pl.ds(x_at * groups, groups)
        ]

    def gathered(t):
        for k in range(1, heads):
            arriving(t, k).wait_recv()

    gathered(KEY)
    first_halo(KEY)
    row_halo(KEY)
    gathered(VAL)
    first_halo(VAL)
    row_halo(VAL)
    relay_one(soon, KEY)
    second_halo(KEY)
    gathered(QRY)
    first_halo(QRY)
    relay_one(soon, VAL)
    second_halo(VAL)
    gathered(GRD)
    first_halo(GRD)
    relay_one(soon, QRY, GRD)

    lane_grid = lax.broadcasted_iota(jnp.int32, (128, 128), 1)
    power = scaling * math.log2(math.e)
    wide_rows = 9 * 128

    def as_rows(level, dot):
        return jnp.where(lane_grid == 0, level, dot).T[0:8]

    def query_step(i, carry):
        h, f = i % groups, (i // groups) ^ flip
        q = wide[QRY, h, f + 1, 1]
        g = wide[GRD, h, f + 1, 1]
        k_band = wide[KEY, h, pl.ds(f, 3)].reshape(wide_rows, 128)
        v_band = wide[VAL, h, pl.ds(f, 3)].reshape(wide_rows, 128)
        s = (nt(q, k_band).reshape(2, 64, wide_rows) + front[f]).reshape(128, wide_rows)
        top = jnp.max(s, axis=1, keepdims=True)
        p = jnp.exp2((s - top) * power)
        total = jnp.sum(p, axis=1, keepdims=True)
        inverse = 1.0 / total
        out = (nn(p.astype(jnp.bfloat16), v_band) * inverse).astype(jnp.bfloat16)
        own[0, h, f] = out
        dot = jnp.sum(g.astype(jnp.float32) * out.astype(jnp.float32), axis=1, keepdims=True)
        ds = (p * (nt(g, v_band) - dot)).astype(jnp.bfloat16)
        own[1, h, f] = (nn(ds, k_band) * (inverse * scaling)).astype(jnp.bfloat16)
        stats[h, f + 1, 1] = as_rows(top * power + jnp.log2(total), dot)
        return carry

    def near_step(h, carry):
        q = wide[QRY, h, edge + 1, 1]
        g = wide[GRD, h, edge + 1, 1]
        k_band = wide[KEY, h, pl.ds(1, 2)].reshape(6 * 128, 128)
        v_band = wide[VAL, h, pl.ds(1, 2)].reshape(6 * 128, 128)
        offset = pl.multiple_of((1 - edge) * 384, 128)
        mask = front[edge, :, :, pl.ds(offset, 768)]
        s = (nt(q, k_band).reshape(2, 64, 768) + mask).reshape(128, 768)
        top = jnp.max(s, axis=1, keepdims=True)
        p = jnp.exp2((s - top) * power)
        total = jnp.sum(p, axis=1, keepdims=True)
        dot = jnp.sum(p * nt(g, v_band), axis=1, keepdims=True) / total
        part[0, h] = as_rows(top * power + jnp.log2(total), dot)
        return carry

    def across_step(h, carry):
        q = wide[QRY, h, beyond, 1]
        g = wide[GRD, h, beyond, 1]
        k_band = wide[KEY, h, edge + 1].reshape(384, 128)
        v_band = wide[VAL, h, edge + 1].reshape(384, 128)
        s = ((nt(k_band, q) * power).reshape(6, 64, 128) + across[...]).reshape(384, 128)
        top = jnp.max(s, axis=0, keepdims=True)
        p = jnp.exp2(s - top)
        total = jnp.sum(p, axis=0, keepdims=True)
        dot = jnp.sum(p * nt(v_band, g), axis=0, keepdims=True) / total
        level = top + jnp.log2(total)
        level_near, dot_near = part[1, h, 0:1], part[1, h, 1:2]
        peak = jnp.maximum(level, level_near)
        whole = peak + jnp.log2(jnp.exp2(level - peak) + jnp.exp2(level_near - peak))
        mixed = jnp.exp2(level - whole) * dot + jnp.exp2(level_near - whole) * dot_near
        stats[h, beyond, 1, 0:1] = whole
        stats[h, beyond, 1, 1:2] = mixed
        return carry

    def key_step(i, carry):
        h, f = i % groups, (i // groups) ^ flip
        k = wide[KEY, h, f + 1, 1]
        v = wide[VAL, h, f + 1, 1]
        q_band = wide[QRY, h, pl.ds(f, 3)].reshape(wide_rows, 128)
        g_band = wide[GRD, h, pl.ds(f, 3)].reshape(wide_rows, 128)
        tiles = [stats[h, f + a, b] for a in range(3) for b in range(3)]
        level = jnp.concatenate([t[0:1] for t in tiles], axis=1)
        dot = jnp.concatenate([t[1:2] for t in tiles], axis=1)
        s = (nt(k, q_band) * power).reshape(2, 64, wide_rows) + (behind[f] - level)
        p = jnp.exp2(s.reshape(128, wide_rows))
        own[3, h, f] = nn(p.astype(jnp.bfloat16), g_band).astype(jnp.bfloat16)
        ds = (p * (nt(v, g_band) - dot)).astype(jnp.bfloat16)
        own[2, h, f] = (nn(ds, q_band) * scaling).astype(jnp.bfloat16)
        return carry

    def giving(o, half_at, k):
        f = half_at ^ flip
        spot = pl.ds(pl.multiple_of(peers[k] * 32, 32), 32)
        return pltpu.make_async_remote_copy(
            src_ref=own.at[o, :, f, spot],
            dst_ref=outs[o].at[pl.ds(x_at * groups, groups), f],
            send_sem=o_send.at[o, half_at, k - 1],
            recv_sem=o_recv.at[o, half_at, k - 1],
            device_id=(f_at, r_at, peers[k]),
            device_id_type=MESH,
        )

    def taking(o, half_at, k):
        f = half_at ^ flip
        return pltpu.make_async_remote_copy(
            src_ref=own.at[o, :, f, pl.ds(0, 32)],
            dst_ref=outs[o].at[pl.ds(froms[k] * groups, groups), f],
            send_sem=o_send.at[o, half_at, k - 1],
            recv_sem=o_recv.at[o, half_at, k - 1],
            device_id=(f_at, r_at, froms[k]),
            device_id_type=MESH,
        )

    def give(half_at, *kinds):
        f = half_at ^ flip
        for o in kinds:
            for k in range(1, heads):
                giving(o, half_at, k).start()
            keeping(o, half_at).start()

    def keeping(o, half_at):
        f = half_at ^ flip
        spot = pl.ds(pl.multiple_of(x_at * 32, 32), 32)
        return pltpu.make_async_copy(
            own.at[o, :, f, spot],
            outs[o].at[pl.ds(x_at * groups, groups), f],
            out_sem.at[o, half_at],
        )

    relay_one(later, KEY, VAL, QRY, GRD)

    @pl.when(far)
    def _():
        lax.fori_loop(0, groups, near_step, 0)

    pl.when(far)(lambda: summary(0).start())
    early_halo(KEY, VAL)
    row_halo(QRY)
    row_halo(GRD)
    lax.fori_loop(0, groups, query_step, 0)
    give(0, 0, 1)
    relay_two(far_down)

    @pl.when(far)
    def _():
        second_halo(QRY)
        second_halo(GRD)

    far_halo(KEY)
    far_halo(VAL)
    late_halo(KEY, VAL)
    lax.fori_loop(groups, groups * 2, query_step, 0)
    first_halo(4)
    row_halo(4)

    @pl.when(near)
    def _():
        second_halo(QRY)
        second_halo(GRD)

    give(1, 0, 1)
    relay_two(jnp.logical_not(far_down))
    second_halo(4)
    early_halo(QRY, GRD, 4)
    lax.fori_loop(0, groups, key_step, 0)
    give(0, 2, 3)
    far_halo(QRY)
    far_halo(GRD)

    @pl.when(far)
    def _():
        summary(0).wait_recv()
        lax.fori_loop(0, groups, across_step, 0)

    far_halo(4)
    late_halo(QRY, GRD, 4)
    lax.fori_loop(groups, groups * 2, key_step, 0)
    give(1, 2, 3)

    for t in range(4):
        for k in range(1, heads):
            exchange(t, k).wait_send()
            giving(t, 0, k).wait_send()
            giving(t, 1, k).wait_send()
    for t in range(5):
        halo_sent(t)
    pl.when(far)(lambda: summary(0).wait_send())
    for h in range(groups):
        pl.when(first_relay)(lambda: leg_two(relay.at[0, h], h).wait_send())
        for v in range(3):
            pl.when(targets[v])(lambda: leg_three(0, h, v).wait_send())
    for o in range(4):
        for half_at in range(2):
            keeping(o, half_at).wait()
            for k in range(1, heads):
                taking(o, half_at, k).wait_recv()


def on_device(sizes, queries, keys, values, out_grad, active):
    frames, rows, heads, groups, scaling = sizes
    frames_here, rows_here, cols_here, heads_all, head_dim = queries.shape
    table = jnp.transpose(active, (1, 3, 2, 0))
    tall = frames_here * rows_here * cols_here * heads_all

    def flat(tensor):
        return jnp.transpose(tensor, (0, 1, 3, 2, 4)).reshape(tall, head_dim)

    def unflat(tensor):
        shaped = tensor.reshape(heads_all, frames_here, rows_here, cols_here, head_dim)
        return jnp.transpose(shaped, (1, 2, 3, 0, 4))

    dma = pltpu.SemaphoreType.DMA
    block = (128, head_dim)
    kinds = heads - 1
    anywhere = pl.BlockSpec(memory_space=pl.ANY)
    results = pl.pallas_call(
        functools.partial(tile_kernel, sizes),
        out_shape=[jax.ShapeDtypeStruct((heads_all, 2, 32, head_dim), jnp.bfloat16)] * 4,
        in_specs=[anywhere] * 5,
        out_specs=[anywhere] * 4,
        scratch_shapes=[
            pltpu.VMEM((4, tall, head_dim), jnp.bfloat16),
            pltpu.VMEM((4, heads_all, 2, 32, head_dim), jnp.bfloat16),
            pltpu.VMEM((4, groups, 4, 3) + block, jnp.bfloat16),
            pltpu.VMEM((groups, 4, 3, 8, 128), jnp.float32),
            pltpu.VMEM((4, groups, 2) + block, jnp.bfloat16),
            pltpu.VMEM((2, groups, 8, 128), jnp.float32),
            pltpu.VMEM((2, 2, 1, 9 * 128), jnp.float32),
            pltpu.VMEM((2, 2, 1, 9 * 128), jnp.float32),
            pltpu.VMEM((6, 1, 128), jnp.float32),
            pltpu.VMEM((2, groups) + block, jnp.bfloat16),
            pltpu.SMEM((3,) + table.shape[1:], jnp.int32),
            dma((4,)),
            dma((4, kinds)),
            dma((4, kinds)),
            dma((5, 2)),
            dma((5, 2)),
            dma((5, 2)),
            dma((5, 2)),
            dma((5, 4)),
            dma((5, 4)),
            dma((4, 2, kinds)),
            dma((4, 2, kinds)),
            dma((4, 2)),
            dma((2,)),
            dma((3,)),
            dma((8 * groups,)),
            dma((2, groups)),
            pltpu.SemaphoreType.REGULAR,
        ],
        compiler_params=pltpu.CompilerParams(
            collective_id=0, has_side_effects=True, vmem_limit_bytes=VMEM
        ),
    )(table, flat(keys), flat(values), flat(queries), flat(out_grad))
    return tuple(unflat(r) for r in results)


def solution(mesh):
    frames, rows, heads = (mesh.shape[a] for a in ("frame", "row", "head"))
    sizes = (frames, rows, heads, 12 // heads, 128**-0.5)
    spec = P("frame", "row", "head", None, None)
    return jax.shard_map(
        functools.partial(on_device, sizes),
        mesh=mesh,
        in_specs=(spec,) * 4 + (P(),),
        out_specs=(spec,) * 4,
        check_vma=False,
    )
```

```python
import functools
import math

import jax
import jax.numpy as jnp
from jax import lax
from jax.experimental import pallas as pl
from jax.experimental.pallas import tpu as pltpu
from jax.sharding import PartitionSpec as P

MESH = pl.DeviceIdType.MESH
NEG = -1e30
KEY, VAL, QRY, GRD = 0, 1, 2, 3
VMEM = 63 << 20


def nt(left, right):
    return lax.dot_general(
        left, right, (((1,), (1,)), ((), ())), preferred_element_type=jnp.float32
    )


def nn(left, right):
    return jnp.dot(left, right, preferred_element_type=jnp.float32)


def tile_kernel(sizes, act_in, k_in, v_in, q_in, g_in, *refs):
    frames, rows, heads, groups, scaling = sizes
    outs, refs = refs[:4], refs[4:]
    land, pack, wide, stats, own, part, front, behind, across, relay, act = refs[:11]
    in_sem, a_send, a_recv, z_send, z_recv, c_send, c_recv, d_send, d_recv = refs[11:20]
    o_send, o_recv, out_sem, part_sem, act_sem, leg_send, leg_recv, ready = refs[20:28]
    ins = (k_in, v_in, q_in, g_in)
    heads_all = groups * heads
    tall = heads_all * 16

    f_at = lax.axis_index("frame")
    r_at = lax.axis_index("row")
    x_at = lax.axis_index("head")
    up, down = f_at < frames - 1, f_at > 0
    right, left = r_at < rows - 1, r_at > 0
    far_up, far_down = f_at == frames // 2 - 1, f_at == frames // 2
    both = jnp.logical_and
    near_up = both(up, jnp.logical_not(far_up))
    near_down = both(down, jnp.logical_not(far_down))
    far = jnp.logical_or(far_up, far_down)

    half, turn = frames // 2, 2 * rows
    upper, place = f_at // half, f_at % half
    core, column = f_at % 2, place // 2
    z_at = upper * rows + r_at
    first_relay = core + upper == 1
    shifted = lax.rem(z_at + rows * (1 - core), turn)
    odd = lax.rem(shifted, 2)
    began = jnp.where(odd == 1, shifted - (rows - 1), lax.rem(shifted + turn - rows - 1, turn))
    second_relay = both(began >= 0, began < rows) & (lax.rem(began + turn, 2) == 1 - odd)
    near = jnp.logical_not(far)
    soon = both(upper == 1, r_at < rows // 2)
    later = jnp.logical_not(soon)

    def relays_of(z, row, member):
        spot = lax.rem(z + rows - 1 + 2 * lax.rem(row, 2), turn)
        return (spot // rows) * half + member, lax.rem(spot, rows)

    def start_relay(t):
        return upper * half + 2 * t + core, r_at

    def proxy_of(side, row):
        return half - 4 + 7 * side, row

    proxy = f_at == proxy_of(upper, r_at)[0]
    next_relay = relays_of(z_at, r_at, place)
    targets = [both(second_relay, both(began + 1 - v >= 0, began + 1 - v < rows)) for v in range(3)]
    edge = far_up.astype(jnp.int32)
    beyond = 3 * edge
    flip = far_down.astype(jnp.int32)

    peers = [lax.rem(x_at + k, heads) for k in range(heads)]
    froms = [lax.rem(x_at + heads - k, heads) for k in range(heads)]

    def loading(t):
        return pltpu.make_async_copy(ins[t], land.at[t], in_sem.at[t])

    def loading_act(j):
        row = jnp.clip(r_at - 1 + j, 0, rows - 1)
        return pltpu.make_async_copy(act_in.at[row], act.at[j], act_sem.at[j])

    for t in range(4):
        loading(t).start()
    for j in range(3):
        loading_act(j).start()

    barrier = pltpu.get_barrier_semaphore()

    def greet(frame, row, head):
        pl.semaphore_signal(barrier, inc=1, device_id=(frame, row, head), device_id_type=MESH)

    for k in range(1, heads):
        greet(f_at, r_at, peers[k])
    pl.when(right)(lambda: greet(f_at, r_at + 1, x_at))
    pl.when(left)(lambda: greet(f_at, r_at - 1, x_at))
    pl.when(near_up)(lambda: greet(f_at + 1, r_at, x_at))
    pl.when(near_down)(lambda: greet(f_at - 1, r_at, x_at))

    @pl.when(far)
    def _():
        greet(*proxy_of(1 - upper, r_at), x_at)
        for v, known in enumerate((left, f_at >= 0, right)):

            @pl.when(known)
            def _():
                for t in range(4):
                    z, row = z_at + rows + v - 1, r_at + v - 1
                    greet(*relays_of(z, row, 2 * t + 1 - core), x_at)

    pl.when(both(first_relay, near))(lambda: greet(half - 1 + upper, r_at, x_at))
    pl.when(first_relay)(lambda: greet(*proxy_of(upper, r_at), x_at))
    pl.when(second_relay)(lambda: greet(*proxy_of(1 - core, began), x_at))

    @pl.when(jnp.logical_not(left))
    def _():
        wide[:, :, :, 0] = jnp.zeros_like(wide[:, :, :, 0])
        stats[:, :, 0] = jnp.zeros_like(stats[:, :, 0])

    @pl.when(jnp.logical_not(right))
    def _():
        wide[:, :, :, 2] = jnp.zeros_like(wide[:, :, :, 2])
        stats[:, :, 2] = jnp.zeros_like(stats[:, :, 2])

    @pl.when(jnp.logical_not(down))
    def _():
        wide[:, :, 0] = jnp.zeros_like(wide[:, :, 0])
        stats[:, 0] = jnp.zeros_like(stats[:, 0])

    @pl.when(jnp.logical_not(up))
    def _():
        wide[:, :, 3] = jnp.zeros_like(wide[:, :, 3])
        stats[:, 3] = jnp.zeros_like(stats[:, 3])

    out_row = lax.broadcasted_iota(jnp.int32, (tall, tall), 0)
    in_row = lax.broadcasted_iota(jnp.int32, (tall, tall), 1)

    def swapped(row):
        return ((row % 16) // 4) * (4 * heads_all) + (row // 16) * 4 + row % 4

    to_heads = (swapped(out_row) == in_row).astype(jnp.bfloat16)

    def exchange(t, k):
        there = peers[k]
        return pltpu.make_async_remote_copy(
            src_ref=pack.at[t, pl.ds(there * groups, groups)],
            dst_ref=wide.at[t, :, pl.ds(1, 2), 1, pl.ds(pl.multiple_of(x_at * 32, 32), 32)],
            send_sem=a_send.at[t, k - 1],
            recv_sem=a_recv.at[t, k - 1],
            device_id=(f_at, r_at, there),
            device_id_type=MESH,
        )

    def arriving(t, k):
        spot = pl.ds(pl.multiple_of(froms[k] * 32, 32), 32)
        return pltpu.make_async_remote_copy(
            src_ref=pack.at[t, pl.ds(0, groups)],
            dst_ref=wide.at[t, :, pl.ds(1, 2), 1, spot],
            send_sem=a_send.at[t, k - 1],
            recv_sem=a_recv.at[t, k - 1],
            device_id=(f_at, r_at, froms[k]),
            device_id_type=MESH,
        )

    def block(t, frame, row):
        ref = stats if t == 4 else wide.at[t]
        return ref.at[:, frame, row]

    def pair(t, row):
        ref = stats if t == 4 else wide.at[t]
        return ref.at[:, pl.ds(1, 2), row]

    def hop(src, dst, ss, rs, frame, row):
        return pltpu.make_async_remote_copy(
            src_ref=src,
            dst_ref=dst,
            send_sem=ss,
            recv_sem=rs,
            device_id=(frame, row, x_at),
            device_id_type=MESH,
        )

    def to_right(t):
        return hop(pair(t, 1), pair(t, 0), z_send.at[t, 0], z_recv.at[t, 0], f_at, r_at + 1)

    def to_left(t):
        return hop(pair(t, 1), pair(t, 2), z_send.at[t, 1], z_recv.at[t, 1], f_at, r_at - 1)

    def to_up(t):
        return hop(block(t, 2, 1), block(t, 0, 1), c_send.at[t, 0], c_recv.at[t, 0], f_at + 1, r_at)

    def to_down(t):
        return hop(block(t, 1, 1), block(t, 3, 1), c_send.at[t, 1], c_recv.at[t, 1], f_at - 1, r_at)

    def side_up(t, row):
        sem = 0 if row == 0 else 1
        return hop(
            block(t, 2, row), block(t, 0, row), d_send.at[t, sem], d_recv.at[t, sem], f_at + 1, r_at
        )

    def side_down(t, row):
        sem = 2 if row == 0 else 3
        return hop(
            block(t, 1, row), block(t, 3, row), d_send.at[t, sem], d_recv.at[t, sem], f_at - 1, r_at
        )

    def along_right(t, frame):
        sem = 0 if frame == 0 else 2
        return hop(
            block(t, frame, 1), block(t, frame, 0), d_send.at[t, sem], d_recv.at[t, sem], f_at, r_at + 1
        )

    def along_left(t, frame):
        sem = 1 if frame == 0 else 3
        return hop(
            block(t, frame, 1), block(t, frame, 2), d_send.at[t, sem], d_recv.at[t, sem], f_at, r_at - 1
        )

    def tell():
        for t in range(4):
            there = (upper * half + 2 * t + 1 - core, r_at, x_at)
            pl.semaphore_signal(ready, inc=1, device_id=there, device_id_type=MESH)

    def leg_one(t, h):
        return hop(
            wide.at[t, h, edge + 1, 1],
            relay.at[0, h],
            leg_send.at[t * groups + h],
            leg_recv.at[0, h],
            *start_relay(t),
        )

    def leg_two(src, h):
        return hop(
            src, relay.at[1, h], leg_send.at[4 * groups + h], leg_recv.at[1, h], *next_relay
        )

    def leg_three(t, h, v):
        side = 1 - core
        sem = c_recv.at[t, side] if v == 1 else d_recv.at[t, 2 * side + v // 2]
        return hop(
            relay.at[1, h],
            wide.at[t, h, 3 * side, v],
            leg_send.at[(5 + v) * groups + h],
            sem,
            half - 1 + core,
            began + 1 - v,
        )

    def first_halo(t):
        if t < 4:

            @pl.when(both(far, column != t))
            def _():
                for h in range(groups):
                    leg_one(t, h).start()

        pl.when(near_up)(lambda: to_up(t).start())
        pl.when(near_down)(lambda: to_down(t).start())

    def row_halo(t):
        pl.when(right)(lambda: to_right(t).start())
        pl.when(left)(lambda: to_left(t).start())

    def relay_one(group, *kinds):
        for t in kinds:
            here = both(group, both(first_relay, column == t))

            @pl.when(both(here, near))
            def _():
                for h in range(groups):
                    leg_one(t, h).wait_recv()
                    if h == 0:
                        pl.semaphore_wait(ready, 1)
                    leg_two(relay.at[0, h], h).start()

            @pl.when(both(here, far))
            def _():
                pl.semaphore_wait(ready, 1)
                for h in range(groups):
                    leg_two(wide.at[t, h, edge + 1, 1], h).start()

    def relay_two(group):
        for t in range(4):
            for h in range(groups):
                here = both(group, column == t)

                @pl.when(both(here, second_relay))
                def _():
                    leg_two(relay.at[0, h], h).wait_recv()

                for v in (1, 0, 2):
                    pl.when(both(here, targets[v]))(lambda: leg_three(t, h, v).start())

    def summary(side):
        there = jnp.where(far_up, half, half - 1)
        return hop(part.at[0], part.at[1], part_sem.at[0], part_sem.at[1], there, r_at)

    def second_halo(t):
        pl.when(left)(lambda: to_right(t).wait_recv())
        pl.when(right)(lambda: to_left(t).wait_recv())
        pl.when(both(near_up, left))(lambda: side_up(t, 0).start())
        pl.when(both(near_up, right))(lambda: side_up(t, 2).start())
        pl.when(both(near_down, left))(lambda: side_down(t, 0).start())
        pl.when(both(near_down, right))(lambda: side_down(t, 2).start())

    def far_halo(t):
        if t < 4:
            pl.when(far_down)(lambda: to_up(t).wait_recv())
            pl.when(far_up)(lambda: to_down(t).wait_recv())
        if t == 4:
            pl.when(both(far_down, right))(lambda: along_right(t, 0).start())
            pl.when(both(far_down, left))(lambda: along_left(t, 0).start())
            pl.when(both(far_up, right))(lambda: along_right(t, 3).start())
            pl.when(both(far_up, left))(lambda: along_left(t, 3).start())

    def low_halo(t):
        pl.when(near_down)(lambda: to_up(t).wait_recv())
        pl.when(both(down, left))(lambda: side_up(t, 0).wait_recv())
        pl.when(both(down, right))(lambda: side_up(t, 2).wait_recv())

    def high_halo(t):
        pl.when(near_up)(lambda: to_down(t).wait_recv())
        pl.when(both(up, left))(lambda: side_down(t, 0).wait_recv())
        pl.when(both(up, right))(lambda: side_down(t, 2).wait_recv())

    def early_halo(*kinds):
        @pl.when(jnp.logical_not(far_down))
        def _():
            for t in kinds:
                low_halo(t)

        @pl.when(far_down)
        def _():
            for t in kinds:
                high_halo(t)

    def late_halo(*kinds):
        @pl.when(far_down)
        def _():
            for t in kinds:
                low_halo(t)

        @pl.when(jnp.logical_not(far_down))
        def _():
            for t in kinds:
                high_halo(t)

    def halo_sent(t):
        if t < 4:

            @pl.when(both(far, column != t))
            def _():
                for h in range(groups):
                    leg_one(t, h).wait_send()

        pl.when(near_up)(lambda: to_up(t).wait_send())
        pl.when(near_down)(lambda: to_down(t).wait_send())
        pl.when(right)(lambda: to_right(t).wait_send())
        pl.when(left)(lambda: to_left(t).wait_send())
        pl.when(both(near_up, left))(lambda: side_up(t, 0).wait_send())
        pl.when(both(near_up, right))(lambda: side_up(t, 2).wait_send())
        pl.when(both(near_down, left))(lambda: side_down(t, 0).wait_send())
        pl.when(both(near_down, right))(lambda: side_down(t, 2).wait_send())
        if t == 4:
            pl.when(both(far_down, right))(lambda: along_right(t, 0).wait_send())
            pl.when(both(far_down, left))(lambda: along_left(t, 0).wait_send())
            pl.when(both(far_up, right))(lambda: along_right(t, 3).wait_send())
            pl.when(both(far_up, left))(lambda: along_left(t, 3).wait_send())

    for j in range(3):
        loading_act(j).wait()

    lanes = lax.broadcasted_iota(jnp.int32, (1, 128), 1)

    def placed(i, j):
        frame, row = 2 * f_at - 1 + i, r_at - 1 + j
        return (frame >= 0) & (frame < 2 * frames) & (row >= 0) & (row < rows)

    def entry(i, j, l, slot, inside):
        frame = jnp.clip(2 * f_at - 1 + i, 0, 2 * frames - 1)
        return jnp.where(inside & (act[j, slot, l, frame] == 1), 0.0, NEG)

    def halves(pair_of):
        return jnp.where(lanes < 64, pair_of[0], pair_of[1])

    def mask_step(i, carry):
        f, a = i // 3, i % 3
        for b in range(3):
            span = pl.ds(pl.multiple_of(a * 384 + b * 128, 128), 128)
            inside = placed(f + a, b)
            for l in range(2):
                slots = [9 * a + 3 * b + m - l + 1 for m in range(2)]
                front[f, l, :, span] = halves([entry(f + 1, 1, l, n, inside) for n in slots])
                slots = [9 * (2 - a) + 3 * (2 - b) + l - m + 1 for m in range(2)]
                behind[f, l, :, span] = halves([entry(f + a, b, l, n, inside) for n in slots])
        return carry

    lax.fori_loop(0, 6, mask_step, 0)

    @pl.when(far)
    def _():
        for b in range(3):
            inside = placed(edge + 1, b)
            for l in range(2):
                slots = [18 * (1 - edge) + 3 * b + l - m + 1 for m in range(2)]
                pieces = [entry(beyond, 1, m, n, inside) for m, n in enumerate(slots)]
                across[2 * b + l] = halves(pieces)

    for t in range(4):
        loading(t).wait()
        for g in range(4):
            moved = nn(to_heads, land[t, pl.ds(g * tall, tall)]).astype(jnp.bfloat16)
            pack[t, :, g // 2, pl.ds(16 * (g % 2), 16)] = moved.reshape(heads_all, 16, 128)
        if t == 0:
            known = [right, left, near_up, near_down] + targets
            count = heads - 1 + sum(c.astype(jnp.int32) for c in known)
            count += 3 * far.astype(jnp.int32) + 9 * proxy.astype(jnp.int32)
            pl.semaphore_wait(barrier, count)
            pl.when(proxy)(tell)
        for k in range(1, heads):
            exchange(t, k).start()
        wide[t, :, pl.ds(1, 2), 1, pl.ds(pl.multiple_of(x_at * 32, 32), 32)] = pack[
            t, pl.ds(x_at * groups, groups)
        ]

    def gathered(t):
        for k in range(1, heads):
            arriving(t, k).wait_recv()

    gathered(KEY)
    first_halo(KEY)
    row_halo(KEY)
    gathered(VAL)
    first_halo(VAL)
    row_halo(VAL)
    relay_one(soon, KEY)
    second_halo(KEY)
    gathered(QRY)
    first_halo(QRY)
    relay_one(soon, VAL)
    second_halo(VAL)
    gathered(GRD)
    first_halo(GRD)
    relay_one(soon, QRY, GRD)

    lane_grid = lax.broadcasted_iota(jnp.int32, (128, 128), 1)
    power = scaling * math.log2(math.e)
    wide_rows = 9 * 128

    def as_rows(level, dot):
        return jnp.where(lane_grid == 0, level, dot).T[0:8]

    def query_step(i, carry):
        h, f = i % groups, (i // groups) ^ flip
        q = wide[QRY, h, f + 1, 1]
        g = wide[GRD, h, f + 1, 1]
        k_band = wide[KEY, h, pl.ds(f, 3)].reshape(wide_rows, 128)
        v_band = wide[VAL, h, pl.ds(f, 3)].reshape(wide_rows, 128)
        s = (nt(q, k_band).reshape(2, 64, wide_rows) + front[f]).reshape(128, wide_rows)
        top = jnp.max(s, axis=1, keepdims=True)
        p = jnp.exp2((s - top) * power)
        total = jnp.sum(p, axis=1, keepdims=True)
        inverse = 1.0 / total
        out = (nn(p.astype(jnp.bfloat16), v_band) * inverse).astype(jnp.bfloat16)
        own[0, h, f] = out
        dot = jnp.sum(g.astype(jnp.float32) * out.astype(jnp.float32), axis=1, keepdims=True)
        ds = (p * (nt(g, v_band) - dot)).astype(jnp.bfloat16)
        own[1, h, f] = (nn(ds, k_band) * (inverse * scaling)).astype(jnp.bfloat16)
        stats[h, f + 1, 1] = as_rows(top * power + jnp.log2(total), dot)
        return carry

    def near_step(h, carry):
        q = wide[QRY, h, edge + 1, 1]
        g = wide[GRD, h, edge + 1, 1]
        k_band = wide[KEY, h, pl.ds(1, 2)].reshape(6 * 128, 128)
        v_band = wide[VAL, h, pl.ds(1, 2)].reshape(6 * 128, 128)
        offset = pl.multiple_of((1 - edge) * 384, 128)
        mask = front[edge, :, :, pl.ds(offset, 768)]
        s = (nt(q, k_band).reshape(2, 64, 768) + mask).reshape(128, 768)
        top = jnp.max(s, axis=1, keepdims=True)
        p = jnp.exp2((s - top) * power)
        total = jnp.sum(p, axis=1, keepdims=True)
        dot = jnp.sum(p * nt(g, v_band), axis=1, keepdims=True) / total
        part[0, h] = as_rows(top * power + jnp.log2(total), dot)
        return carry

    def across_step(h, carry):
        q = wide[QRY, h, beyond, 1]
        g = wide[GRD, h, beyond, 1]
        k_band = wide[KEY, h, edge + 1].reshape(384, 128)
        v_band = wide[VAL, h, edge + 1].reshape(384, 128)
        s = ((nt(k_band, q) * power).reshape(6, 64, 128) + across[...]).reshape(384, 128)
        top = jnp.max(s, axis=0, keepdims=True)
        p = jnp.exp2(s - top)
        total = jnp.sum(p, axis=0, keepdims=True)
        dot = jnp.sum(p * nt(v_band, g), axis=0, keepdims=True) / total
        level = top + jnp.log2(total)
        level_near, dot_near = part[1, h, 0:1], part[1, h, 1:2]
        peak = jnp.maximum(level, level_near)
        whole = peak + jnp.log2(jnp.exp2(level - peak) + jnp.exp2(level_near - peak))
        mixed = jnp.exp2(level - whole) * dot + jnp.exp2(level_near - whole) * dot_near
        stats[h, beyond, 1, 0:1] = whole
        stats[h, beyond, 1, 1:2] = mixed
        return carry

    def key_step(i, carry):
        h, f = i % groups, (i // groups) ^ flip
        k = wide[KEY, h, f + 1, 1]
        v = wide[VAL, h, f + 1, 1]
        q_band = wide[QRY, h, pl.ds(f, 3)].reshape(wide_rows, 128)
        g_band = wide[GRD, h, pl.ds(f, 3)].reshape(wide_rows, 128)
        tiles = [stats[h, f + a, b] for a in range(3) for b in range(3)]
        level = jnp.concatenate([t[0:1] for t in tiles], axis=1)
        dot = jnp.concatenate([t[1:2] for t in tiles], axis=1)
        s = (nt(k, q_band) * power).reshape(2, 64, wide_rows) + (behind[f] - level)
        p = jnp.exp2(s.reshape(128, wide_rows))
        own[3, h, f] = nn(p.astype(jnp.bfloat16), g_band).astype(jnp.bfloat16)
        ds = (p * (nt(v, g_band) - dot)).astype(jnp.bfloat16)
        own[2, h, f] = (nn(ds, q_band) * scaling).astype(jnp.bfloat16)
        return carry

    def giving(o, half_at, k):
        f = half_at ^ flip
        spot = pl.ds(pl.multiple_of(peers[k] * 32, 32), 32)
        return pltpu.make_async_remote_copy(
            src_ref=own.at[o, :, f, spot],
            dst_ref=outs[o].at[pl.ds(x_at * groups, groups), f],
            send_sem=o_send.at[o, half_at, k - 1],
            recv_sem=o_recv.at[o, half_at, k - 1],
            device_id=(f_at, r_at, peers[k]),
            device_id_type=MESH,
        )

    def taking(o, half_at, k):
        f = half_at ^ flip
        return pltpu.make_async_remote_copy(
            src_ref=own.at[o, :, f, pl.ds(0, 32)],
            dst_ref=outs[o].at[pl.ds(froms[k] * groups, groups), f],
            send_sem=o_send.at[o, half_at, k - 1],
            recv_sem=o_recv.at[o, half_at, k - 1],
            device_id=(f_at, r_at, froms[k]),
            device_id_type=MESH,
        )

    def give(half_at, *kinds):
        f = half_at ^ flip
        for o in kinds:
            for k in range(1, heads):
                giving(o, half_at, k).start()
            keeping(o, half_at).start()

    def keeping(o, half_at):
        f = half_at ^ flip
        spot = pl.ds(pl.multiple_of(x_at * 32, 32), 32)
        return pltpu.make_async_copy(
            own.at[o, :, f, spot],
            outs[o].at[pl.ds(x_at * groups, groups), f],
            out_sem.at[o, half_at],
        )

    relay_one(later, KEY, VAL, QRY, GRD)

    @pl.when(far)
    def _():
        lax.fori_loop(0, groups, near_step, 0)

    pl.when(far)(lambda: summary(0).start())
    early_halo(KEY, VAL)

    @pl.when(far)
    def _():
        row_halo(QRY)
        row_halo(GRD)

    lax.fori_loop(0, groups, query_step, 0)
    relay_two(far_down)

    @pl.when(near)
    def _():
        row_halo(QRY)
        row_halo(GRD)

    give(0, 0, 1)

    @pl.when(far)
    def _():
        second_halo(QRY)
        second_halo(GRD)

    far_halo(KEY)
    far_halo(VAL)
    late_halo(KEY, VAL)
    lax.fori_loop(groups, groups * 2, query_step, 0)
    first_halo(4)
    row_halo(4)

    @pl.when(near)
    def _():
        second_halo(QRY)
        second_halo(GRD)

    give(1, 0, 1)
    relay_two(jnp.logical_not(far_down))
    second_halo(4)
    early_halo(QRY, GRD, 4)
    lax.fori_loop(0, groups, key_step, 0)
    give(0, 2, 3)
    far_halo(QRY)
    far_halo(GRD)

    @pl.when(far)
    def _():
        summary(0).wait_recv()
        lax.fori_loop(0, groups, across_step, 0)

    far_halo(4)
    late_halo(QRY, GRD, 4)
    lax.fori_loop(groups, groups * 2, key_step, 0)
    give(1, 2, 3)

    for t in range(4):
        for k in range(1, heads):
            exchange(t, k).wait_send()
            giving(t, 0, k).wait_send()
            giving(t, 1, k).wait_send()
    for t in range(5):
        halo_sent(t)
    pl.when(far)(lambda: summary(0).wait_send())
    for h in range(groups):
        pl.when(first_relay)(lambda: leg_two(relay.at[0, h], h).wait_send())
        for v in range(3):
            pl.when(targets[v])(lambda: leg_three(0, h, v).wait_send())
    for o in range(4):
        for half_at in range(2):
            keeping(o, half_at).wait()
            for k in range(1, heads):
                taking(o, half_at, k).wait_recv()


def on_device(sizes, queries, keys, values, out_grad, active):
    frames, rows, heads, groups, scaling = sizes
    frames_here, rows_here, cols_here, heads_all, head_dim = queries.shape
    table = jnp.transpose(active, (1, 3, 2, 0))
    tall = frames_here * rows_here * cols_here * heads_all

    def flat(tensor):
        return jnp.transpose(tensor, (0, 1, 3, 2, 4)).reshape(tall, head_dim)

    def unflat(tensor):
        shaped = tensor.reshape(heads_all, frames_here, rows_here, cols_here, head_dim)
        return jnp.transpose(shaped, (1, 2, 3, 0, 4))

    dma = pltpu.SemaphoreType.DMA
    block = (128, head_dim)
    kinds = heads - 1
    anywhere = pl.BlockSpec(memory_space=pl.ANY)
    results = pl.pallas_call(
        functools.partial(tile_kernel, sizes),
        out_shape=[jax.ShapeDtypeStruct((heads_all, 2, 32, head_dim), jnp.bfloat16)] * 4,
        in_specs=[anywhere] * 5,
        out_specs=[anywhere] * 4,
        scratch_shapes=[
            pltpu.VMEM((4, tall, head_dim), jnp.bfloat16),
            pltpu.VMEM((4, heads_all, 2, 32, head_dim), jnp.bfloat16),
            pltpu.VMEM((4, groups, 4, 3) + block, jnp.bfloat16),
            pltpu.VMEM((groups, 4, 3, 8, 128), jnp.float32),
            pltpu.VMEM((4, groups, 2) + block, jnp.bfloat16),
            pltpu.VMEM((2, groups, 8, 128), jnp.float32),
            pltpu.VMEM((2, 2, 1, 9 * 128), jnp.float32),
            pltpu.VMEM((2, 2, 1, 9 * 128), jnp.float32),
            pltpu.VMEM((6, 1, 128), jnp.float32),
            pltpu.VMEM((2, groups) + block, jnp.bfloat16),
            pltpu.SMEM((3,) + table.shape[1:], jnp.int32),
            dma((4,)),
            dma((4, kinds)),
            dma((4, kinds)),
            dma((5, 2)),
            dma((5, 2)),
            dma((5, 2)),
            dma((5, 2)),
            dma((5, 4)),
            dma((5, 4)),
            dma((4, 2, kinds)),
            dma((4, 2, kinds)),
            dma((4, 2)),
            dma((2,)),
            dma((3,)),
            dma((8 * groups,)),
            dma((2, groups)),
            pltpu.SemaphoreType.REGULAR,
        ],
        compiler_params=pltpu.CompilerParams(
            collective_id=0, has_side_effects=True, vmem_limit_bytes=VMEM
        ),
    )(table, flat(keys), flat(values), flat(queries), flat(out_grad))
    return tuple(unflat(r) for r in results)


def solution(mesh):
    frames, rows, heads = (mesh.shape[a] for a in ("frame", "row", "head"))
    sizes = (frames, rows, heads, 12 // heads, 128**-0.5)
    spec = P("frame", "row", "head", None, None)
    return jax.shard_map(
        functools.partial(on_device, sizes),
        mesh=mesh,
        in_specs=(spec,) * 4 + (P(),),
        out_specs=(spec,) * 4,
        check_vma=False,
    )
```

```python
import functools
import math

import jax
import jax.numpy as jnp
from jax import lax
from jax.experimental import pallas as pl
from jax.experimental.pallas import tpu as pltpu
from jax.sharding import PartitionSpec as P

MESH = pl.DeviceIdType.MESH
NEG = -1e30
KEY, VAL, QRY, GRD = 0, 1, 2, 3
VMEM = 63 << 20


def nt(left, right):
    return lax.dot_general(
        left, right, (((1,), (1,)), ((), ())), preferred_element_type=jnp.float32
    )


def nn(left, right):
    return jnp.dot(left, right, preferred_element_type=jnp.float32)


def tile_kernel(sizes, act_in, k_in, v_in, q_in, g_in, *refs):
    frames, rows, heads, groups, scaling = sizes
    outs, refs = refs[:4], refs[4:]
    land, pack, wide, stats, own, part, front, behind, across, relay, act = refs[:11]
    in_sem, a_send, a_recv, z_send, z_recv, c_send, c_recv, d_send, d_recv = refs[11:20]
    o_send, o_recv, out_sem, part_sem, act_sem, leg_send, leg_recv, ready = refs[20:28]
    ins = (k_in, v_in, q_in, g_in)
    heads_all = groups * heads
    tall = heads_all * 16

    f_at = lax.axis_index("frame")
    r_at = lax.axis_index("row")
    x_at = lax.axis_index("head")
    up, down = f_at < frames - 1, f_at > 0
    right, left = r_at < rows - 1, r_at > 0
    far_up, far_down = f_at == frames // 2 - 1, f_at == frames // 2
    both = jnp.logical_and
    near_up = both(up, jnp.logical_not(far_up))
    near_down = both(down, jnp.logical_not(far_down))
    far = jnp.logical_or(far_up, far_down)

    half, turn = frames // 2, 2 * rows
    upper, place = f_at // half, f_at % half
    core, column = f_at % 2, place // 2
    z_at = upper * rows + r_at
    first_relay = core + upper == 1
    shifted = lax.rem(z_at + rows * (1 - core), turn)
    odd = lax.rem(shifted, 2)
    began = jnp.where(odd == 1, shifted - (rows - 1), lax.rem(shifted + turn - rows - 1, turn))
    second_relay = both(began >= 0, began < rows) & (lax.rem(began + turn, 2) == 1 - odd)
    near = jnp.logical_not(far)
    soon = both(upper == 1, r_at < rows // 2)
    later = jnp.logical_not(soon)

    def relays_of(z, row, member):
        spot = lax.rem(z + rows - 1 + 2 * lax.rem(row, 2), turn)
        return (spot // rows) * half + member, lax.rem(spot, rows)

    def start_relay(t):
        return upper * half + 2 * t + core, r_at

    def proxy_of(side, row):
        return half - 4 + 7 * side, row

    proxy = f_at == proxy_of(upper, r_at)[0]
    next_relay = relays_of(z_at, r_at, place)
    targets = [both(second_relay, both(began + 1 - v >= 0, began + 1 - v < rows)) for v in range(3)]
    edge = far_up.astype(jnp.int32)
    beyond = 3 * edge
    flip = far_down.astype(jnp.int32)

    peers = [lax.rem(x_at + k, heads) for k in range(heads)]
    froms = [lax.rem(x_at + heads - k, heads) for k in range(heads)]

    def loading(t):
        return pltpu.make_async_copy(ins[t], land.at[t], in_sem.at[t])

    def loading_act(j):
        row = jnp.clip(r_at - 1 + j, 0, rows - 1)
        return pltpu.make_async_copy(act_in.at[row], act.at[j], act_sem.at[j])

    for t in range(4):
        loading(t).start()
    for j in range(3):
        loading_act(j).start()

    barrier = pltpu.get_barrier_semaphore()

    def greet(frame, row, head):
        pl.semaphore_signal(barrier, inc=1, device_id=(frame, row, head), device_id_type=MESH)

    for k in range(1, heads):
        greet(f_at, r_at, peers[k])
    pl.when(right)(lambda: greet(f_at, r_at + 1, x_at))
    pl.when(left)(lambda: greet(f_at, r_at - 1, x_at))
    pl.when(near_up)(lambda: greet(f_at + 1, r_at, x_at))
    pl.when(near_down)(lambda: greet(f_at - 1, r_at, x_at))

    @pl.when(far)
    def _():
        greet(*proxy_of(1 - upper, r_at), x_at)
        for v, known in enumerate((left, f_at >= 0, right)):

            @pl.when(known)
            def _():
                for t in range(4):
                    z, row = z_at + rows + v - 1, r_at + v - 1
                    greet(*relays_of(z, row, 2 * t + 1 - core), x_at)

    pl.when(both(first_relay, near))(lambda: greet(half - 1 + upper, r_at, x_at))
    pl.when(first_relay)(lambda: greet(*proxy_of(upper, r_at), x_at))
    pl.when(second_relay)(lambda: greet(*proxy_of(1 - core, began), x_at))

    @pl.when(jnp.logical_not(left))
    def _():
        wide[:, :, :, 0] = jnp.zeros_like(wide[:, :, :, 0])
        stats[:, :, 0] = jnp.zeros_like(stats[:, :, 0])

    @pl.when(jnp.logical_not(right))
    def _():
        wide[:, :, :, 2] = jnp.zeros_like(wide[:, :, :, 2])
        stats[:, :, 2] = jnp.zeros_like(stats[:, :, 2])

    @pl.when(jnp.logical_not(down))
    def _():
        wide[:, :, 0] = jnp.zeros_like(wide[:, :, 0])
        stats[:, 0] = jnp.zeros_like(stats[:, 0])

    @pl.when(jnp.logical_not(up))
    def _():
        wide[:, :, 3] = jnp.zeros_like(wide[:, :, 3])
        stats[:, 3] = jnp.zeros_like(stats[:, 3])

    out_row = lax.broadcasted_iota(jnp.int32, (tall, tall), 0)
    in_row = lax.broadcasted_iota(jnp.int32, (tall, tall), 1)

    def swapped(row):
        return ((row % 16) // 4) * (4 * heads_all) + (row // 16) * 4 + row % 4

    to_heads = (swapped(out_row) == in_row).astype(jnp.bfloat16)

    def exchange(t, k):
        there = peers[k]
        return pltpu.make_async_remote_copy(
            src_ref=pack.at[t, pl.ds(there * groups, groups)],
            dst_ref=wide.at[t, :, pl.ds(1, 2), 1, pl.ds(pl.multiple_of(x_at * 32, 32), 32)],
            send_sem=a_send.at[t, k - 1],
            recv_sem=a_recv.at[t, k - 1],
            device_id=(f_at, r_at, there),
            device_id_type=MESH,
        )

    def arriving(t, k):
        spot = pl.ds(pl.multiple_of(froms[k] * 32, 32), 32)
        return pltpu.make_async_remote_copy(
            src_ref=pack.at[t, pl.ds(0, groups)],
            dst_ref=wide.at[t, :, pl.ds(1, 2), 1, spot],
            send_sem=a_send.at[t, k - 1],
            recv_sem=a_recv.at[t, k - 1],
            device_id=(f_at, r_at, froms[k]),
            device_id_type=MESH,
        )

    def block(t, frame, row):
        ref = stats if t == 4 else wide.at[t]
        return ref.at[:, frame, row]

    def pair(t, row):
        ref = stats if t == 4 else wide.at[t]
        return ref.at[:, pl.ds(1, 2), row]

    def hop(src, dst, ss, rs, frame, row):
        return pltpu.make_async_remote_copy(
            src_ref=src,
            dst_ref=dst,
            send_sem=ss,
            recv_sem=rs,
            device_id=(frame, row, x_at),
            device_id_type=MESH,
        )

    def to_right(t):
        return hop(pair(t, 1), pair(t, 0), z_send.at[t, 0], z_recv.at[t, 0], f_at, r_at + 1)

    def to_left(t):
        return hop(pair(t, 1), pair(t, 2), z_send.at[t, 1], z_recv.at[t, 1], f_at, r_at - 1)

    def to_up(t):
        return hop(block(t, 2, 1), block(t, 0, 1), c_send.at[t, 0], c_recv.at[t, 0], f_at + 1, r_at)

    def to_down(t):
        return hop(block(t, 1, 1), block(t, 3, 1), c_send.at[t, 1], c_recv.at[t, 1], f_at - 1, r_at)

    def side_up(t, row):
        sem = 0 if row == 0 else 1
        return hop(
            block(t, 2, row), block(t, 0, row), d_send.at[t, sem], d_recv.at[t, sem], f_at + 1, r_at
        )

    def side_down(t, row):
        sem = 2 if row == 0 else 3
        return hop(
            block(t, 1, row), block(t, 3, row), d_send.at[t, sem], d_recv.at[t, sem], f_at - 1, r_at
        )

    def along_right(t, frame):
        sem = 0 if frame == 0 else 2
        return hop(
            block(t, frame, 1), block(t, frame, 0), d_send.at[t, sem], d_recv.at[t, sem], f_at, r_at + 1
        )

    def along_left(t, frame):
        sem = 1 if frame == 0 else 3
        return hop(
            block(t, frame, 1), block(t, frame, 2), d_send.at[t, sem], d_recv.at[t, sem], f_at, r_at - 1
        )

    def tell():
        for t in range(4):
            there = (upper * half + 2 * t + 1 - core, r_at, x_at)
            pl.semaphore_signal(ready, inc=1, device_id=there, device_id_type=MESH)

    def leg_one(t, h):
        return hop(
            wide.at[t, h, edge + 1, 1],
            relay.at[0, h],
            leg_send.at[t * groups + h],
            leg_recv.at[0, h],
            *start_relay(t),
        )

    def leg_two(src, h):
        return hop(
            src, relay.at[1, h], leg_send.at[4 * groups + h], leg_recv.at[1, h], *next_relay
        )

    def leg_three(t, h, v):
        side = 1 - core
        sem = c_recv.at[t, side] if v == 1 else d_recv.at[t, 2 * side + v // 2]
        return hop(
            relay.at[1, h],
            wide.at[t, h, 3 * side, v],
            leg_send.at[(5 + v) * groups + h],
            sem,
            half - 1 + core,
            began + 1 - v,
        )

    def first_halo(t):
        if t < 4:

            @pl.when(both(far, column != t))
            def _():
                for h in range(groups):
                    leg_one(t, h).start()

        pl.when(near_up)(lambda: to_up(t).start())
        pl.when(near_down)(lambda: to_down(t).start())

    def row_halo(t):
        pl.when(right)(lambda: to_right(t).start())
        pl.when(left)(lambda: to_left(t).start())

    def relay_one(group, *kinds):
        for t in kinds:
            here = both(group, both(first_relay, column == t))

            @pl.when(both(here, near))
            def _():
                for h in range(groups):
                    leg_one(t, h).wait_recv()
                    if h == 0:
                        pl.semaphore_wait(ready, 1)
                    leg_two(relay.at[0, h], h).start()

            @pl.when(both(here, far))
            def _():
                pl.semaphore_wait(ready, 1)
                for h in range(groups):
                    leg_two(wide.at[t, h, edge + 1, 1], h).start()

    def relay_two(group):
        for t in range(4):
            for h in range(groups):
                here = both(group, column == t)

                @pl.when(both(here, second_relay))
                def _():
                    leg_two(relay.at[0, h], h).wait_recv()

                for v in (1, 0, 2):
                    pl.when(both(here, targets[v]))(lambda: leg_three(t, h, v).start())

    def summary(side):
        there = jnp.where(far_up, half, half - 1)
        return hop(part.at[0], part.at[1], part_sem.at[0], part_sem.at[1], there, r_at)

    def second_halo(t):
        pl.when(left)(lambda: to_right(t).wait_recv())
        pl.when(right)(lambda: to_left(t).wait_recv())
        pl.when(both(near_up, left))(lambda: side_up(t, 0).start())
        pl.when(both(near_up, right))(lambda: side_up(t, 2).start())
        pl.when(both(near_down, left))(lambda: side_down(t, 0).start())
        pl.when(both(near_down, right))(lambda: side_down(t, 2).start())

    def far_halo(t):
        if t < 4:
            pl.when(far_down)(lambda: to_up(t).wait_recv())
            pl.when(far_up)(lambda: to_down(t).wait_recv())
        if t == 4:
            pl.when(both(far_down, right))(lambda: along_right(t, 0).start())
            pl.when(both(far_down, left))(lambda: along_left(t, 0).start())
            pl.when(both(far_up, right))(lambda: along_right(t, 3).start())
            pl.when(both(far_up, left))(lambda: along_left(t, 3).start())

    def low_halo(t):
        pl.when(near_down)(lambda: to_up(t).wait_recv())
        pl.when(both(down, left))(lambda: side_up(t, 0).wait_recv())
        pl.when(both(down, right))(lambda: side_up(t, 2).wait_recv())

    def high_halo(t):
        pl.when(near_up)(lambda: to_down(t).wait_recv())
        pl.when(both(up, left))(lambda: side_down(t, 0).wait_recv())
        pl.when(both(up, right))(lambda: side_down(t, 2).wait_recv())

    def early_halo(*kinds):
        @pl.when(jnp.logical_not(far_down))
        def _():
            for t in kinds:
                low_halo(t)

        @pl.when(far_down)
        def _():
            for t in kinds:
                high_halo(t)

    def late_halo(*kinds):
        @pl.when(far_down)
        def _():
            for t in kinds:
                low_halo(t)

        @pl.when(jnp.logical_not(far_down))
        def _():
            for t in kinds:
                high_halo(t)

    def halo_sent(t):
        if t < 4:

            @pl.when(both(far, column != t))
            def _():
                for h in range(groups):
                    leg_one(t, h).wait_send()

        pl.when(near_up)(lambda: to_up(t).wait_send())
        pl.when(near_down)(lambda: to_down(t).wait_send())
        pl.when(right)(lambda: to_right(t).wait_send())
        pl.when(left)(lambda: to_left(t).wait_send())
        pl.when(both(near_up, left))(lambda: side_up(t, 0).wait_send())
        pl.when(both(near_up, right))(lambda: side_up(t, 2).wait_send())
        pl.when(both(near_down, left))(lambda: side_down(t, 0).wait_send())
        pl.when(both(near_down, right))(lambda: side_down(t, 2).wait_send())
        if t == 4:
            pl.when(both(far_down, right))(lambda: along_right(t, 0).wait_send())
            pl.when(both(far_down, left))(lambda: along_left(t, 0).wait_send())
            pl.when(both(far_up, right))(lambda: along_right(t, 3).wait_send())
            pl.when(both(far_up, left))(lambda: along_left(t, 3).wait_send())

    for j in range(3):
        loading_act(j).wait()

    lanes = lax.broadcasted_iota(jnp.int32, (1, 128), 1)

    def placed(i, j):
        frame, row = 2 * f_at - 1 + i, r_at - 1 + j
        return (frame >= 0) & (frame < 2 * frames) & (row >= 0) & (row < rows)

    def entry(i, j, l, slot, inside):
        frame = jnp.clip(2 * f_at - 1 + i, 0, 2 * frames - 1)
        return jnp.where(inside & (act[j, slot, l, frame] == 1), 0.0, NEG)

    def halves(pair_of):
        return jnp.where(lanes < 64, pair_of[0], pair_of[1])

    def mask_step(i, carry):
        f, a = i // 3, i % 3
        for b in range(3):
            span = pl.ds(pl.multiple_of(a * 384 + b * 128, 128), 128)
            inside = placed(f + a, b)
            for l in range(2):
                slots = [9 * a + 3 * b + m - l + 1 for m in range(2)]
                front[f, l, :, span] = halves([entry(f + 1, 1, l, n, inside) for n in slots])
                slots = [9 * (2 - a) + 3 * (2 - b) + l - m + 1 for m in range(2)]
                behind[f, l, :, span] = halves([entry(f + a, b, l, n, inside) for n in slots])
        return carry

    lax.fori_loop(0, 6, mask_step, 0)

    @pl.when(far)
    def _():
        for b in range(3):
            inside = placed(edge + 1, b)
            for l in range(2):
                slots = [18 * (1 - edge) + 3 * b + l - m + 1 for m in range(2)]
                pieces = [entry(beyond, 1, m, n, inside) for m, n in enumerate(slots)]
                across[2 * b + l] = halves(pieces)

    for t in range(4):
        loading(t).wait()
        for g in range(4):
            moved = nn(to_heads, land[t, pl.ds(g * tall, tall)]).astype(jnp.bfloat16)
            pack[t, :, g // 2, pl.ds(16 * (g % 2), 16)] = moved.reshape(heads_all, 16, 128)
        if t == 0:
            known = [right, left, near_up, near_down] + targets
            count = heads - 1 + sum(c.astype(jnp.int32) for c in known)
            count += 3 * far.astype(jnp.int32) + 9 * proxy.astype(jnp.int32)
            pl.semaphore_wait(barrier, count)
            pl.when(proxy)(tell)
        for k in range(1, heads):
            exchange(t, k).start()
        wide[t, :, pl.ds(1, 2), 1, pl.ds(pl.multiple_of(x_at * 32, 32), 32)] = pack[
            t, pl.ds(x_at * groups, groups)
        ]

    def gathered(t):
        for k in range(1, heads):
            arriving(t, k).wait_recv()

    gathered(KEY)
    first_halo(KEY)
    row_halo(KEY)
    gathered(VAL)
    first_halo(VAL)
    row_halo(VAL)
    relay_one(soon, KEY)
    second_halo(KEY)
    gathered(QRY)
    first_halo(QRY)
    relay_one(soon, VAL)
    second_halo(VAL)
    gathered(GRD)
    first_halo(GRD)
    relay_one(soon, QRY, GRD)
    row_halo(QRY)
    row_halo(GRD)

    lane_grid = lax.broadcasted_iota(jnp.int32, (128, 128), 1)
    power = scaling * math.log2(math.e)
    wide_rows = 9 * 128

    def as_rows(level, dot):
        return jnp.where(lane_grid == 0, level, dot).T[0:8]

    def query_step(i, carry):
        h, f = i % groups, (i // groups) ^ flip
        q = wide[QRY, h, f + 1, 1]
        g = wide[GRD, h, f + 1, 1]
        k_band = wide[KEY, h, pl.ds(f, 3)].reshape(wide_rows, 128)
        v_band = wide[VAL, h, pl.ds(f, 3)].reshape(wide_rows, 128)
        s = (nt(q, k_band).reshape(2, 64, wide_rows) + front[f]).reshape(128, wide_rows)
        top = jnp.max(s, axis=1, keepdims=True)
        p = jnp.exp2((s - top) * power)
        total = jnp.sum(p, axis=1, keepdims=True)
        inverse = 1.0 / total
        out = (nn(p.astype(jnp.bfloat16), v_band) * inverse).astype(jnp.bfloat16)
        own[0, h, f] = out
        dot = jnp.sum(g.astype(jnp.float32) * out.astype(jnp.float32), axis=1, keepdims=True)
        ds = (p * (nt(g, v_band) - dot)).astype(jnp.bfloat16)
        own[1, h, f] = (nn(ds, k_band) * (inverse * scaling)).astype(jnp.bfloat16)
        stats[h, f + 1, 1] = as_rows(top * power + jnp.log2(total), dot)
        return carry

    def near_step(h, carry):
        q = wide[QRY, h, edge + 1, 1]
        g = wide[GRD, h, edge + 1, 1]
        k_band = wide[KEY, h, pl.ds(1, 2)].reshape(6 * 128, 128)
        v_band = wide[VAL, h, pl.ds(1, 2)].reshape(6 * 128, 128)
        offset = pl.multiple_of((1 - edge) * 384, 128)
        mask = front[edge, :, :, pl.ds(offset, 768)]
        s = (nt(q, k_band).reshape(2, 64, 768) + mask).reshape(128, 768)
        top = jnp.max(s, axis=1, keepdims=True)
        p = jnp.exp2((s - top) * power)
        total = jnp.sum(p, axis=1, keepdims=True)
        dot = jnp.sum(p * nt(g, v_band), axis=1, keepdims=True) / total
        part[0, h] = as_rows(top * power + jnp.log2(total), dot)
        return carry

    def across_step(h, carry):
        q = wide[QRY, h, beyond, 1]
        g = wide[GRD, h, beyond, 1]
        k_band = wide[KEY, h, edge + 1].reshape(384, 128)
        v_band = wide[VAL, h, edge + 1].reshape(384, 128)
        s = ((nt(k_band, q) * power).reshape(6, 64, 128) + across[...]).reshape(384, 128)
        top = jnp.max(s, axis=0, keepdims=True)
        p = jnp.exp2(s - top)
        total = jnp.sum(p, axis=0, keepdims=True)
        dot = jnp.sum(p * nt(v_band, g), axis=0, keepdims=True) / total
        level = top + jnp.log2(total)
        level_near, dot_near = part[1, h, 0:1], part[1, h, 1:2]
        peak = jnp.maximum(level, level_near)
        whole = peak + jnp.log2(jnp.exp2(level - peak) + jnp.exp2(level_near - peak))
        mixed = jnp.exp2(level - whole) * dot + jnp.exp2(level_near - whole) * dot_near
        stats[h, beyond, 1, 0:1] = whole
        stats[h, beyond, 1, 1:2] = mixed
        return carry

    def key_step(i, carry):
        h, f = i % groups, (i // groups) ^ flip
        k = wide[KEY, h, f + 1, 1]
        v = wide[VAL, h, f + 1, 1]
        q_band = wide[QRY, h, pl.ds(f, 3)].reshape(wide_rows, 128)
        g_band = wide[GRD, h, pl.ds(f, 3)].reshape(wide_rows, 128)
        tiles = [stats[h, f + a, b] for a in range(3) for b in range(3)]
        level = jnp.concatenate([t[0:1] for t in tiles], axis=1)
        dot = jnp.concatenate([t[1:2] for t in tiles], axis=1)
        s = (nt(k, q_band) * power).reshape(2, 64, wide_rows) + (behind[f] - level)
        p = jnp.exp2(s.reshape(128, wide_rows))
        own[3, h, f] = nn(p.astype(jnp.bfloat16), g_band).astype(jnp.bfloat16)
        ds = (p * (nt(v, g_band) - dot)).astype(jnp.bfloat16)
        own[2, h, f] = (nn(ds, q_band) * scaling).astype(jnp.bfloat16)
        return carry

    def giving(o, half_at, k):
        f = half_at ^ flip
        spot = pl.ds(pl.multiple_of(peers[k] * 32, 32), 32)
        return pltpu.make_async_remote_copy(
            src_ref=own.at[o, :, f, spot],
            dst_ref=outs[o].at[pl.ds(x_at * groups, groups), f],
            send_sem=o_send.at[o, half_at, k - 1],
            recv_sem=o_recv.at[o, half_at, k - 1],
            device_id=(f_at, r_at, peers[k]),
            device_id_type=MESH,
        )

    def taking(o, half_at, k):
        f = half_at ^ flip
        return pltpu.make_async_remote_copy(
            src_ref=own.at[o, :, f, pl.ds(0, 32)],
            dst_ref=outs[o].at[pl.ds(froms[k] * groups, groups), f],
            send_sem=o_send.at[o, half_at, k - 1],
            recv_sem=o_recv.at[o, half_at, k - 1],
            device_id=(f_at, r_at, froms[k]),
            device_id_type=MESH,
        )

    def give(half_at, *kinds):
        f = half_at ^ flip
        for o in kinds:
            for k in range(1, heads):
                giving(o, half_at, k).start()
            keeping(o, half_at).start()

    def keeping(o, half_at):
        f = half_at ^ flip
        spot = pl.ds(pl.multiple_of(x_at * 32, 32), 32)
        return pltpu.make_async_copy(
            own.at[o, :, f, spot],
            outs[o].at[pl.ds(x_at * groups, groups), f],
            out_sem.at[o, half_at],
        )

    relay_one(later, KEY, VAL, QRY, GRD)

    @pl.when(far)
    def _():
        lax.fori_loop(0, groups, near_step, 0)

    pl.when(far)(lambda: summary(0).start())
    early_halo(KEY, VAL)
    lax.fori_loop(0, groups, query_step, 0)
    give(0, 0, 1)
    relay_two(far_down)

    @pl.when(far)
    def _():
        second_halo(QRY)
        second_halo(GRD)

    far_halo(KEY)
    far_halo(VAL)
    late_halo(KEY, VAL)
    lax.fori_loop(groups, groups * 2, query_step, 0)
    first_halo(4)
    row_halo(4)

    @pl.when(near)
    def _():
        second_halo(QRY)
        second_halo(GRD)

    give(1, 0, 1)
    relay_two(jnp.logical_not(far_down))
    second_halo(4)
    early_halo(QRY, GRD, 4)
    lax.fori_loop(0, groups, key_step, 0)
    give(0, 2, 3)
    far_halo(QRY)
    far_halo(GRD)

    @pl.when(far)
    def _():
        summary(0).wait_recv()
        lax.fori_loop(0, groups, across_step, 0)

    far_halo(4)
    late_halo(QRY, GRD, 4)
    lax.fori_loop(groups, groups * 2, key_step, 0)
    give(1, 2, 3)

    for t in range(4):
        for k in range(1, heads):
            exchange(t, k).wait_send()
            giving(t, 0, k).wait_send()
            giving(t, 1, k).wait_send()
    for t in range(5):
        halo_sent(t)
    pl.when(far)(lambda: summary(0).wait_send())
    for h in range(groups):
        pl.when(first_relay)(lambda: leg_two(relay.at[0, h], h).wait_send())
        for v in range(3):
            pl.when(targets[v])(lambda: leg_three(0, h, v).wait_send())
    for o in range(4):
        for half_at in range(2):
            keeping(o, half_at).wait()
            for k in range(1, heads):
                taking(o, half_at, k).wait_recv()


def on_device(sizes, queries, keys, values, out_grad, active):
    frames, rows, heads, groups, scaling = sizes
    frames_here, rows_here, cols_here, heads_all, head_dim = queries.shape
    table = jnp.transpose(active, (1, 3, 2, 0))
    tall = frames_here * rows_here * cols_here * heads_all

    def flat(tensor):
        return jnp.transpose(tensor, (0, 1, 3, 2, 4)).reshape(tall, head_dim)

    def unflat(tensor):
        shaped = tensor.reshape(heads_all, frames_here, rows_here, cols_here, head_dim)
        return jnp.transpose(shaped, (1, 2, 3, 0, 4))

    dma = pltpu.SemaphoreType.DMA
    block = (128, head_dim)
    kinds = heads - 1
    anywhere = pl.BlockSpec(memory_space=pl.ANY)
    results = pl.pallas_call(
        functools.partial(tile_kernel, sizes),
        out_shape=[jax.ShapeDtypeStruct((heads_all, 2, 32, head_dim), jnp.bfloat16)] * 4,
        in_specs=[anywhere] * 5,
        out_specs=[anywhere] * 4,
        scratch_shapes=[
            pltpu.VMEM((4, tall, head_dim), jnp.bfloat16),
            pltpu.VMEM((4, heads_all, 2, 32, head_dim), jnp.bfloat16),
            pltpu.VMEM((4, groups, 4, 3) + block, jnp.bfloat16),
            pltpu.VMEM((groups, 4, 3, 8, 128), jnp.float32),
            pltpu.VMEM((4, groups, 2) + block, jnp.bfloat16),
            pltpu.VMEM((2, groups, 8, 128), jnp.float32),
            pltpu.VMEM((2, 2, 1, 9 * 128), jnp.float32),
            pltpu.VMEM((2, 2, 1, 9 * 128), jnp.float32),
            pltpu.VMEM((6, 1, 128), jnp.float32),
            pltpu.VMEM((2, groups) + block, jnp.bfloat16),
            pltpu.SMEM((3,) + table.shape[1:], jnp.int32),
            dma((4,)),
            dma((4, kinds)),
            dma((4, kinds)),
            dma((5, 2)),
            dma((5, 2)),
            dma((5, 2)),
            dma((5, 2)),
            dma((5, 4)),
            dma((5, 4)),
            dma((4, 2, kinds)),
            dma((4, 2, kinds)),
            dma((4, 2)),
            dma((2,)),
            dma((3,)),
            dma((8 * groups,)),
            dma((2, groups)),
            pltpu.SemaphoreType.REGULAR,
        ],
        compiler_params=pltpu.CompilerParams(
            collective_id=0, has_side_effects=True, vmem_limit_bytes=VMEM
        ),
    )(table, flat(keys), flat(values), flat(queries), flat(out_grad))
    return tuple(unflat(r) for r in results)


def solution(mesh):
    frames, rows, heads = (mesh.shape[a] for a in ("frame", "row", "head"))
    sizes = (frames, rows, heads, 12 // heads, 128**-0.5)
    spec = P("frame", "row", "head", None, None)
    return jax.shard_map(
        functools.partial(on_device, sizes),
        mesh=mesh,
        in_specs=(spec,) * 4 + (P(),),
        out_specs=(spec,) * 4,
        check_vma=False,
    )
```
